32 devices in a mesh: fsdp: 16 (over z, x, core), tensor: 2 (over y).
Axes of the slice: x: 2, y: 2, z: 4, core: 2. Of those that a mesh axis runs over, the one named last changes fastest.
Arguments:
- tokens: bfloat16 [2, 4096, 1024], P(None, ('fsdp', 'tensor')), may hold values from -6 to 6
- segment_ids: int32 [2, 4096], P(None, 'fsdp'), may hold values from 0 to 3, as said below
- variate_ids: int32 [2, 4096], P(None, 'fsdp'), may hold values from 0 to 3, as said below
- time_ids: int32 [2, 4096], P(None, 'fsdp'), may hold values from 0 to 255, as said below
- attn_gain: float32 [1024], replicated, may hold values from 0.25 to 1.75
- w_query: bfloat16 [1024, 1024], P('fsdp', 'tensor'), may hold values from -0.1875 to 0.1875
- w_key: bfloat16 [1024, 1024], P('fsdp', 'tensor'), may hold values from -0.1875 to 0.1875
- w_value: bfloat16 [1024, 1024], P('fsdp', 'tensor'), may hold values from -0.1875 to 0.1875
- head_bias: float32 [2, 16], replicated, may hold values from -1.5 to 1.5
- w_out: bfloat16 [1024, 1024], P('tensor', 'fsdp'), may hold values from -0.75 to 0.75
- ffn_gain: float32 [1024], replicated, may hold values from 0.25 to 1.75
- w_gate: bfloat16 [1024, 4096], P('fsdp', 'tensor'), may hold values from -0.1875 to 0.1875
- w_up: bfloat16 [1024, 4096], P('fsdp', 'tensor'), may hold values from -0.1875 to 0.1875
- w_down: bfloat16 [4096, 1024], P('tensor', 'fsdp'), may hold values from -0.09375 to 0.09375
- cotangent: bfloat16 [2, 4096, 1024], P(None, ('fsdp', 'tensor')), may hold values from -6 to 6
Outputs:
- layer_out: bfloat16 [2, 4096, 1024], P(None, ('fsdp', 'tensor'))
- tokens_grad: bfloat16 [2, 4096, 1024], P(None, ('fsdp', 'tensor'))
- attn_gain_grad: float32 [1024], replicated
- w_query_grad: float32 [1024, 1024], P('fsdp', 'tensor')
- w_key_grad: float32 [1024, 1024], P('fsdp', 'tensor')
- w_value_grad: float32 [1024, 1024], P('fsdp', 'tensor')
- head_bias_grad: float32 [2, 16], replicated
- w_out_grad: float32 [1024, 1024], P('tensor', 'fsdp')
- ffn_gain_grad: float32 [1024], replicated
- w_gate_grad: float32 [1024, 4096], P('fsdp', 'tensor')
- w_up_grad: float32 [1024, 4096], P('fsdp', 'tensor')
- w_down_grad: float32 [4096, 1024], P('tensor', 'fsdp')
The draws below stay inside these ranges and needn't reach their ends.
Inputs may be any that keep to these rules, and one draw needn't show every extreme that they name: `segment_ids`: within each aligned run of 256 tokens (one packed sequence) the ids start at 0, never fall, and each id covers 60 or more consecutive tokens. `variate_ids`: within one document the ids count its variates from 0 upward, each variate's tokens consecutive; a document has at most 4 variates. `time_ids`: the position of a token within its variate's consecutive tokens, from 0.
All inputs are finite; a program needn't handle non-finite values.
Results may differ from the reference program's by a relative error of at most 0.025.
Values may be sent and summed in bfloat16 or wider, within the bound.
A program may use at most 128 MiB of HBM per device.

```python
import jax
import jax.numpy as jnp
from jax import lax

D = 1024
HEADS = 16
HEAD_DIM = 64
FF = 4096
MICRO = 2
DOC_MIN = 60
DOC_MAX = 800
SEQ = 256
TOKENS_MB = 4096


def id_layout(key):
    sequences = MICRO * TOKENS_MB // SEQ
    stride_count = SEQ // DOC_MIN + 1
    key_strides, key_variates = jax.random.split(jax.random.fold_in(key, 11))
    strides = jax.random.randint(key_strides, (sequences, stride_count), DOC_MIN, DOC_MAX // 2 + 1)
    seq_index = jnp.arange(sequences)[:, None]
    strides = jnp.where(seq_index == 0, DOC_MIN, strides)
    strides = jnp.where(seq_index == sequences - 1, SEQ, strides)
    boundary = jnp.cumsum(strides, axis=1)
    usable = boundary <= SEQ - DOC_MIN
    places = jnp.arange(SEQ)
    passed = (boundary[:, None, :] <= places[None, :, None]) & usable[:, None, :]
    segment = jnp.sum(passed.astype(jnp.int32), axis=2)
    opening = jnp.max(jnp.where(passed, boundary[:, None, :], 0), axis=2)
    upcoming = (boundary[:, None, :] > places[None, :, None]) & usable[:, None, :]
    closing = jnp.min(jnp.where(upcoming, boundary[:, None, :], SEQ), axis=2)
    extent = closing - opening
    variates = jax.random.randint(key_variates, (sequences, stride_count + 1), 1, 5)
    variates = jnp.where(seq_index == sequences - 1, 1, variates)
    chosen = jnp.take_along_axis(variates, segment, axis=1)
    offset = places[None, :] - opening
    variate = offset * chosen // extent
    begins = (variate * extent + chosen - 1) // chosen
    moments = offset - begins
    full_shape = (MICRO, TOKENS_MB)
    return (segment.reshape(full_shape), variate.reshape(full_shape), moments.reshape(full_shape))


def draw_segment_ids(key, part):
    return id_layout(key)[0].astype(jnp.int32)


def draw_variate_ids(key, part):
    return id_layout(key)[1].astype(jnp.int32)


def draw_time_ids(key, part):
    return id_layout(key)[2].astype(jnp.int32)


def shard_levels(key, dims, pieces, smallest, top_value):
    factor_of, own = 1.0, jax.random.fold_in(key, 6)
    for dim, blocks in pieces:
        steps = jnp.exp(jax.random.uniform(jax.random.fold_in(own, dim), (blocks,), jnp.float32, smallest / len(pieces), top_value / len(pieces)))
        factor_of = factor_of * jnp.repeat(steps, dims[dim] // blocks).reshape([-1 if axis == dim else 1 for axis in range(len(dims))])
    return factor_of


def centred(own_key, dims, scale, bound, cuts=(), held_as=jnp.bfloat16):
    result = scale * jax.random.normal(own_key, dims, jnp.float32)
    if cuts:
        result = result * shard_levels(own_key, dims, cuts, -0.22, 0.18)
    return jnp.clip(result, -bound, bound).astype(held_as)


def setup_inputs(seed: int = 0) -> dict:
    key_of = jax.random.split(jax.random.key(seed), 16)
    return {
        "tokens": centred(key_of[0], (MICRO, TOKENS_MB, D), 1.0, 6.0, ((1, 32),)),
        "segment_ids": draw_segment_ids(jax.random.fold_in(key_of[15], 71), 0),
        "variate_ids": draw_variate_ids(jax.random.fold_in(key_of[15], 71), 0),
        "time_ids": draw_time_ids(jax.random.fold_in(key_of[15], 71), 0),
        "attn_gain": jnp.clip(1.0 + 0.15 * jax.random.normal(key_of[4], (D,), jnp.float32), 0.25, 1.75),
        "w_query": centred(key_of[5], (D, D), D ** -0.5, 0.1875, ((0, 16), (1, 2))),
        "w_key": centred(key_of[6], (D, D), D ** -0.5, 0.1875, ((0, 16), (1, 2))),
        "w_value": centred(key_of[7], (D, D), D ** -0.5, 0.1875, ((0, 16), (1, 2))),
        "head_bias": jnp.clip(jax.random.uniform(key_of[8], (2, HEADS), jnp.float32, -1.5, 1.5), -1.5, 1.5),
        "w_out": centred(key_of[9], (D, D), (D // 16) ** -0.5, 0.75, ((0, 2), (1, 16))),
        "ffn_gain": jnp.clip(1.0 + 0.15 * jax.random.normal(key_of[10], (D,), jnp.float32), 0.25, 1.75),
        "w_gate": centred(key_of[11], (D, FF), D ** -0.5, 0.1875, ((0, 16), (1, 2))),
        "w_up": centred(key_of[12], (D, FF), D ** -0.5, 0.1875, ((0, 16), (1, 2))),
        "w_down": centred(key_of[13], (FF, D), FF ** -0.5, 0.09375, ((0, 2), (1, 16))),
        "cotangent": centred(key_of[14], (MICRO, TOKENS_MB, D), 1.0, 6.0, ((1, 32),)),
    }


EPS = 1e-06
HIGHEST_PRECISION = lax.Precision.HIGHEST

@jax.custom_vjp
def low(v):
    return lax.optimization_barrier(v.astype(jnp.bfloat16)).astype(jnp.float32)

@jax.custom_vjp
def low_back(v):
    return v

def low_keep(v):
    return (low(v), None)

def low_pass(kept, grad):
    return (grad,)

def back_keep(v):
    return (v, None)

def back_low(kept, grad):
    return (low(grad),)
low.defvjp(low_keep, low_pass)
low_back.defvjp(back_keep, back_low)

def rope_tables(moments, half_width):
    inverse = 10000.0 ** (-(jnp.arange(half_width, dtype=jnp.float32) / half_width))
    angles = moments.astype(jnp.float32)[:, None] * inverse[None, :]
    return (jnp.cos(angles), jnp.sin(angles))

def rotate(values, cosine, sine):
    half_width = values.shape[-1] // 2
    leading = values[..., :half_width]
    trailing = values[..., half_width:]
    cosine = cosine[:, None, :]
    sine = sine[:, None, :]
    return jnp.concatenate([leading * cosine - trailing * sine, trailing * cosine + leading * sine], axis=-1)

def rms_norm(values, gain):
    return values * lax.rsqrt(lax.optimization_barrier(jnp.mean(values * values, axis=-1, keepdims=True)) + EPS) * gain

def matmul(left, right):
    return jnp.dot(left, right, precision=HIGHEST_PRECISION)

def sequence_block(params, resid, segment, variate, moments):
    attn_gain, w_query, w_key, w_value, head_bias, w_out, ffn_gain, w_gate, w_up, w_down = params
    length = resid.shape[0]
    heads_shape = (length, HEADS, HEAD_DIM)
    normed = low(rms_norm(resid, attn_gain))
    query = low_back(matmul(normed, w_query)).reshape(heads_shape)
    keys = low_back(matmul(normed, w_key)).reshape(heads_shape)
    values = low(low_back(matmul(normed, w_value))).reshape(heads_shape)
    cosine, sine = rope_tables(moments, HEAD_DIM // 2)
    query = low(rotate(query, cosine, sine))
    keys = low(rotate(keys, cosine, sine))
    scores = jnp.einsum('qhd,khd->hqk', query, keys, precision=HIGHEST_PRECISION) * HEAD_DIM ** (-0.5)
    same_variate = variate[:, None] == variate[None, :]
    scores = scores + jnp.where(same_variate[None], head_bias[0][:, None, None], head_bias[1][:, None, None])
    scores = low_back(scores)
    allowed = segment[:, None] == segment[None, :]
    scores = jnp.where(allowed[None], scores, -1e+30)
    highest = lax.optimization_barrier(jnp.max(scores, axis=-1, keepdims=True))
    expo = jnp.exp(scores - highest)
    probs = low(expo / lax.optimization_barrier(jnp.sum(expo, axis=-1, keepdims=True)))
    attended = jnp.einsum('hqk,khd->qhd', probs, values, precision=HIGHEST_PRECISION).reshape(length, D)
    attended = low(low_back(attended))
    middle = resid + low_back(matmul(attended, w_out))
    normed_ffn = low(rms_norm(middle, ffn_gain))
    gate = low_back(matmul(normed_ffn, w_gate))
    upward = low_back(matmul(normed_ffn, w_up))
    hidden = low(gate * jax.nn.sigmoid(gate) * upward)
    return middle + low_back(matmul(hidden, w_down))

def reference(tokens, segment_ids, variate_ids, time_ids, attn_gain, w_query, w_key, w_value, head_bias, w_out, ffn_gain, w_gate, w_up, w_down, cotangent):
    sequences = MICRO * TOKENS_MB // SEQ
    inputs = tokens.astype(jnp.float32).reshape(sequences, SEQ, D)
    segments = segment_ids.reshape(sequences, SEQ)
    variates = variate_ids.reshape(sequences, SEQ)
    moments = time_ids.reshape(sequences, SEQ)
    params = tuple((weight.astype(jnp.float32) for weight in (attn_gain, w_query, w_key, w_value, head_bias, w_out, ffn_gain, w_gate, w_up, w_down)))

    def forward(params, inputs):

        def advance(carry, item):
            return (carry, jax.checkpoint(sequence_block)(params, *item))
        unused, outputs = lax.scan(advance, 0, (inputs, segments, variates, moments))
        return outputs
    outputs, pullback = jax.vjp(forward, params, inputs)
    param_grads, input_grads = pullback(cotangent.astype(jnp.float32).reshape(sequences, SEQ, D))
    grad_attn_gain, grad_query, grad_key, grad_value, grad_bias, grad_out, grad_ffn_gain, grad_gate, grad_up, grad_down = param_grads
    full_shape = (MICRO, TOKENS_MB, D)
    return (outputs.reshape(full_shape).astype(jnp.bfloat16), input_grads.reshape(full_shape).astype(jnp.bfloat16), grad_attn_gain, grad_query, grad_key, grad_value, grad_bias, grad_out, grad_ffn_gain, grad_gate, grad_up, grad_down)
```

```python
from functools import partial
from functools import reduce

import jax
import jax.numpy as jnp
import numpy as np
from jax import lax
from jax.experimental import pallas as pl
from jax.experimental.pallas import tpu as pltpu
from jax.sharding import PartitionSpec as P

HEAD_DIM = 64
SEQ_MAX = 1024


EPS = 1e-06


def product(left, right):
    return jnp.dot(left, right, preferred_element_type=jnp.float32)


def product_back(left, right):
    return lax.dot_general(
        left, right, (((1,), (1,)), ((), ())), preferred_element_type=jnp.float32
    )


def outer_sum(left, right):
    return lax.dot_general(
        left, right, (((0,), (0,)), ((), ())), preferred_element_type=jnp.float32
    )


def norm_forward(resid, gain):
    inverse = lax.rsqrt(jnp.mean(resid * resid, axis=-1, keepdims=True) + EPS)
    return (resid * inverse * gain, inverse)


def norm_backward(resid, inverse, gain, upstream):
    scaled = resid * inverse
    weighted = upstream * gain
    back = inverse * (weighted - scaled * jnp.mean(weighted * scaled, axis=-1, keepdims=True))
    return (back, jnp.sum(upstream * scaled, axis=0))


def rope_tables(moments, half_width):
    inverse = 10000.0 ** (-(jnp.arange(half_width, dtype=jnp.float32) / half_width))
    angles = moments.astype(jnp.float32)[:, None] * inverse[None, :]
    return (jnp.cos(angles), jnp.sin(angles))


def rotate(values, cosine, sine):
    half_width = values.shape[-1] // 2
    leading = values[..., :half_width]
    trailing = values[..., half_width:]
    cosine = cosine[:, None, :]
    sine = sine[:, None, :]
    return jnp.concatenate(
        [leading * cosine - trailing * sine, trailing * cosine + leading * sine], axis=-1
    )


def rotate_back(grads, cosine, sine):
    half_width = grads.shape[-1] // 2
    leading = grads[..., :half_width]
    trailing = grads[..., half_width:]
    cosine = cosine[:, None, :]
    sine = sine[:, None, :]
    return jnp.concatenate(
        [leading * cosine + trailing * sine, trailing * cosine - leading * sine], axis=-1
    )


def masked_scores(query, keys, segment, variate, bias_pair):
    scores = jnp.einsum(
        "qhd,khd->hqk", query, keys, preferred_element_type=jnp.float32
    ) * HEAD_DIM ** (-0.5)
    same_variate = variate[:, None] == variate[None, :]
    scores = scores + jnp.where(
        same_variate[None], bias_pair[0][:, None, None], bias_pair[1][:, None, None]
    )
    allowed = segment[:, None] == segment[None, :]
    return (jnp.where(allowed[None], scores, -1e30), same_variate)


def attend_forward(bias_pair, item):
    query, keys, values, segment, variate = item
    scores, unused = masked_scores(query, keys, segment, variate, bias_pair)
    highest = jnp.max(scores, axis=-1, keepdims=True)
    expo = jnp.exp(scores - highest)
    total = jnp.sum(expo, axis=-1, keepdims=True)
    probs = (expo / total).astype(jnp.bfloat16)
    attended = jnp.einsum("hqk,khd->qhd", probs, values, preferred_element_type=jnp.float32)
    return (attended.astype(jnp.bfloat16), (highest + jnp.log(total))[..., 0])


def attend_backward(bias_pair, item):
    query, keys, values, dattended, segment, variate, logsum = item
    scores, same_variate = masked_scores(query, keys, segment, variate, bias_pair)
    probs = jnp.exp(scores - logsum[..., None])
    probs_low = probs.astype(jnp.bfloat16)
    dprobs = jnp.einsum("qhd,khd->hqk", dattended, values, preferred_element_type=jnp.float32)
    dvalues = jnp.einsum("hqk,qhd->khd", probs_low, dattended, preferred_element_type=jnp.float32)
    dscores = (probs * (dprobs - jnp.sum(probs * dprobs, axis=-1, keepdims=True))).astype(
        jnp.bfloat16
    )
    widened = dscores.astype(jnp.float32)
    same_sum = jnp.sum(jnp.where(same_variate[None], widened, 0.0), axis=(1, 2))
    other_sum = jnp.sum(jnp.where(same_variate[None], 0.0, widened), axis=(1, 2))
    dquery = jnp.einsum(
        "hqk,khd->qhd", dscores, keys, preferred_element_type=jnp.float32
    ) * HEAD_DIM ** (-0.5)
    dkeys = jnp.einsum(
        "hqk,qhd->khd", dscores, query, preferred_element_type=jnp.float32
    ) * HEAD_DIM ** (-0.5)
    return (dquery, dkeys, dvalues, jnp.stack([same_sum, other_sum]))


def local(
    tokens,
    segment_ids,
    variate_ids,
    time_ids,
    attn_gain,
    w_query,
    w_key,
    w_value,
    head_bias,
    w_out,
    ffn_gain,
    w_gate,
    w_up,
    w_down,
    cotangent,
):
    micro_count, row_count, model_width = tokens.shape
    group_rows = segment_ids.shape[1]
    seq_len = min(SEQ_MAX, group_rows)
    seq_count = group_rows // seq_len
    local_width = w_query.shape[1]
    local_heads = local_width // HEAD_DIM
    head_start = lax.axis_index("tensor") * local_heads
    bias_pair = lax.dynamic_slice_in_dim(head_bias, head_start, local_heads, 1)
    shards = (w_query, w_key, w_value, w_out, w_gate, w_up, w_down)
    heads_shape = (group_rows, local_heads, HEAD_DIM)
    seq_shape = (seq_count, seq_len, local_heads, HEAD_DIM)

    def spread_normed(block):
        return lax.all_gather(block, "tensor", axis=0, tiled=True)

    def spread_grads(block):
        return lax.all_gather(block, "tensor", axis=0, tiled=True)

    def branch_rows(left, right):
        return lax.psum_scatter(product(left, right), "tensor", scatter_dimension=0, tiled=True)

    def back_rows(lefts, rights):
        pieces = [product_back(left, right) for left, right in zip(lefts, rights)]
        return lax.psum_scatter(reduce(jnp.add, pieces), "tensor", scatter_dimension=0, tiled=True)

    outputs = []
    input_grads = []
    grad_shards = None
    gain_first = jnp.zeros((model_width,), jnp.float32)
    gain_second = jnp.zeros((model_width,), jnp.float32)
    bias_grad = jnp.zeros((2, local_heads), jnp.float32)
    for micro_index in range(micro_count):
        full_weights = (
            lax.all_gather(shards[0], "fsdp", axis=0, tiled=True),
            lax.all_gather(shards[1], "fsdp", axis=0, tiled=True),
            lax.all_gather(shards[2], "fsdp", axis=0, tiled=True),
            lax.all_gather(shards[3], "fsdp", axis=1, tiled=True),
            lax.all_gather(shards[4], "fsdp", axis=0, tiled=True),
            lax.all_gather(shards[5], "fsdp", axis=0, tiled=True),
            lax.all_gather(shards[6], "fsdp", axis=1, tiled=True),
        )
        query_full, key_full, value_full, out_full, gate_full, up_full, down_full = full_weights
        resid = tokens[micro_index].astype(jnp.float32)
        segment = segment_ids[micro_index].reshape(seq_count, seq_len)
        variate = variate_ids[micro_index].reshape(seq_count, seq_len)
        cosine, sine = rope_tables(time_ids[micro_index], HEAD_DIM // 2)
        normed, inverse_first = norm_forward(resid, attn_gain)
        normed_all = spread_normed(normed.astype(jnp.bfloat16))
        query = rotate(product(normed_all, query_full).reshape(heads_shape), cosine, sine).astype(
            jnp.bfloat16
        )
        keys = rotate(product(normed_all, key_full).reshape(heads_shape), cosine, sine).astype(
            jnp.bfloat16
        )
        values = product(normed_all, value_full).astype(jnp.bfloat16)
        query_seq = query.reshape(seq_shape)
        keys_seq = keys.reshape(seq_shape)
        values_seq = values.reshape(seq_shape)
        attended, logsum = lax.map(
            partial(attend_forward, bias_pair), (query_seq, keys_seq, values_seq, segment, variate)
        )
        attended = attended.reshape(group_rows, local_width)
        middle = resid + branch_rows(attended, out_full)
        normed_ffn, inverse_second = norm_forward(middle, ffn_gain)
        normed_ffn_all = spread_normed(normed_ffn.astype(jnp.bfloat16))
        gate = product(normed_ffn_all, gate_full)
        upward = product(normed_ffn_all, up_full)
        sigmoid = jax.nn.sigmoid(gate)
        hidden = (gate * sigmoid * upward).astype(jnp.bfloat16)
        outputs.append((middle + branch_rows(hidden, down_full)).astype(jnp.bfloat16))
        full_weights = (
            lax.all_gather(shards[0], "fsdp", axis=0, tiled=True),
            lax.all_gather(shards[1], "fsdp", axis=0, tiled=True),
            lax.all_gather(shards[2], "fsdp", axis=0, tiled=True),
            lax.all_gather(shards[3], "fsdp", axis=1, tiled=True),
            lax.all_gather(shards[4], "fsdp", axis=0, tiled=True),
            lax.all_gather(shards[5], "fsdp", axis=0, tiled=True),
            lax.all_gather(shards[6], "fsdp", axis=1, tiled=True),
        )
        query_full, key_full, value_full, out_full, gate_full, up_full, down_full = full_weights
        grad_out = cotangent[micro_index].astype(jnp.float32)
        grad_ffn_all = spread_grads(cotangent[micro_index])
        dhidden = product_back(grad_ffn_all, down_full)
        dgate = (dhidden * upward * (sigmoid + gate * sigmoid * (1.0 - sigmoid))).astype(
            jnp.bfloat16
        )
        dupward = (dhidden * gate * sigmoid).astype(jnp.bfloat16)
        dnormed_ffn = back_rows((dgate, dupward), (gate_full, up_full))
        grad_gate = outer_sum(normed_ffn_all, dgate)
        grad_up = outer_sum(normed_ffn_all, dupward)
        grad_down = outer_sum(hidden, grad_ffn_all)
        dmiddle, gain_term = norm_backward(middle, inverse_second, ffn_gain, dnormed_ffn)
        gain_second = gain_second + gain_term
        dmiddle = dmiddle + grad_out
        grad_attn_all = spread_grads(dmiddle.astype(jnp.bfloat16))
        dattended = product_back(grad_attn_all, out_full).astype(jnp.bfloat16)
        grad_out_proj = outer_sum(attended, grad_attn_all)
        back_items = (
            query_seq,
            keys_seq,
            values_seq,
            dattended.reshape(seq_shape),
            segment,
            variate,
            logsum,
        )
        dquery, dkeys, dvalues, bias_terms = lax.map(
            partial(attend_backward, bias_pair), back_items
        )
        bias_grad = bias_grad + jnp.sum(bias_terms, axis=0)
        dquery = (
            rotate_back(dquery.reshape(heads_shape), cosine, sine)
            .astype(jnp.bfloat16)
            .reshape(group_rows, local_width)
        )
        dkeys = (
            rotate_back(dkeys.reshape(heads_shape), cosine, sine)
            .astype(jnp.bfloat16)
            .reshape(group_rows, local_width)
        )
        dvalues = dvalues.astype(jnp.bfloat16).reshape(group_rows, local_width)
        dnormed = back_rows((dquery, dkeys, dvalues), (query_full, key_full, value_full))
        grad_query = outer_sum(normed_all, dquery)
        grad_key = outer_sum(normed_all, dkeys)
        grad_value = outer_sum(normed_all, dvalues)
        dresid, gain_term = norm_backward(resid, inverse_first, attn_gain, dnormed)
        gain_first = gain_first + gain_term
        input_grads.append((dresid + dmiddle).astype(jnp.bfloat16))
        summed = (
            lax.psum_scatter(
                grad_query.astype(jnp.bfloat16), "fsdp", scatter_dimension=0, tiled=True
            ).astype(jnp.float32),
            lax.psum_scatter(
                grad_key.astype(jnp.bfloat16), "fsdp", scatter_dimension=0, tiled=True
            ).astype(jnp.float32),
            lax.psum_scatter(
                grad_value.astype(jnp.bfloat16), "fsdp", scatter_dimension=0, tiled=True
            ).astype(jnp.float32),
            lax.psum_scatter(
                grad_out_proj.astype(jnp.bfloat16), "fsdp", scatter_dimension=1, tiled=True
            ).astype(jnp.float32),
            lax.psum_scatter(
                grad_gate.astype(jnp.bfloat16), "fsdp", scatter_dimension=0, tiled=True
            ).astype(jnp.float32),
            lax.psum_scatter(
                grad_up.astype(jnp.bfloat16), "fsdp", scatter_dimension=0, tiled=True
            ).astype(jnp.float32),
            lax.psum_scatter(
                grad_down.astype(jnp.bfloat16), "fsdp", scatter_dimension=1, tiled=True
            ).astype(jnp.float32),
        )
        grad_shards = summed if grad_shards is None else jax.tree.map(jnp.add, grad_shards, summed)
    bias_full = lax.dynamic_update_slice_in_dim(
        jnp.zeros((2, head_bias.shape[1]), jnp.float32), bias_grad, head_start, 1
    )
    gain_first, gain_second, bias_full = lax.psum(
        (gain_first, gain_second, bias_full), ("fsdp", "tensor")
    )
    return (
        jnp.stack(outputs),
        jnp.stack(input_grads),
        gain_first,
        grad_shards[0],
        grad_shards[1],
        grad_shards[2],
        bias_full,
        grad_shards[3],
        gain_second,
        grad_shards[4],
        grad_shards[5],
        grad_shards[6],
    )


BF = jnp.bfloat16
F32 = jnp.float32
MESH = pl.DeviceIdType.MESH
SHARD = 64
SEQ_LEN = 256
HALF = 128
WIDTH = 1024
LOCAL = 512
HIDDEN = 2048
PAIRS = 4
COL_QKV, COL_OUT, COL_GATE, COL_UP, COL_DOWN = 0, 1536, 2048, 4096, 6144
ALL_COLS = 8192
GATHER_PIECES = (
    (0, 768),
    (768, 768),
    (1536, 512),
    (2048, 1024),
    (3072, 1024),
    (4096, 1024),
    (5120, 1024),
    (6144, 1024),
    (7168, 1024),
)
CHUNK = 2048
PIECE = 1024
NEGATIVE = -1e30


def mm(left, right):
    return jnp.dot(left, right, preferred_element_type=F32)


def mm_nt(left, right):
    return lax.dot_general(left, right, (((1,), (1,)), ((), ())), preferred_element_type=F32)


def mm_tn(left, right):
    return lax.dot_general(left, right, (((0,), (0,)), ((), ())), preferred_element_type=F32)


def layer_kernel(
    tok_ref,
    cot_in,
    seg_ref,
    var_ref,
    time_ref,
    again_ref,
    fgain_ref,
    freq_ref,
    bias_ref,
    wq_ref,
    wk_ref,
    wv_ref,
    wo_ref,
    wg_ref,
    wu_ref,
    wd_ref,
    out_ref,
    tgrad_ref,
    gqkvo_ref,
    gg_ref,
    gu_ref,
    gd_ref,
    sv_ref,
    W,
    GD,
    RC,
    RX,
    RZ,
    X,
    COT,
    N1,
    NF,
    Q,
    K,
    V,
    ATT,
    PT,
    MID,
    GT,
    UP,
    HID,
    YS,
    YR,
    YDS,
    YDR,
    YNR,
    T,
    SAME,
    NEGM,
    COS,
    SIN,
    GF,
    GA,
    BS,
    SV,
    SR,
    local_sem,
    ag_send,
    ag_recv,
    rs_send,
    rs_recv,
    y_send,
    y_recv,
    sv_send,
    sv_recv,
    credit,
):
    f = lax.axis_index("fsdp")
    y = lax.axis_index("tensor")
    z, x, c = f // 4, (f // 2) % 2, f % 2
    zs = (z + 1 - 2 * (z % 2), (z + 2) % 4, 3 - z)
    z_devs = [(zk * 4 + x * 2 + c, y) for zk in zs]
    x_dev = (z * 4 + (1 - x) * 2 + c, y)
    c_dev = (z * 4 + x * 2 + 1 - c, y)
    y_dev = (f, 1 - y)
    partners = z_devs + [x_dev, c_dev, y_dev]

    def remote(src, dst, send, recv, dev):
        return pltpu.make_async_remote_copy(
            src_ref=src, dst_ref=dst, send_sem=send, recv_sem=recv, device_id=dev, device_id_type=MESH
        )

    barrier = pltpu.get_barrier_semaphore()
    for dev in partners:
        pl.semaphore_signal(barrier, inc=1, device_id=dev, device_id_type=MESH)
    own_rows = pl.ds(pl.multiple_of(y * HALF, HALF), HALF)
    other_rows = pl.ds(pl.multiple_of((1 - y) * HALF, HALF), HALF)
    loads = [
        (tok_ref, X.at[:, own_rows]),
        (cot_in, COT.at[:, own_rows]),
        (wq_ref, W.at[z, x, c, :, pl.ds(0, LOCAL)]),
        (wk_ref, W.at[z, x, c, :, pl.ds(LOCAL, LOCAL)]),
        (wv_ref, W.at[z, x, c, :, pl.ds(2 * LOCAL, LOCAL)]),
        (wo_ref, W.at[z, x, c, :, pl.ds(COL_OUT, LOCAL)]),
        (wg_ref, W.at[z, x, c, :, pl.ds(COL_GATE, HIDDEN)]),
        (wu_ref, W.at[z, x, c, :, pl.ds(COL_UP, HIDDEN)]),
        (wd_ref, W.at[z, x, c, :, pl.ds(COL_DOWN, HIDDEN)]),
    ]
    loads = [
        pltpu.make_async_copy(src, dst, local_sem.at[i]) for i, (src, dst) in enumerate(loads)
    ]
    for load in loads:
        load.start()
    for load in loads:
        load.wait()
    pl.semaphore_wait(barrier, len(partners))

    pieces = len(GATHER_PIECES)
    ag_z, ag_x, ag_c = [], [], []
    for i, (c0, n) in enumerate(GATHER_PIECES):
        cols = pl.ds(c0, n)
        block = W.at[z, x, c, :, cols]
        ag_z.append(
            [
                remote(block, block, ag_send.at[i * 5 + k], ag_recv.at[i * 5 + k], z_devs[k])
                for k in range(3)
            ]
        )
        block = W.at[:, x, c, :, cols]
        ag_x.append(remote(block, block, ag_send.at[i * 5 + 3], ag_recv.at[i * 5 + 3], x_dev))
        block = W.at[:, :, c, :, cols]
        ag_c.append(remote(block, block, ag_send.at[i * 5 + 4], ag_recv.at[i * 5 + 4], c_dev))
    for copies in ag_z:
        for copy in copies:
            copy.start()
    y_tok = remote(X.at[:, own_rows], X.at[:, own_rows], y_send.at[0], y_recv.at[0], y_dev)
    y_cot = remote(COT.at[:, own_rows], COT.at[:, own_rows], y_send.at[1], y_recv.at[1], y_dev)
    y_tok.start()
    y_cot.start()

    def gather_x(i):
        for copy in ag_z[i]:
            copy.wait_recv()
        ag_x[i].start()

    def gather_c(i):
        ag_x[i].wait_recv()
        ag_c[i].start()

    def gather_end(i):
        ag_c[i].wait_recv()

    lane = lax.broadcasted_iota(jnp.int32, (1, 128), 1)
    low_lane = lane < 64
    lead_lane = (lane % 64) < 32

    def column(row):
        return jnp.transpose(jnp.broadcast_to(row.astype(F32), (128, SEQ_LEN)))

    for s in range(2):
        moments = column(time_ref[s : s + 1, :])
        angles = moments * freq_ref[...]
        COS[s] = jnp.cos(angles)
        sine = jnp.sin(angles)
        SIN[s] = jnp.where(lead_lane, -sine, sine)
        seg_row = seg_ref[s : s + 1, :].astype(F32)
        var_row = var_ref[s : s + 1, :].astype(F32)
        seg_col = column(seg_ref[s : s + 1, :])
        var_col = column(var_ref[s : s + 1, :])
        for h in range(2):
            part = slice(h * 128, (h + 1) * 128)
            SAME[s, :, part] = jnp.where(var_col == var_row[:, part], 1.0, 0.0)
            NEGM[s, :, part] = jnp.where(seg_col == seg_row[:, part], 0.0, NEGATIVE)

    def swap(values):
        return jnp.where(
            lead_lane, pltpu.roll(values, 96, axis=1), pltpu.roll(values, 32, axis=1)
        )

    ROWS = 64
    BLOCKS = SEQ_LEN // ROWS

    def row_loop(body):
        def step(b, carry):
            body(b, pl.ds(pl.multiple_of(b * ROWS, ROWS), ROWS))
            return carry

        lax.fori_loop(0, BLOCKS, step, 0)

    def tile_loop(count, body):
        def step(j, carry):
            body(j)
            return carry

        lax.fori_loop(0, count, step, 0)

    def tile_cols(base, j, size=256):
        return pl.ds(pl.multiple_of(base + j * size, size), size)

    def w_tile(cols):
        return W[:, :, :, :, cols].reshape(WIDTH, 256)

    def w_rows(zi, c0, n):
        return W[zi, :, :, :, pl.ds(c0, n)].reshape(256, n)

    def transpose_into(src):
        for s in range(2):

            def body(j):
                cols = tile_cols(0, j)
                T[cols, s * SEQ_LEN : (s + 1) * SEQ_LEN] = jnp.transpose(src[s, :, cols])

            tile_loop(4, body)

    y_tok.wait_recv()
    for s in range(2):

        def body(b, rows):
            v = X[s, rows, :].astype(F32)
            inv = lax.rsqrt(jnp.mean(v * v, axis=-1, keepdims=True) + EPS)
            N1[s, rows, :] = (v * inv * again_ref[...]).astype(BF)

        row_loop(body)

    for i in range(3):
        gather_x(i)
    for i in range(3):
        gather_c(i)
    gather_end(0)
    gather_end(1)

    for kind, dest in enumerate((Q, K, V)):

        def body(j):
            r = mm(N1[...].reshape(2 * SEQ_LEN, WIDTH), w_tile(tile_cols(kind * LOCAL, j)))
            for h in range(2):
                part = r[:, h * 128 : (h + 1) * 128]
                if kind < 2:
                    cosine = COS[...].reshape(2 * SEQ_LEN, 128)
                    sine = SIN[...].reshape(2 * SEQ_LEN, 128)
                    part = part * cosine + swap(part) * sine
                dest[:, :, pl.ds(pl.multiple_of(j * 256 + h * 128, 128), 128)] = part.astype(
                    BF
                ).reshape(2, SEQ_LEN, 128)

        tile_loop(2, body)

    def stacked(values):
        zero = jnp.zeros_like(values)
        return jnp.concatenate(
            [jnp.where(low_lane, values, zero), jnp.where(low_lane, zero, values)], axis=0
        )

    def pair_cols(p):
        return pl.ds(pl.multiple_of(p * 128, 128), 128)

    y_att = [
        remote(YS.at[s], YR.at[s], y_send.at[2 + s], y_recv.at[2 + s], y_dev) for s in range(2)
    ]
    for s in range(2):

        def body(p):
            cols = pair_cols(p)
            keys = stacked(K[s, :, cols] * jnp.asarray(0.125, BF))
            scores = mm_nt(keys, Q[s, :, cols])
            parts = []
            for h in range(2):
                head = y * 8 + p * 2 + h
                same_bias = bias_ref[0, head]
                other_bias = bias_ref[1, head]
                sc = scores[h * SEQ_LEN : (h + 1) * SEQ_LEN]
                sc = sc + (SAME[s] * (same_bias - other_bias) + (NEGM[s] + other_bias))
                top = jnp.max(sc, axis=0, keepdims=True)
                expo = jnp.exp(sc - top)
                total = jnp.sum(expo, axis=0, keepdims=True)
                parts.append((expo * (1.0 / total)).astype(BF))
            probs = jnp.concatenate(parts, axis=0)
            PT[s * PAIRS + p] = probs
            ATT[s, :, cols] = mm_tn(probs, stacked(V[s, :, cols])).astype(BF)

        tile_loop(PAIRS, body)
        if s == 0:
            gather_end(2)
        for zi in range(4):
            YS[s, :, zi * 256 : (zi + 1) * 256] = mm_nt(
                ATT[s], w_rows(zi, COL_OUT, LOCAL)
            ).astype(BF)
        y_att[s].start()

    gather_x(3)
    gather_x(4)
    gather_c(3)
    gather_c(4)
    for s in range(2):
        y_att[s].wait_recv()

        def body(b, rows):
            v = X[s, rows, :].astype(F32) + (YS[s, rows, :].astype(F32) + YR[s, rows, :].astype(F32))
            MID[s, rows, :] = v
            inv = lax.rsqrt(jnp.mean(v * v, axis=-1, keepdims=True) + EPS)
            NF[s, rows, :] = (v * inv * fgain_ref[...]).astype(BF)

        row_loop(body)
    for s in range(2):
        y_att[s].wait_send()
    pl.semaphore_signal(credit, inc=1, device_id=y_dev, device_id_type=MESH)

    gather_end(3)
    gather_end(4)

    def body(j):
        GT[:, tile_cols(0, j)] = mm(
            NF[...].reshape(2 * SEQ_LEN, WIDTH), w_tile(tile_cols(COL_GATE, j))
        ).astype(BF)

    tile_loop(8, body)
    gather_x(5)
    gather_x(6)
    y_cot.wait_recv()
    transpose_into(COT)
    gather_c(5)
    gather_c(6)
    gather_end(5)
    gather_end(6)

    def body(j):
        cols = tile_cols(0, j)
        up = mm(NF[...].reshape(2 * SEQ_LEN, WIDTH), w_tile(tile_cols(COL_UP, j)))
        UP[:, cols] = up.astype(BF)
        gate = GT[:, cols].astype(F32)
        HID[:, cols] = (gate * jax.nn.sigmoid(gate) * up).astype(BF)

    tile_loop(8, body)

    homes = ((GD, 0), (W, COL_DOWN), (W, COL_GATE), (W, COL_UP))
    results = (gd_ref, gg_ref, gu_ref, gqkvo_ref)

    def home(ch, *index, c0=0, n=CHUNK):
        ref, base = homes[ch]
        return ref.at[index + (slice(None), pl.ds(base + c0, n))]

    halves = CHUNK // PIECE
    per_chunk = 1 + 4 * halves
    rs_c, rs_x, rs_z = [], [], []
    every = slice(None)
    for ch in range(4):
        base = ch * per_chunk
        rs_c.append(
            remote(home(ch, every, every, 1 - c), RC.at[ch], rs_send.at[base], rs_recv.at[base], c_dev)
        )
        xs, zcopies = [], []
        for i in range(halves):
            n0 = base + 1 + i * 4
            cols = pl.ds(i * PIECE, PIECE)
            xs.append(
                remote(
                    home(ch, every, 1 - x, c, c0=i * PIECE, n=PIECE),
                    RX.at[ch, :, :, cols],
                    rs_send.at[n0],
                    rs_recv.at[n0],
                    x_dev,
                )
            )
            zcopies.append(
                [
                    remote(
                        home(ch, zs[k], x, c, c0=i * PIECE, n=PIECE),
                        RZ.at[ch, k, :, cols],
                        rs_send.at[n0 + 1 + k],
                        rs_recv.at[n0 + 1 + k],
                        z_devs[k],
                    )
                    for k in range(3)
                ]
            )
        rs_x.append(xs)
        rs_z.append(zcopies)

    def add_core(ch, xi):
        ref, base = homes[ch]

        def body(zi):
            view = ref.at[zi, xi, c, :, pl.ds(base, CHUNK)]
            view[...] = view[...] + RC[ch, zi, xi]

        tile_loop(4, body)

    def scatter_core(ch):
        rs_c[ch].start()

    def scatter_x(ch):
        rs_c[ch].wait_recv()
        add_core(ch, 1 - x)
        for copy in rs_x[ch]:
            copy.start()
        add_core(ch, x)

    def scatter_z(ch):
        ref, base = homes[ch]
        for i in range(halves):
            rs_x[ch][i].wait_recv()

            def body(zi):
                view = ref.at[zi, x, c, :, pl.ds(base + i * PIECE, PIECE)]
                view[...] = view[...] + RX[ch, zi, :, pl.ds(i * PIECE, PIECE)]

            tile_loop(4, body)
            for copy in rs_z[ch][i]:
                copy.start()

    def scatter_end(ch):
        ref, base = homes[ch]
        for i in range(halves):
            for copy in rs_z[ch][i]:
                copy.wait_recv()

            def body(j):
                cols = tile_cols(i * PIECE, j)
                total = ref[z, x, c, :, tile_cols(base + i * PIECE, j)].astype(F32)
                for k in range(3):
                    total = total + RZ[ch, k, :, cols].astype(F32)
                results[ch][:, cols] = total

            tile_loop(PIECE // 256, body)

    def weight_grad(ch, c0, right, r0, count):
        ref, base = homes[ch]

        def body(j):
            r = mm(T[...], right(j, r0))
            ref[:, :, :, :, tile_cols(base + c0, j)] = r.astype(BF).reshape(4, 2, 2, SHARD, 256)

        tile_loop(count, body)

    weight_grad(0, 0, lambda j, r0: HID[:, tile_cols(r0, j)], 0, 8)
    scatter_core(0)
    transpose_into(NF)
    gather_x(7)
    gather_x(8)
    gather_c(7)
    gather_c(8)
    scatter_x(0)
    gather_end(7)
    gather_end(8)

    def body(j):
        cols = tile_cols(0, j)
        dhid = mm(COT[...].reshape(2 * SEQ_LEN, WIDTH), w_tile(tile_cols(COL_DOWN, j)))
        gate = GT[:, cols].astype(F32)
        up = UP[:, cols].astype(F32)
        sig = jax.nn.sigmoid(gate)
        GT[:, cols] = (dhid * up * (sig + gate * sig * (1.0 - sig))).astype(BF)
        UP[:, cols] = (dhid * gate * sig).astype(BF)

    tile_loop(8, body)

    y_dnf = [
        remote(YS.at[s], YR.at[s], y_send.at[4 + s], y_recv.at[4 + s], y_dev) for s in range(2)
    ]
    pl.semaphore_wait(credit, 1)
    for s in range(2):
        rows = slice(s * SEQ_LEN, (s + 1) * SEQ_LEN)

        def body(zi):
            r = mm_nt(GT[rows, :], w_rows(zi, COL_GATE, HIDDEN))
            r = r + mm_nt(UP[rows, :], w_rows(zi, COL_UP, HIDDEN))
            YS[s, :, tile_cols(0, zi)] = r.astype(BF)

        tile_loop(4, body)
        y_dnf[s].start()

    def body(zi):
        r = mm_nt(HID[...], w_rows(zi, COL_DOWN, HIDDEN))
        YDS[:, :, tile_cols(0, zi)] = r.astype(BF).reshape(2, SEQ_LEN, 256)

    tile_loop(4, body)
    y_out = remote(YDS.at[:, other_rows], YDR, y_send.at[6], y_recv.at[6], y_dev)
    y_out.start()
    for copies in (ag_c, ag_x):
        for copy in copies:
            copy.wait_send()
    for copies in ag_z:
        for copy in copies:
            copy.wait_send()

    weight_grad(1, 0, lambda j, r0: GT[:, tile_cols(r0, j)], 0, 8)
    scatter_core(1)
    scatter_z(0)
    scatter_x(1)
    weight_grad(2, 0, lambda j, r0: UP[:, tile_cols(r0, j)], 0, 8)
    scatter_core(2)

    GF[...] = jnp.zeros_like(GF)
    GA[...] = jnp.zeros_like(GA)
    y_out.wait_recv()
    for s in range(2):

        def body(b, carry):
            rows = pl.ds(pl.multiple_of(b * ROWS, ROWS), ROWS)
            mine = pl.ds(pl.multiple_of(y * HALF + b * ROWS, ROWS), ROWS)
            out_ref[s, rows, :] = (
                MID[s, mine, :] + (YDS[s, mine, :].astype(F32) + YDR[s, rows, :].astype(F32))
            ).astype(BF)
            return carry

        lax.fori_loop(0, HALF // ROWS, body, 0)
    y_out.wait_send()

    DML = YDS
    DAT = HID.at[:, 3 * LOCAL : 4 * LOCAL]
    DQKV = HID
    dout = DAT
    for s in range(2):
        y_dnf[s].wait_recv()

        def body(b, rows):
            v = MID[s, rows, :]
            inv = lax.rsqrt(jnp.mean(v * v, axis=-1, keepdims=True) + EPS)
            scaled = v * inv
            dn = YS[s, rows, :].astype(F32) + YR[s, rows, :].astype(F32)
            flag = jnp.where(b // (HALF // ROWS) == y, 1.0, 0.0)
            GF[...] += flag * jnp.sum((dn * scaled).reshape(ROWS // 8, 8, WIDTH), axis=0)
            u = dn * fgain_ref[...]
            dm = COT[s, rows, :].astype(F32) + inv * (
                u - scaled * jnp.mean(u * scaled, axis=-1, keepdims=True)
            )
            MID[s, rows, :] = dm
            DML[s, rows, :] = dm.astype(BF)

        row_loop(body)
        if s == 0:
            scatter_x(2)
            scatter_z(1)
        seq_rows = slice(s * SEQ_LEN, (s + 1) * SEQ_LEN)

        def body(j):
            dout[seq_rows, tile_cols(0, j)] = mm(DML[s], w_tile(tile_cols(COL_OUT, j))).astype(BF)

        tile_loop(2, body)

        def body(p):
            cols = pair_cols(p)
            do = dout[seq_rows, cols]
            dprobs = mm_nt(stacked(V[s, :, cols]), do)
            probs_low = PT[s * PAIRS + p]
            parts = []
            for h in range(2):
                part = slice(h * SEQ_LEN, (h + 1) * SEQ_LEN)
                pr = probs_low[part].astype(F32)
                dp = dprobs[part]
                dot = jnp.sum(pr * dp, axis=0, keepdims=True)
                ds = (pr * (dp - dot)).astype(BF)
                wide = ds.astype(F32)
                same = wide * SAME[s]
                same_sum = jnp.sum(same, axis=0, keepdims=True)
                other_sum = jnp.sum(wide - same, axis=0, keepdims=True)
                if s == 0:
                    BS[0, p * 2 + h] = same_sum
                    BS[1, p * 2 + h] = other_sum
                else:
                    BS[0, p * 2 + h] += same_sum
                    BS[1, p * 2 + h] += other_sum
                parts.append(ds)
            dsc = jnp.concatenate(parts, axis=0)
            dv = mm(probs_low, do)
            dv = jnp.where(low_lane, dv[:SEQ_LEN], dv[SEQ_LEN:])
            dk = mm(dsc, Q[s, :, cols])
            dk = jnp.where(low_lane, dk[:SEQ_LEN], dk[SEQ_LEN:]) * 0.125
            dq = mm_tn(dsc, stacked(K[s, :, cols] * jnp.asarray(0.125, BF)))
            dq = dq * COS[s] - swap(dq) * SIN[s]
            dk = dk * COS[s] - swap(dk) * SIN[s]
            DQKV[seq_rows, cols] = dq.astype(BF)
            DQKV[seq_rows, pl.ds(pl.multiple_of(LOCAL + p * 128, 128), 128)] = dk.astype(BF)
            DQKV[seq_rows, pl.ds(pl.multiple_of(2 * LOCAL + p * 128, 128), 128)] = dv.astype(BF)

        tile_loop(PAIRS, body)

    for s in range(2):
        y_dnf[s].wait_send()
    y_dn = [
        remote(YS.at[s, other_rows], YNR.at[s], y_send.at[7 + s], y_recv.at[7 + s], y_dev)
        for s in range(2)
    ]
    for s in range(2):
        seq_rows = slice(s * SEQ_LEN, (s + 1) * SEQ_LEN)

        def body(zi):
            r = mm_nt(DQKV[seq_rows, 0 : 3 * LOCAL], w_rows(zi, COL_QKV, 3 * LOCAL))
            YS[s, :, tile_cols(0, zi)] = r.astype(BF)

        tile_loop(4, body)
        y_dn[s].start()

    scatter_z(2)
    transpose_into(DML)
    weight_grad(3, 3 * LOCAL, lambda j, r0: ATT[:, :, tile_cols(r0, j)].reshape(512, 256), 0, 2)
    transpose_into(N1)
    weight_grad(3, 0, lambda j, r0: DQKV[:, tile_cols(r0, j)], 0, 6)
    scatter_core(3)
    scatter_end(0)
    scatter_x(3)
    scatter_end(1)

    for s in range(2):
        y_dn[s].wait_recv()

        def body(b, carry):
            rows = pl.ds(pl.multiple_of(b * ROWS, ROWS), ROWS)
            mine = pl.ds(pl.multiple_of(y * HALF + b * ROWS, ROWS), ROWS)
            v = X[s, mine, :].astype(F32)
            inv = lax.rsqrt(jnp.mean(v * v, axis=-1, keepdims=True) + EPS)
            scaled = v * inv
            dn = YS[s, mine, :].astype(F32) + YNR[s, rows, :].astype(F32)
            GA[...] += jnp.sum((dn * scaled).reshape(ROWS // 8, 8, WIDTH), axis=0)
            u = dn * again_ref[...]
            dx = MID[s, mine, :] + inv * (
                u - scaled * jnp.mean(u * scaled, axis=-1, keepdims=True)
            )
            tgrad_ref[s, rows, :] = dx.astype(BF)
            return carry

        lax.fori_loop(0, HALF // ROWS, body, 0)

    SV[0] = jnp.zeros((16, WIDTH), F32)
    SV[0, 0:1, :] = jnp.sum(GA[...], axis=0, keepdims=True)
    SV[0, 1:2, :] = jnp.sum(GF[...], axis=0, keepdims=True)
    for kind in range(2):
        cols = pl.ds(pl.multiple_of((y * 2 + kind) * 128, 128), 128)
        for h in range(8):
            row = BS[kind, h]
            SV[0, 8 + h : 9 + h, cols] = row[:, 0:128] + row[:, 128:256]

    sums = [
        [remote(SV.at[0], SR.at[0], sv_send.at[0], sv_recv.at[0], c_dev)],
        [remote(SV.at[1], SR.at[1], sv_send.at[1], sv_recv.at[1], x_dev)],
        [
            remote(SV.at[2], SR.at[2 + k], sv_send.at[2 + k], sv_recv.at[2 + k], z_devs[k])
            for k in range(3)
        ],
        [remote(SV.at[3], SR.at[5], sv_send.at[5], sv_recv.at[5], y_dev)],
    ]

    def sum_stage(i):
        total = SV[i]
        for copy in sums[i]:
            copy.wait_recv()
        first = (0, 1, 2, 5)[i]
        for k in range(len(sums[i])):
            total = total + SR[first + k]
        if i < 3:
            SV[i + 1] = total
            for copy in sums[i + 1]:
                copy.start()
        else:
            sv_ref[...] = total

    sums[0][0].start()
    sum_stage(0)
    sum_stage(1)
    scatter_end(2)
    sum_stage(2)
    scatter_z(3)
    sum_stage(3)
    scatter_end(3)

    for s in range(2):
        y_dn[s].wait_send()
    y_tok.wait_send()
    y_cot.wait_send()
    for group in sums:
        for copy in group:
            copy.wait_send()
    for ch in range(4):
        rs_c[ch].wait_send()
        for i in range(halves):
            rs_x[ch][i].wait_send()
            for copy in rs_z[ch][i]:
                copy.wait_send()


def fused_local(
    tokens,
    segment_ids,
    variate_ids,
    time_ids,
    attn_gain,
    w_query,
    w_key,
    w_value,
    head_bias,
    w_out,
    ffn_gain,
    w_gate,
    w_up,
    w_down,
    cotangent,
):
    inverse = 10000.0 ** (-(np.arange(32, dtype=np.float32) / np.float32(32)))
    freq = jnp.asarray(np.tile(inverse.astype(np.float32), 4)[None, :])
    vmem = pl.BlockSpec(memory_space=pltpu.VMEM)
    anym = pl.BlockSpec(memory_space=pl.ANY)
    smem = pl.BlockSpec(memory_space=pltpu.SMEM)
    bf = lambda *shape: pltpu.VMEM(shape, BF)
    fl = lambda *shape: pltpu.VMEM(shape, F32)
    seq3 = (2, SEQ_LEN, WIDTH)
    half3 = (2, HALF, WIDTH)
    pieces = len(GATHER_PIECES)
    per_chunk = 1 + 4 * (CHUNK // PIECE)
    dma = pltpu.SemaphoreType.DMA
    scratch = [
        bf(4, 2, 2, SHARD, ALL_COLS),
        bf(4, 2, 2, SHARD, CHUNK),
        bf(4, 4, 2, SHARD, CHUNK),
        bf(4, 4, SHARD, CHUNK),
        bf(4, 3, SHARD, CHUNK),
        bf(*seq3),
        bf(*seq3),
        bf(*seq3),
        bf(*seq3),
        bf(2, SEQ_LEN, LOCAL),
        bf(2, SEQ_LEN, LOCAL),
        bf(2, SEQ_LEN, LOCAL),
        bf(2, SEQ_LEN, LOCAL),
        bf(2 * PAIRS, 2 * SEQ_LEN, SEQ_LEN),
        fl(*seq3),
        bf(2 * SEQ_LEN, HIDDEN),
        bf(2 * SEQ_LEN, HIDDEN),
        bf(2 * SEQ_LEN, HIDDEN),
        bf(*seq3),
        bf(*seq3),
        bf(*seq3),
        bf(*half3),
        bf(*half3),
        bf(WIDTH, 2 * SEQ_LEN),
        fl(2, SEQ_LEN, SEQ_LEN),
        fl(2, SEQ_LEN, SEQ_LEN),
        fl(2, SEQ_LEN, 128),
        fl(2, SEQ_LEN, 128),
        fl(8, WIDTH),
        fl(8, WIDTH),
        fl(2, 8, 1, SEQ_LEN),
        fl(4, 16, WIDTH),
        fl(6, 16, WIDTH),
        dma((9,)),
        dma((5 * pieces,)),
        dma((5 * pieces,)),
        dma((4 * per_chunk,)),
        dma((4 * per_chunk,)),
        dma((9,)),
        dma((9,)),
        dma((6,)),
        dma((6,)),
        pltpu.SemaphoreType.REGULAR,
    ]
    shape = jax.ShapeDtypeStruct
    outs = pl.pallas_call(
        layer_kernel,
        out_shape=(
            shape(half3, BF),
            shape(half3, BF),
            shape((SHARD, HIDDEN), F32),
            shape((SHARD, HIDDEN), F32),
            shape((SHARD, HIDDEN), F32),
            shape((SHARD, HIDDEN), F32),
            shape((16, WIDTH), F32),
        ),
        in_specs=[anym, anym, vmem, vmem, vmem, vmem, vmem, vmem, smem] + [anym] * 7,
        out_specs=(vmem,) * 7,
        scratch_shapes=scratch,
        compiler_params=pltpu.CompilerParams(
            collective_id=0, has_side_effects=True, vmem_limit_bytes=67043328
        ),
        name="layer",
    )(
        tokens,
        cotangent,
        segment_ids,
        variate_ids,
        time_ids,
        attn_gain.reshape(1, WIDTH),
        ffn_gain.reshape(1, WIDTH),
        freq,
        head_bias,
        w_query,
        w_key,
        w_value,
        w_out.T,
        w_gate,
        w_up,
        w_down.T,
    )
    layer_out, tokens_grad, gqkvo, gg, gu, gd, sums = outs
    bias = jnp.sum(sums[8:, 0:512].reshape(8, 2, 2, 128), axis=-1)
    bias = bias.transpose(2, 1, 0).reshape(2, 16)
    return (
        layer_out,
        tokens_grad,
        sums[0],
        gqkvo[:, 0:LOCAL],
        gqkvo[:, LOCAL : 2 * LOCAL],
        gqkvo[:, 2 * LOCAL : 3 * LOCAL],
        bias,
        gqkvo[:, 3 * LOCAL :].T,
        sums[1],
        gg,
        gu,
        gd.T,
    )


def fits(mesh, tokens, w_query, w_gate):
    sizes = dict(mesh.shape)
    return (
        sizes["fsdp"] == 16
        and sizes["tensor"] == 2
        and tokens.shape == (2, 16 * SEQ_LEN, WIDTH)
        and w_query.shape == (WIDTH, 2 * LOCAL)
        and w_gate.shape == (WIDTH, 2 * HIDDEN)
    )


def solution(mesh):
    placed = (
        P(None, ("fsdp", "tensor"), None),
        P(None, "fsdp"),
        P(None, "fsdp"),
        P(None, "fsdp"),
        P(),
        P("fsdp", "tensor"),
        P("fsdp", "tensor"),
        P("fsdp", "tensor"),
        P(),
        P("tensor", "fsdp"),
        P(),
        P("fsdp", "tensor"),
        P("fsdp", "tensor"),
        P("tensor", "fsdp"),
        P(None, ("fsdp", "tensor"), None),
    )
    outs = (
        P(None, ("fsdp", "tensor"), None),
        P(None, ("fsdp", "tensor"), None),
        P(),
        P("fsdp", "tensor"),
        P("fsdp", "tensor"),
        P("fsdp", "tensor"),
        P(),
        P("tensor", "fsdp"),
        P(),
        P("fsdp", "tensor"),
        P("fsdp", "tensor"),
        P("tensor", "fsdp"),
    )

    def whole(*args):
        body = fused_local if fits(mesh, args[0], args[5], args[11]) else local
        return jax.shard_map(
            body, mesh=mesh, in_specs=placed, out_specs=outs, check_vma=False
        )(*args)

    return whole
```

```python
from functools import partial
from functools import reduce

import jax
import jax.numpy as jnp
import numpy as np
from jax import lax
from jax.experimental import pallas as pl
from jax.experimental.pallas import tpu as pltpu
from jax.sharding import PartitionSpec as P

HEAD_DIM = 64
SEQ_MAX = 1024


EPS = 1e-06


def product(left, right):
    return jnp.dot(left, right, preferred_element_type=jnp.float32)


def product_back(left, right):
    return lax.dot_general(
        left, right, (((1,), (1,)), ((), ())), preferred_element_type=jnp.float32
    )


def outer_sum(left, right):
    return lax.dot_general(
        left, right, (((0,), (0,)), ((), ())), preferred_element_type=jnp.float32
    )


def norm_forward(resid, gain):
    inverse = lax.rsqrt(jnp.mean(resid * resid, axis=-1, keepdims=True) + EPS)
    return (resid * inverse * gain, inverse)


def norm_backward(resid, inverse, gain, upstream):
    scaled = resid * inverse
    weighted = upstream * gain
    back = inverse * (weighted - scaled * jnp.mean(weighted * scaled, axis=-1, keepdims=True))
    return (back, jnp.sum(upstream * scaled, axis=0))


def rope_tables(moments, half_width):
    inverse = 10000.0 ** (-(jnp.arange(half_width, dtype=jnp.float32) / half_width))
    angles = moments.astype(jnp.float32)[:, None] * inverse[None, :]
    return (jnp.cos(angles), jnp.sin(angles))


def rotate(values, cosine, sine):
    half_width = values.shape[-1] // 2
    leading = values[..., :half_width]
    trailing = values[..., half_width:]
    cosine = cosine[:, None, :]
    sine = sine[:, None, :]
    return jnp.concatenate(
        [leading * cosine - trailing * sine, trailing * cosine + leading * sine], axis=-1
    )


def rotate_back(grads, cosine, sine):
    half_width = grads.shape[-1] // 2
    leading = grads[..., :half_width]
    trailing = grads[..., half_width:]
    cosine = cosine[:, None, :]
    sine = sine[:, None, :]
    return jnp.concatenate(
        [leading * cosine + trailing * sine, trailing * cosine - leading * sine], axis=-1
    )


def masked_scores(query, keys, segment, variate, bias_pair):
    scores = jnp.einsum(
        "qhd,khd->hqk", query, keys, preferred_element_type=jnp.float32
    ) * HEAD_DIM ** (-0.5)
    same_variate = variate[:, None] == variate[None, :]
    scores = scores + jnp.where(
        same_variate[None], bias_pair[0][:, None, None], bias_pair[1][:, None, None]
    )
    allowed = segment[:, None] == segment[None, :]
    return (jnp.where(allowed[None], scores, -1e30), same_variate)


def attend_forward(bias_pair, item):
    query, keys, values, segment, variate = item
    scores, unused = masked_scores(query, keys, segment, variate, bias_pair)
    highest = jnp.max(scores, axis=-1, keepdims=True)
    expo = jnp.exp(scores - highest)
    total = jnp.sum(expo, axis=-1, keepdims=True)
    probs = (expo / total).astype(jnp.bfloat16)
    attended = jnp.einsum("hqk,khd->qhd", probs, values, preferred_element_type=jnp.float32)
    return (attended.astype(jnp.bfloat16), (highest + jnp.log(total))[..., 0])


def attend_backward(bias_pair, item):
    query, keys, values, dattended, segment, variate, logsum = item
    scores, same_variate = masked_scores(query, keys, segment, variate, bias_pair)
    probs = jnp.exp(scores - logsum[..., None])
    probs_low = probs.astype(jnp.bfloat16)
    dprobs = jnp.einsum("qhd,khd->hqk", dattended, values, preferred_element_type=jnp.float32)
    dvalues = jnp.einsum("hqk,qhd->khd", probs_low, dattended, preferred_element_type=jnp.float32)
    dscores = (probs * (dprobs - jnp.sum(probs * dprobs, axis=-1, keepdims=True))).astype(
        jnp.bfloat16
    )
    widened = dscores.astype(jnp.float32)
    same_sum = jnp.sum(jnp.where(same_variate[None], widened, 0.0), axis=(1, 2))
    other_sum = jnp.sum(jnp.where(same_variate[None], 0.0, widened), axis=(1, 2))
    dquery = jnp.einsum(
        "hqk,khd->qhd", dscores, keys, preferred_element_type=jnp.float32
    ) * HEAD_DIM ** (-0.5)
    dkeys = jnp.einsum(
        "hqk,qhd->khd", dscores, query, preferred_element_type=jnp.float32
    ) * HEAD_DIM ** (-0.5)
    return (dquery, dkeys, dvalues, jnp.stack([same_sum, other_sum]))


def local(
    tokens,
    segment_ids,
    variate_ids,
    time_ids,
    attn_gain,
    w_query,
    w_key,
    w_value,
    head_bias,
    w_out,
    ffn_gain,
    w_gate,
    w_up,
    w_down,
    cotangent,
):
    micro_count, row_count, model_width = tokens.shape
    group_rows = segment_ids.shape[1]
    seq_len = min(SEQ_MAX, group_rows)
    seq_count = group_rows // seq_len
    local_width = w_query.shape[1]
    local_heads = local_width // HEAD_DIM
    head_start = lax.axis_index("tensor") * local_heads
    bias_pair = lax.dynamic_slice_in_dim(head_bias, head_start, local_heads, 1)
    shards = (w_query, w_key, w_value, w_out, w_gate, w_up, w_down)
    heads_shape = (group_rows, local_heads, HEAD_DIM)
    seq_shape = (seq_count, seq_len, local_heads, HEAD_DIM)

    def spread_normed(block):
        return lax.all_gather(block, "tensor", axis=0, tiled=True)

    def spread_grads(block):
        return lax.all_gather(block, "tensor", axis=0, tiled=True)

    def branch_rows(left, right):
        return lax.psum_scatter(product(left, right), "tensor", scatter_dimension=0, tiled=True)

    def back_rows(lefts, rights):
        pieces = [product_back(left, right) for left, right in zip(lefts, rights)]
        return lax.psum_scatter(reduce(jnp.add, pieces), "tensor", scatter_dimension=0, tiled=True)

    outputs = []
    input_grads = []
    grad_shards = None
    gain_first = jnp.zeros((model_width,), jnp.float32)
    gain_second = jnp.zeros((model_width,), jnp.float32)
    bias_grad = jnp.zeros((2, local_heads), jnp.float32)
    for micro_index in range(micro_count):
        full_weights = (
            lax.all_gather(shards[0], "fsdp", axis=0, tiled=True),
            lax.all_gather(shards[1], "fsdp", axis=0, tiled=True),
            lax.all_gather(shards[2], "fsdp", axis=0, tiled=True),
            lax.all_gather(shards[3], "fsdp", axis=1, tiled=True),
            lax.all_gather(shards[4], "fsdp", axis=0, tiled=True),
            lax.all_gather(shards[5], "fsdp", axis=0, tiled=True),
            lax.all_gather(shards[6], "fsdp", axis=1, tiled=True),
        )
        query_full, key_full, value_full, out_full, gate_full, up_full, down_full = full_weights
        resid = tokens[micro_index].astype(jnp.float32)
        segment = segment_ids[micro_index].reshape(seq_count, seq_len)
        variate = variate_ids[micro_index].reshape(seq_count, seq_len)
        cosine, sine = rope_tables(time_ids[micro_index], HEAD_DIM // 2)
        normed, inverse_first = norm_forward(resid, attn_gain)
        normed_all = spread_normed(normed.astype(jnp.bfloat16))
        query = rotate(product(normed_all, query_full).reshape(heads_shape), cosine, sine).astype(
            jnp.bfloat16
        )
        keys = rotate(product(normed_all, key_full).reshape(heads_shape), cosine, sine).astype(
            jnp.bfloat16
        )
        values = product(normed_all, value_full).astype(jnp.bfloat16)
        query_seq = query.reshape(seq_shape)
        keys_seq = keys.reshape(seq_shape)
        values_seq = values.reshape(seq_shape)
        attended, logsum = lax.map(
            partial(attend_forward, bias_pair), (query_seq, keys_seq, values_seq, segment, variate)
        )
        attended = attended.reshape(group_rows, local_width)
        middle = resid + branch_rows(attended, out_full)
        normed_ffn, inverse_second = norm_forward(middle, ffn_gain)
        normed_ffn_all = spread_normed(normed_ffn.astype(jnp.bfloat16))
        gate = product(normed_ffn_all, gate_full)
        upward = product(normed_ffn_all, up_full)
        sigmoid = jax.nn.sigmoid(gate)
        hidden = (gate * sigmoid * upward).astype(jnp.bfloat16)
        outputs.append((middle + branch_rows(hidden, down_full)).astype(jnp.bfloat16))
        full_weights = (
            lax.all_gather(shards[0], "fsdp", axis=0, tiled=True),
            lax.all_gather(shards[1], "fsdp", axis=0, tiled=True),
            lax.all_gather(shards[2], "fsdp", axis=0, tiled=True),
            lax.all_gather(shards[3], "fsdp", axis=1, tiled=True),
            lax.all_gather(shards[4], "fsdp", axis=0, tiled=True),
            lax.all_gather(shards[5], "fsdp", axis=0, tiled=True),
            lax.all_gather(shards[6], "fsdp", axis=1, tiled=True),
        )
        query_full, key_full, value_full, out_full, gate_full, up_full, down_full = full_weights
        grad_out = cotangent[micro_index].astype(jnp.float32)
        grad_ffn_all = spread_grads(cotangent[micro_index])
        dhidden = product_back(grad_ffn_all, down_full)
        dgate = (dhidden * upward * (sigmoid + gate * sigmoid * (1.0 - sigmoid))).astype(
            jnp.bfloat16
        )
        dupward = (dhidden * gate * sigmoid).astype(jnp.bfloat16)
        dnormed_ffn = back_rows((dgate, dupward), (gate_full, up_full))
        grad_gate = outer_sum(normed_ffn_all, dgate)
        grad_up = outer_sum(normed_ffn_all, dupward)
        grad_down = outer_sum(hidden, grad_ffn_all)
        dmiddle, gain_term = norm_backward(middle, inverse_second, ffn_gain, dnormed_ffn)
        gain_second = gain_second + gain_term
        dmiddle = dmiddle + grad_out
        grad_attn_all = spread_grads(dmiddle.astype(jnp.bfloat16))
        dattended = product_back(grad_attn_all, out_full).astype(jnp.bfloat16)
        grad_out_proj = outer_sum(attended, grad_attn_all)
        back_items = (
            query_seq,
            keys_seq,
            values_seq,
            dattended.reshape(seq_shape),
            segment,
            variate,
            logsum,
        )
        dquery, dkeys, dvalues, bias_terms = lax.map(
            partial(attend_backward, bias_pair), back_items
        )
        bias_grad = bias_grad + jnp.sum(bias_terms, axis=0)
        dquery = (
            rotate_back(dquery.reshape(heads_shape), cosine, sine)
            .astype(jnp.bfloat16)
            .reshape(group_rows, local_width)
        )
        dkeys = (
            rotate_back(dkeys.reshape(heads_shape), cosine, sine)
            .astype(jnp.bfloat16)
            .reshape(group_rows, local_width)
        )
        dvalues = dvalues.astype(jnp.bfloat16).reshape(group_rows, local_width)
        dnormed = back_rows((dquery, dkeys, dvalues), (query_full, key_full, value_full))
        grad_query = outer_sum(normed_all, dquery)
        grad_key = outer_sum(normed_all, dkeys)
        grad_value = outer_sum(normed_all, dvalues)
        dresid, gain_term = norm_backward(resid, inverse_first, attn_gain, dnormed)
        gain_first = gain_first + gain_term
        input_grads.append((dresid + dmiddle).astype(jnp.bfloat16))
        summed = (
            lax.psum_scatter(
                grad_query.astype(jnp.bfloat16), "fsdp", scatter_dimension=0, tiled=True
            ).astype(jnp.float32),
            lax.psum_scatter(
                grad_key.astype(jnp.bfloat16), "fsdp", scatter_dimension=0, tiled=True
            ).astype(jnp.float32),
            lax.psum_scatter(
                grad_value.astype(jnp.bfloat16), "fsdp", scatter_dimension=0, tiled=True
            ).astype(jnp.float32),
            lax.psum_scatter(
                grad_out_proj.astype(jnp.bfloat16), "fsdp", scatter_dimension=1, tiled=True
            ).astype(jnp.float32),
            lax.psum_scatter(
                grad_gate.astype(jnp.bfloat16), "fsdp", scatter_dimension=0, tiled=True
            ).astype(jnp.float32),
            lax.psum_scatter(
                grad_up.astype(jnp.bfloat16), "fsdp", scatter_dimension=0, tiled=True
            ).astype(jnp.float32),
            lax.psum_scatter(
                grad_down.astype(jnp.bfloat16), "fsdp", scatter_dimension=1, tiled=True
            ).astype(jnp.float32),
        )
        grad_shards = summed if grad_shards is None else jax.tree.map(jnp.add, grad_shards, summed)
    bias_full = lax.dynamic_update_slice_in_dim(
        jnp.zeros((2, head_bias.shape[1]), jnp.float32), bias_grad, head_start, 1
    )
    gain_first, gain_second, bias_full = lax.psum(
        (gain_first, gain_second, bias_full), ("fsdp", "tensor")
    )
    return (
        jnp.stack(outputs),
        jnp.stack(input_grads),
        gain_first,
        grad_shards[0],
        grad_shards[1],
        grad_shards[2],
        bias_full,
        grad_shards[3],
        gain_second,
        grad_shards[4],
        grad_shards[5],
        grad_shards[6],
    )


BF = jnp.bfloat16
F32 = jnp.float32
MESH = pl.DeviceIdType.MESH
SHARD = 64
SEQ_LEN = 256
HALF = 128
WIDTH = 1024
LOCAL = 512
HIDDEN = 2048
PAIRS = 4
COL_QKV, COL_OUT, COL_GATE, COL_UP, COL_DOWN = 0, 1536, 2048, 4096, 6144
ALL_COLS = 8192
GATHER = (
    (0, 512),
    (512, 512),
    (1024, 512),
    (1536, 512),
    (2048, 1024),
    (3072, 1024),
    (4096, 1024),
    (5120, 1024),
    (6144, 1024),
    (7168, 1024),
)
FIRST_X = len(GATHER) - 2
CHUNK = 2048
SCATTER = (
    (0, 0, 1024),
    (0, 1024, 1024),
    (1, 0, 1024),
    (1, 1024, 1024),
    (2, 0, 1024),
    (2, 1024, 1024),
    (3, 0, 512),
    (3, 512, 512),
    (3, 1024, 1024),
)
FINAL = len(SCATTER) - 1
NORMAL_COLS = 7168
NEGATIVE = -1e30


def mm(left, right):
    return jnp.dot(left, right, preferred_element_type=F32)


def mm_nt(left, right):
    return lax.dot_general(left, right, (((1,), (1,)), ((), ())), preferred_element_type=F32)


def mm_tn(left, right):
    return lax.dot_general(left, right, (((0,), (0,)), ((), ())), preferred_element_type=F32)


def layer_kernel(
    tok_ref,
    cot_in,
    seg_ref,
    var_ref,
    time_ref,
    again_ref,
    fgain_ref,
    freq_ref,
    bias_ref,
    wq_ref,
    wk_ref,
    wv_ref,
    wo_ref,
    wg_ref,
    wu_ref,
    wd_ref,
    out_ref,
    tgrad_ref,
    gqkvo_ref,
    gg_ref,
    gu_ref,
    gd_ref,
    ga_ref,
    gf_ref,
    gb_ref,
    W,
    GD,
    RC,
    RX,
    RZ,
    RL,
    RXS,
    RZS,
    RLS,
    X,
    COT,
    N1,
    NF,
    Q,
    K,
    V,
    ATT,
    PT,
    MID,
    GT,
    UP,
    HID,
    YS,
    YR,
    YDS,
    YDR,
    YNR,
    T,
    T2,
    OUTM,
    DML,
    SAME,
    NEGM,
    COS,
    SIN,
    GF,
    GA,
    BS,
    SV,
    SR,
    local_sem,
    ag_send,
    ag_recv,
    rs_send,
    rs_recv,
    y_send,
    y_recv,
    sv_send,
    sv_recv,
    credit,
    core_credit,
):
    f = lax.axis_index("fsdp")
    y = lax.axis_index("tensor")
    z, x, c = f // 4, (f // 2) % 2, f % 2
    zs = (z + 1 - 2 * (z % 2), (z + 2) % 4, 3 - z)
    z_devs = [(zk * 4 + x * 2 + c, y) for zk in zs]
    x_dev = (z * 4 + (1 - x) * 2 + c, y)
    c_dev = (z * 4 + x * 2 + 1 - c, y)
    y_dev = (f, 1 - y)
    partners = z_devs + [x_dev, c_dev, y_dev]

    def remote(src, dst, send, recv, dev):
        return pltpu.make_async_remote_copy(
            src_ref=src, dst_ref=dst, send_sem=send, recv_sem=recv, device_id=dev, device_id_type=MESH
        )

    barrier = pltpu.get_barrier_semaphore()
    for dev in partners:
        pl.semaphore_signal(barrier, inc=1, device_id=dev, device_id_type=MESH)
    own_rows = pl.ds(pl.multiple_of(y * HALF, HALF), HALF)
    other_rows = pl.ds(pl.multiple_of((1 - y) * HALF, HALF), HALF)
    loads = [
        (tok_ref, X.at[:, own_rows]),
        (cot_in, COT.at[:, own_rows]),
        (wq_ref, W.at[z, x, c, :, pl.ds(0, LOCAL)]),
        (wk_ref, W.at[z, x, c, :, pl.ds(LOCAL, LOCAL)]),
        (wv_ref, W.at[z, x, c, :, pl.ds(2 * LOCAL, LOCAL)]),
        (wo_ref, W.at[z, x, c, :, pl.ds(COL_OUT, LOCAL)]),
        (wg_ref, W.at[z, x, c, :, pl.ds(COL_GATE, HIDDEN)]),
        (wu_ref, W.at[z, x, c, :, pl.ds(COL_UP, HIDDEN)]),
        (wd_ref, W.at[z, x, c, :, pl.ds(COL_DOWN, HIDDEN)]),
    ]
    loads = [
        pltpu.make_async_copy(src, dst, local_sem.at[i]) for i, (src, dst) in enumerate(loads)
    ]
    for load in loads:
        load.start()
    for load in loads:
        load.wait()
    pl.semaphore_wait(barrier, len(partners))

    middle = ((z + 1) // 2) % 2 == 1
    edge = ((z + 1) // 2) % 2 == 0

    ag_own, ag_pass, ag_x, ag_c = [], [], [], []
    for i, (c0, n) in enumerate(GATHER):
        cols = pl.ds(c0, n)

        def block(zi):
            if i >= FIRST_X:
                return W.at[zi, :, c, :, cols]
            return W.at[zi, x, c, :, cols]

        at = i * 6
        ag_own.append(
            [
                remote(block(z), block(z), ag_send.at[at + k], ag_recv.at[at + k], z_devs[k])
                for k in range(3)
            ]
        )
        ag_pass.append(
            remote(block(zs[1]), block(zs[1]), ag_send.at[at + 3], ag_recv.at[at + 2], z_devs[0])
        )
        part = W.at[z, x, c, :, cols] if i >= FIRST_X else W.at[:, x, c, :, cols]
        ag_x.append(remote(part, part, ag_send.at[at + 4], ag_recv.at[at + 4], x_dev))
        part = W.at[:, :, c, :, cols]
        ag_c.append(remote(part, part, ag_send.at[at + 5], ag_recv.at[at + 5], c_dev))

    def gather_own(i):
        if i >= FIRST_X:
            ag_x[i].wait_recv()
        ag_own[i][0].start()
        ag_own[i][1].start()

        @pl.when(middle)
        def _():
            ag_own[i][2].start()

    def gather_z(i):
        ag_own[i][1].wait_recv()

        @pl.when(middle)
        def _():
            ag_pass[i].start()

        if i + 2 < len(GATHER):
            gather_own(i + 2)
        ag_own[i][0].wait_recv()
        ag_own[i][2].wait_recv()
        if i >= FIRST_X:
            ag_c[i].start()
        else:
            ag_x[i].start()

    def gather_c(i):
        ag_x[i].wait_recv()
        ag_c[i].start()

    def gather_end(i):
        ag_c[i].wait_recv()

    gather_own(0)
    gather_own(1)
    for i in range(FIRST_X, len(GATHER)):
        ag_x[i].start()
    y_tok = remote(X.at[:, own_rows], X.at[:, own_rows], y_send.at[0], y_recv.at[0], y_dev)
    y_cot = remote(COT.at[:, own_rows], COT.at[:, own_rows], y_send.at[1], y_recv.at[1], y_dev)
    y_tok.start()
    y_cot.start()

    @pl.when(edge)
    def _():
        RZ[2] = jnp.zeros((SHARD, NORMAL_COLS), BF)
        RZS[2] = jnp.zeros((2, SHARD, SCATTER[FINAL][2]), BF)

    lane = lax.broadcasted_iota(jnp.int32, (1, 128), 1)
    low_lane = lane < 64
    lead_lane = (lane % 64) < 32

    def column(row):
        return jnp.transpose(jnp.broadcast_to(row.astype(F32), (128, SEQ_LEN)))

    for s in range(2):
        moments = column(time_ref[s : s + 1, :])
        angles = moments * freq_ref[...]
        COS[s] = jnp.cos(angles)
        sine = jnp.sin(angles)
        SIN[s] = jnp.where(lead_lane, -sine, sine)
        seg_row = seg_ref[s : s + 1, :].astype(F32)
        var_row = var_ref[s : s + 1, :].astype(F32)
        seg_col = column(seg_ref[s : s + 1, :])
        var_col = column(var_ref[s : s + 1, :])
        for h in range(2):
            part = slice(h * 128, (h + 1) * 128)
            SAME[s, :, part] = jnp.where(var_col == var_row[:, part], 1.0, 0.0)
            NEGM[s, :, part] = jnp.where(seg_col == seg_row[:, part], 0.0, NEGATIVE)

    def swap(values):
        return jnp.where(
            lead_lane, pltpu.roll(values, 96, axis=1), pltpu.roll(values, 32, axis=1)
        )

    ROWS = 64
    BLOCKS = SEQ_LEN // ROWS

    def row_loop(body):
        def step(b, carry):
            body(b, pl.ds(pl.multiple_of(b * ROWS, ROWS), ROWS))
            return carry

        lax.fori_loop(0, BLOCKS, step, 0)

    def tile_loop(count, body):
        def step(j, carry):
            body(j)
            return carry

        lax.fori_loop(0, count, step, 0)

    def tile_cols(base, j, size=256):
        return pl.ds(pl.multiple_of(base + j * size, size), size)

    def w_tile(cols):
        return W[:, :, :, :, cols].reshape(WIDTH, 256)

    def w_rows(zi, c0, n):
        return W[zi, :, :, :, pl.ds(c0, n)].reshape(256, n)

    def transpose_into(src, T):
        for s in range(2):

            def body(j):
                cols = tile_cols(0, j)
                T[cols, s * SEQ_LEN : (s + 1) * SEQ_LEN] = jnp.transpose(src[s, :, cols])

            tile_loop(4, body)

    y_tok.wait_recv()
    for s in range(2):

        def body(b, rows):
            v = X[s, rows, :].astype(F32)
            inv = lax.rsqrt(jnp.mean(v * v, axis=-1, keepdims=True) + EPS)
            N1[s, rows, :] = (v * inv * again_ref[...]).astype(BF)

        row_loop(body)

    gather_z(0)
    gather_z(1)
    gather_c(0)
    gather_z(2)
    gather_c(1)
    gather_z(3)
    gather_c(2)

    for kind, dest in enumerate((Q, K, V)):
        gather_end(kind)

        def body(j):
            r = mm(N1[...].reshape(2 * SEQ_LEN, WIDTH), w_tile(tile_cols(kind * LOCAL, j)))
            for h in range(2):
                part = r[:, h * 128 : (h + 1) * 128]
                if kind < 2:
                    cosine = COS[...].reshape(2 * SEQ_LEN, 128)
                    sine = SIN[...].reshape(2 * SEQ_LEN, 128)
                    part = part * cosine + swap(part) * sine
                dest[:, :, pl.ds(pl.multiple_of(j * 256 + h * 128, 128), 128)] = part.astype(
                    BF
                ).reshape(2, SEQ_LEN, 128)

        tile_loop(2, body)

    gather_z(4)
    gather_c(3)

    def stacked(values):
        zero = jnp.zeros_like(values)
        return jnp.concatenate(
            [jnp.where(low_lane, values, zero), jnp.where(low_lane, zero, values)], axis=0
        )

    def pair_cols(p):
        return pl.ds(pl.multiple_of(p * 128, 128), 128)

    y_att = [
        remote(YS.at[s], YR.at[s], y_send.at[2 + s], y_recv.at[2 + s], y_dev) for s in range(2)
    ]
    for s in range(2):

        def body(p):
            cols = pair_cols(p)
            keys = stacked(K[s, :, cols] * jnp.asarray(0.125, BF))
            scores = mm_nt(keys, Q[s, :, cols])
            parts = []
            for h in range(2):
                head = y * 8 + p * 2 + h
                same_bias = bias_ref[0, head]
                other_bias = bias_ref[1, head]
                sc = scores[h * SEQ_LEN : (h + 1) * SEQ_LEN]
                sc = sc + (SAME[s] * (same_bias - other_bias) + (NEGM[s] + other_bias))
                top = jnp.max(sc, axis=0, keepdims=True)
                expo = jnp.exp(sc - top)
                total = jnp.sum(expo, axis=0, keepdims=True)
                parts.append((expo * (1.0 / total)).astype(BF))
            probs = jnp.concatenate(parts, axis=0)
            PT[s * PAIRS + p] = probs
            ATT[s, :, cols] = mm_tn(probs, stacked(V[s, :, cols])).astype(BF)

        tile_loop(PAIRS, body)
        if s == 0:
            gather_end(3)
        for zi in range(4):
            YS[s, :, zi * 256 : (zi + 1) * 256] = mm_nt(
                ATT[s], w_rows(zi, COL_OUT, LOCAL)
            ).astype(BF)
        y_att[s].start()
        if s == 0:
            gather_z(5)
            gather_c(4)

    gather_z(6)
    for s in range(2):
        y_att[s].wait_recv()

        def body(b, rows):
            v = X[s, rows, :].astype(F32) + (YS[s, rows, :].astype(F32) + YR[s, rows, :].astype(F32))
            MID[s, rows, :] = v
            inv = lax.rsqrt(jnp.mean(v * v, axis=-1, keepdims=True) + EPS)
            NF[s, rows, :] = (v * inv * fgain_ref[...]).astype(BF)

        row_loop(body)
        if s == 0:
            gather_c(5)
            gather_z(7)
    for s in range(2):
        y_att[s].wait_send()
    pl.semaphore_signal(credit, inc=1, device_id=y_dev, device_id_type=MESH)

    def gate_tiles(half):
        def body(j):
            cols = tile_cols(half * 1024, j)
            GT[:, cols] = mm(
                NF[...].reshape(2 * SEQ_LEN, WIDTH), w_tile(tile_cols(COL_GATE + half * 1024, j))
            ).astype(BF)

        tile_loop(4, body)

    def up_tiles(half):
        def body(j):
            cols = tile_cols(half * 1024, j)
            up = mm(
                NF[...].reshape(2 * SEQ_LEN, WIDTH), w_tile(tile_cols(COL_UP + half * 1024, j))
            )
            UP[:, cols] = up.astype(BF)
            gate = GT[:, cols].astype(F32)
            HID[:, cols] = (gate * jax.nn.sigmoid(gate) * up).astype(BF)

        tile_loop(4, body)

    gather_end(4)
    gate_tiles(0)
    gather_end(5)
    gate_tiles(1)
    y_cot.wait_recv()
    transpose_into(COT, T)
    gather_c(6)
    gather_end(6)
    up_tiles(0)
    gather_z(8)

    homes = ((GD, 0), (W, COL_DOWN), (W, COL_GATE), (W, COL_UP))
    results = (gd_ref, gg_ref, gu_ref, gqkvo_ref)

    def home(ch, *index, c0=0, n=CHUNK):
        ref, base = homes[ch]
        return ref.at[index + (slice(None), pl.ds(base + c0, n))]

    every = slice(None)
    slots = (0, 1, 2, 0)
    rs_c, rs_x, rs_z, rs_relay = [], [], [], []
    spots = []
    for p, (ch, c0, n) in enumerate(SCATTER):
        spot = sum(size for _, _, size in SCATTER[:p])
        spots.append(spot)
        at = p * 6

        def sems(k):
            return rs_send.at[at + k], rs_recv.at[at + k]

        rs_c.append(
            remote(
                home(ch, every, every, 1 - c, c0=c0, n=n),
                RC.at[slots[ch], :, :, :, pl.ds(c0, n)],
                *sems(0),
                c_dev,
            )
        )
        cols = pl.ds(spot, n)
        if p == FINAL:
            rs_x.append(remote(home(ch, z, 1 - x, c, c0=c0, n=n), RXS, *sems(1), x_dev))
            views = [home(ch, zk, every, c, c0=c0, n=n) for zk in zs]
            boxes, relay = [RZS.at[k] for k in range(3)], RLS
        else:
            rs_x.append(
                remote(
                    home(ch, every, 1 - x, c, c0=c0, n=n), RX.at[:, :, cols], *sems(1), x_dev
                )
            )
            views = [home(ch, zk, x, c, c0=c0, n=n) for zk in zs]
            boxes, relay = [RZ.at[k, :, cols] for k in range(3)], RL.at[:, cols]
        rs_z.append(
            [remote(views[k], boxes[k], *sems(2 + k), z_devs[k]) for k in range(3)]
        )
        rs_relay.append(remote(views[2], relay, *sems(5), z_devs[0]))

    def add_core(p, xi):
        ch, c0, n = SCATTER[p]

        def body(zi):
            view = home(ch, zi, xi, c, c0=c0, n=n)
            view[...] = view[...] + RC[slots[ch], zi, xi, :, pl.ds(c0, n)]

        tile_loop(4, body)

    def send_z(p):
        rs_z[p][0].start()

        @pl.when(middle)
        def _():
            rs_z[p][2].start()

        @pl.when(edge)
        def _():
            rs_z[p][1].start()
            rs_relay[p].start()

    def scatter_core(p):
        rs_c[p].start()

    def scatter_x(p):
        rs_c[p].wait_recv()
        add_core(p, 1 - x)
        if p == FINAL:
            add_core(p, x)
            send_z(p)
        else:
            rs_x[p].start()
            add_core(p, x)

    def scatter_z(p):
        ch, c0, n = SCATTER[p]
        rs_x[p].wait_recv()

        def body(zi):
            view = home(ch, zi, x, c, c0=c0, n=n)
            view[...] = view[...] + RX[zi, :, pl.ds(spots[p], n)]

        tile_loop(4, body)
        send_z(p)

    def scatter_pass(p):
        ch, c0, n = SCATTER[p]

        @pl.when(middle)
        def _():
            rs_relay[p].wait_recv()
            if p == FINAL:
                view = home(ch, zs[1], every, c, c0=c0, n=n)
                view[...] = view[...] + RLS[...]
            else:
                view = home(ch, zs[1], x, c, c0=c0, n=n)
                view[...] = view[...] + RL[:, pl.ds(spots[p], n)]
            rs_z[p][1].start()

    def wait_z(p):
        rs_z[p][0].wait_recv()
        rs_z[p][1].wait_recv()

        @pl.when(middle)
        def _():
            rs_z[p][2].wait_recv()

    def scatter_end(p):
        ch, c0, n = SCATTER[p]
        wait_z(p)

        def body(j):
            total = home(ch, z, x, c)[:, tile_cols(c0, j)].astype(F32)
            for k in range(3):
                total = total + RZ[k, :, tile_cols(spots[p], j)].astype(F32)
            results[ch][:, tile_cols(c0, j)] = total

        tile_loop(n // 256, body)

    def final_x():
        ch, c0, n = SCATTER[FINAL]
        wait_z(FINAL)
        for xi in range(2):
            view = home(ch, z, xi, c, c0=c0, n=n)
            total = view[...].astype(F32)
            for k in range(3):
                total = total + RZS[k, xi].astype(F32)
            view[...] = total.astype(BF)
        rs_x[FINAL].start()

    def final_end():
        ch, c0, n = SCATTER[FINAL]
        rs_x[FINAL].wait_recv()
        results[ch][:, c0 : c0 + n] = home(ch, z, x, c, c0=c0, n=n)[...].astype(F32) + RXS[
            ...
        ].astype(F32)

    def weight_grad(ch, c0, left, right, r0, count):
        ref, base = homes[ch]

        def body(j):
            r = mm(left[...], right(j, r0))
            ref[:, :, :, :, tile_cols(base + c0, j)] = r.astype(BF).reshape(4, 2, 2, SHARD, 256)

        tile_loop(count, body)

    def down_grad(half):
        weight_grad(0, half * 1024, T, lambda j, r0: HID[:, tile_cols(r0, j)], half * 1024, 4)

    def gate_grad(half):
        weight_grad(1, half * 1024, T2, lambda j, r0: GT[:, tile_cols(r0, j)], half * 1024, 4)

    def up_grad(half):
        weight_grad(2, half * 1024, T2, lambda j, r0: UP[:, tile_cols(r0, j)], half * 1024, 4)

    def hidden_back(half):
        def body(j):
            cols = tile_cols(half * 1024, j)
            dhid = mm(
                COT[...].reshape(2 * SEQ_LEN, WIDTH), w_tile(tile_cols(COL_DOWN + half * 1024, j))
            )
            gate = GT[:, cols].astype(F32)
            up = UP[:, cols].astype(F32)
            sig = jax.nn.sigmoid(gate)
            GT[:, cols] = (dhid * up * (sig + gate * sig * (1.0 - sig))).astype(BF)
            UP[:, cols] = (dhid * gate * sig).astype(BF)

        tile_loop(4, body)

    down_grad(0)
    scatter_core(0)
    transpose_into(NF, T2)
    scatter_x(0)
    gather_c(7)
    gather_end(7)
    up_tiles(1)
    down_grad(1)
    scatter_core(1)
    gather_end(8)
    hidden_back(0)
    scatter_x(1)
    pl.semaphore_signal(core_credit, inc=1, device_id=c_dev, device_id_type=MESH)
    gather_z(9)
    gather_end(9)
    hidden_back(1)
    scatter_z(0)

    for i in range(len(GATHER)):
        ag_own[i][0].wait_send()
        ag_own[i][1].wait_send()
        ag_x[i].wait_send()
        ag_c[i].wait_send()

        @pl.when(middle)
        def _():
            ag_own[i][2].wait_send()
            ag_pass[i].wait_send()

    def body(zi):
        cols = tile_cols(0, zi)
        r = mm_nt(HID[...], w_rows(zi, COL_DOWN, HIDDEN)).reshape(2, 2, HALF, 256)
        mine = jnp.where(y == 0, r[:, 0], r[:, 1])
        OUTM[:, :, cols] = MID[:, own_rows, cols] + mine
        YDS[:, :, cols] = jnp.where(y == 0, r[:, 1], r[:, 0]).astype(BF)

    tile_loop(4, body)
    gate_grad(0)
    scatter_core(2)
    gate_grad(1)
    scatter_core(3)
    y_dnf = [
        remote(YS.at[s], YR.at[s], y_send.at[4 + s], y_recv.at[4 + s], y_dev) for s in range(2)
    ]
    pl.semaphore_wait(credit, 1)
    for s in range(2):
        rows = slice(s * SEQ_LEN, (s + 1) * SEQ_LEN)

        def body(zi):
            r = mm_nt(GT[rows, :], w_rows(zi, COL_GATE, HIDDEN))
            r = r + mm_nt(UP[rows, :], w_rows(zi, COL_UP, HIDDEN))
            YS[s, :, tile_cols(0, zi)] = r.astype(BF)

        tile_loop(4, body)
        y_dnf[s].start()

    y_out = remote(YDS, YDR, y_send.at[6], y_recv.at[6], y_dev)
    y_out.start()
    scatter_x(2)
    scatter_x(3)
    up_grad(0)
    scatter_core(4)
    up_grad(1)
    scatter_core(5)
    scatter_pass(0)
    scatter_z(1)
    scatter_x(4)
    scatter_x(5)
    transpose_into(N1, T2)

    GF[...] = jnp.zeros_like(GF)
    GA[...] = jnp.zeros_like(GA)
    DAT = HID.at[:, 3 * LOCAL : 4 * LOCAL]
    DQKV = HID
    dout = DAT
    scatter_pass(1)
    scatter_z(2)
    for s in range(2):
        y_dnf[s].wait_recv()

        def body(b, rows):
            v = MID[s, rows, :]
            inv = lax.rsqrt(jnp.mean(v * v, axis=-1, keepdims=True) + EPS)
            scaled = v * inv
            dn = YS[s, rows, :].astype(F32) + YR[s, rows, :].astype(F32)
            flag = jnp.where(b // (HALF // ROWS) == y, 1.0, 0.0)
            GF[...] += flag * jnp.sum((dn * scaled).reshape(ROWS // 8, 8, WIDTH), axis=0)
            u = dn * fgain_ref[...]
            dm = COT[s, rows, :].astype(F32) + inv * (
                u - scaled * jnp.mean(u * scaled, axis=-1, keepdims=True)
            )
            MID[s, rows, :] = dm
            DML[s, rows, :] = dm.astype(BF)

        row_loop(body)
        seq_rows = slice(s * SEQ_LEN, (s + 1) * SEQ_LEN)

        def body(j):
            dout[seq_rows, tile_cols(0, j)] = mm(DML[s], w_tile(tile_cols(COL_OUT, j))).astype(BF)

        tile_loop(2, body)

        def body(p):
            cols = pair_cols(p)
            do = dout[seq_rows, cols]
            dprobs = mm_nt(stacked(V[s, :, cols]), do)
            probs_low = PT[s * PAIRS + p]
            parts = []
            for h in range(2):
                part = slice(h * SEQ_LEN, (h + 1) * SEQ_LEN)
                pr = probs_low[part].astype(F32)
                dp = dprobs[part]
                dot = jnp.sum(pr * dp, axis=0, keepdims=True)
                ds = (pr * (dp - dot)).astype(BF)
                wide = ds.astype(F32)
                same = wide * SAME[s]
                same_sum = jnp.sum(same, axis=0, keepdims=True)
                other_sum = jnp.sum(wide - same, axis=0, keepdims=True)
                if s == 0:
                    BS[0, p * 2 + h] = same_sum
                    BS[1, p * 2 + h] = other_sum
                else:
                    BS[0, p * 2 + h] += same_sum
                    BS[1, p * 2 + h] += other_sum
                parts.append(ds)
            dsc = jnp.concatenate(parts, axis=0)
            dv = mm(probs_low, do)
            dv = jnp.where(low_lane, dv[:SEQ_LEN], dv[SEQ_LEN:])
            dk = mm(dsc, Q[s, :, cols])
            dk = jnp.where(low_lane, dk[:SEQ_LEN], dk[SEQ_LEN:]) * 0.125
            dq = mm_tn(dsc, stacked(K[s, :, cols] * jnp.asarray(0.125, BF)))
            dq = dq * COS[s] - swap(dq) * SIN[s]
            dk = dk * COS[s] - swap(dk) * SIN[s]
            DQKV[seq_rows, cols] = dq.astype(BF)
            DQKV[seq_rows, pl.ds(pl.multiple_of(LOCAL + p * 128, 128), 128)] = dk.astype(BF)
            DQKV[seq_rows, pl.ds(pl.multiple_of(2 * LOCAL + p * 128, 128), 128)] = dv.astype(BF)

        tile_loop(PAIRS, body)
        scatter_pass(2 + s)
        scatter_z(3 + s)

    for s in range(2):
        y_dnf[s].wait_send()
    y_dn = [
        remote(YS.at[s, other_rows], YNR.at[s], y_send.at[7 + s], y_recv.at[7 + s], y_dev)
        for s in range(2)
    ]
    for s in range(2):
        seq_rows = slice(s * SEQ_LEN, (s + 1) * SEQ_LEN)

        def body(zi):
            r = mm_nt(DQKV[seq_rows, 0 : 3 * LOCAL], w_rows(zi, COL_QKV, 3 * LOCAL))
            YS[s, :, tile_cols(0, zi)] = r.astype(BF)

        tile_loop(4, body)
        y_dn[s].start()

    pl.semaphore_wait(core_credit, 1)
    weight_grad(3, 1024, T2, lambda j, r0: DQKV[:, tile_cols(1024, j)], 0, 2)
    transpose_into(DML, T)
    weight_grad(3, 1536, T, lambda j, r0: ATT[:, :, tile_cols(0, j)].reshape(512, 256), 0, 2)
    scatter_core(8)
    weight_grad(3, 0, T2, lambda j, r0: DQKV[:, tile_cols(0, j)], 0, 2)
    scatter_core(6)
    weight_grad(3, 512, T2, lambda j, r0: DQKV[:, tile_cols(512, j)], 0, 2)
    scatter_core(7)
    scatter_x(8)
    scatter_x(6)
    scatter_x(7)

    scatter_end(0)
    scatter_pass(4)
    scatter_z(5)
    scatter_end(1)
    scatter_pass(8)
    y_out.wait_recv()
    for s in range(2):

        def body(b, carry):
            rows = pl.ds(pl.multiple_of(b * ROWS, ROWS), ROWS)
            out_ref[s, rows, :] = (OUTM[s, rows, :] + YDR[s, rows, :].astype(F32)).astype(BF)
            return carry

        lax.fori_loop(0, HALF // ROWS, body, 0)
    y_out.wait_send()
    scatter_end(2)

    for s in range(2):
        y_dn[s].wait_recv()

        def body(b, carry):
            rows = pl.ds(pl.multiple_of(b * ROWS, ROWS), ROWS)
            mine = pl.ds(pl.multiple_of(y * HALF + b * ROWS, ROWS), ROWS)
            v = X[s, mine, :].astype(F32)
            inv = lax.rsqrt(jnp.mean(v * v, axis=-1, keepdims=True) + EPS)
            scaled = v * inv
            dn = YS[s, mine, :].astype(F32) + YNR[s, rows, :].astype(F32)
            GA[...] += jnp.sum((dn * scaled).reshape(ROWS // 8, 8, WIDTH), axis=0)
            u = dn * again_ref[...]
            dx = MID[s, mine, :] + inv * (
                u - scaled * jnp.mean(u * scaled, axis=-1, keepdims=True)
            )
            tgrad_ref[s, rows, :] = dx.astype(BF)
            return carry

        lax.fori_loop(0, HALF // ROWS, body, 0)

    SV[0] = jnp.zeros((24, 128), F32)
    first_sum = jnp.sum(GA[...], axis=0, keepdims=True)
    second_sum = jnp.sum(GF[...], axis=0, keepdims=True)
    for j in range(8):
        SV[0, j : j + 1, :] = first_sum[:, j * 128 : (j + 1) * 128]
        SV[0, 8 + j : 9 + j, :] = second_sum[:, j * 128 : (j + 1) * 128]
    for kind in range(2):
        row = jnp.zeros((1, 128), F32)
        for h in range(8):
            head_sum = jnp.sum(BS[kind, h], axis=1, keepdims=True)
            row = row + jnp.where(lane == y * 8 + h, head_sum, 0.0)
        SV[0, 16 + kind : 17 + kind, :] = row

    sums = [
        [remote(SV.at[0], SR.at[0], sv_send.at[0], sv_recv.at[0], c_dev)],
        [remote(SV.at[1], SR.at[1], sv_send.at[1], sv_recv.at[1], y_dev)],
        [
            remote(SV.at[2], SR.at[2 + k], sv_send.at[2 + k], sv_recv.at[2 + k], z_devs[k])
            for k in range(3)
        ],
        [remote(SV.at[3], SR.at[5], sv_send.at[5], sv_recv.at[5], x_dev)],
    ]

    def sum_stage(i):
        total = SV[i]
        for copy in sums[i]:
            copy.wait_recv()
        first = (0, 1, 2, 5)[i]
        for k in range(len(sums[i])):
            total = total + SR[first + k]
        if i < 3:
            SV[i + 1] = total
            for copy in sums[i + 1]:
                copy.start()
        else:
            for j in range(8):
                cols = slice(j * 128, (j + 1) * 128)
                ga_ref[:, cols] = total[j : j + 1]
                gf_ref[:, cols] = total[8 + j : 9 + j]
            gb_ref[...] = total[16:18, 0:16]

    sums[0][0].start()
    scatter_end(3)
    sum_stage(0)
    scatter_pass(5)
    scatter_z(6)
    sum_stage(1)
    scatter_end(4)
    final_x()
    scatter_pass(6)
    scatter_z(7)
    scatter_end(5)
    sum_stage(2)
    scatter_pass(7)
    scatter_end(6)
    final_end()
    sum_stage(3)
    scatter_end(7)

    for s in range(2):
        y_dn[s].wait_send()
    y_tok.wait_send()
    y_cot.wait_send()
    for group in sums:
        for copy in group:
            copy.wait_send()
    for p in range(len(SCATTER)):
        rs_c[p].wait_send()
        rs_x[p].wait_send()
        rs_z[p][0].wait_send()
        rs_z[p][1].wait_send()

        @pl.when(middle)
        def _():
            rs_z[p][2].wait_send()

        @pl.when(edge)
        def _():
            rs_relay[p].wait_send()


def finish_kernel(*refs):
    sources, dests, boxes = refs[:9], refs[9:21], refs[21:30]
    in_sem, out_sem = refs[30], refs[31]
    order = (0, 1, 5, 4, 3, 2, 6, 7, 8)
    loads = {k: pltpu.make_async_copy(sources[k], boxes[k], in_sem.at[k]) for k in order}
    for k in order:
        loads[k].start()
    places = {0: (0,), 1: (1,), 2: (3, 4, 5, 7), 3: (9,), 4: (10,), 5: (11,), 6: (2,), 7: (8,), 8: (6,)}
    stores = []
    for k in order:
        loads[k].wait()
        for i, place in enumerate(places[k]):
            box = boxes[k].at[:, pl.ds(i * LOCAL, LOCAL)] if k == 2 else boxes[k]
            store = pltpu.make_async_copy(box, dests[place], out_sem.at[place])
            store.start()
            stores.append(store)
    for store in stores:
        store.wait()


def fused_local(
    tokens,
    segment_ids,
    variate_ids,
    time_ids,
    attn_gain,
    w_query,
    w_key,
    w_value,
    head_bias,
    w_out,
    ffn_gain,
    w_gate,
    w_up,
    w_down,
    cotangent,
):
    inverse = 10000.0 ** (-(np.arange(32, dtype=np.float32) / np.float32(32)))
    freq = jnp.asarray(np.tile(inverse.astype(np.float32), 4)[None, :])
    vmem = pl.BlockSpec(memory_space=pltpu.VMEM)
    anym = pl.BlockSpec(memory_space=pl.ANY)
    smem = pl.BlockSpec(memory_space=pltpu.SMEM)
    bf = lambda *shape: pltpu.VMEM(shape, BF)
    fl = lambda *shape: pltpu.VMEM(shape, F32)
    seq3 = (2, SEQ_LEN, WIDTH)
    half3 = (2, HALF, WIDTH)
    dma = pltpu.SemaphoreType.DMA
    final_cols = SCATTER[FINAL][2]
    scratch = [
        bf(4, 2, 2, SHARD, ALL_COLS),
        bf(4, 2, 2, SHARD, CHUNK),
        bf(3, 4, 2, SHARD, CHUNK),
        bf(4, SHARD, NORMAL_COLS),
        bf(3, SHARD, NORMAL_COLS),
        bf(SHARD, NORMAL_COLS),
        bf(SHARD, final_cols),
        bf(3, 2, SHARD, final_cols),
        bf(2, SHARD, final_cols),
        bf(*seq3),
        bf(*seq3),
        bf(*seq3),
        bf(*seq3),
        bf(2, SEQ_LEN, LOCAL),
        bf(2, SEQ_LEN, LOCAL),
        bf(2, SEQ_LEN, LOCAL),
        bf(2, SEQ_LEN, LOCAL),
        bf(2 * PAIRS, 2 * SEQ_LEN, SEQ_LEN),
        fl(*seq3),
        bf(2 * SEQ_LEN, HIDDEN),
        bf(2 * SEQ_LEN, HIDDEN),
        bf(2 * SEQ_LEN, HIDDEN),
        bf(*seq3),
        bf(*seq3),
        bf(*half3),
        bf(*half3),
        bf(*half3),
        bf(WIDTH, 2 * SEQ_LEN),
        bf(WIDTH, 2 * SEQ_LEN),
        fl(*half3),
        bf(*seq3),
        fl(2, SEQ_LEN, SEQ_LEN),
        fl(2, SEQ_LEN, SEQ_LEN),
        fl(2, SEQ_LEN, 128),
        fl(2, SEQ_LEN, 128),
        fl(8, WIDTH),
        fl(8, WIDTH),
        fl(2, 8, 1, SEQ_LEN),
        fl(4, 24, 128),
        fl(6, 24, 128),
        dma((9,)),
        dma((6 * len(GATHER),)),
        dma((6 * len(GATHER),)),
        dma((6 * len(SCATTER),)),
        dma((6 * len(SCATTER),)),
        dma((9,)),
        dma((9,)),
        dma((6,)),
        dma((6,)),
        pltpu.SemaphoreType.REGULAR,
        pltpu.SemaphoreType.REGULAR,
    ]
    shape = jax.ShapeDtypeStruct
    outs = pl.pallas_call(
        layer_kernel,
        out_shape=(
            shape(half3, BF),
            shape(half3, BF),
            shape((SHARD, HIDDEN), F32),
            shape((SHARD, HIDDEN), F32),
            shape((SHARD, HIDDEN), F32),
            shape((SHARD, HIDDEN), F32),
            shape((1, WIDTH), F32),
            shape((1, WIDTH), F32),
            shape((2, 16), F32),
        ),
        in_specs=[anym, anym, vmem, vmem, vmem, vmem, vmem, vmem, smem] + [anym] * 7,
        out_specs=(vmem,) * 9,
        scratch_shapes=scratch,
        compiler_params=pltpu.CompilerParams(
            collective_id=0, has_side_effects=True, vmem_limit_bytes=67043328
        ),
        name="layer",
    )(
        tokens,
        cotangent,
        segment_ids,
        variate_ids,
        time_ids,
        attn_gain.reshape(1, WIDTH),
        ffn_gain.reshape(1, WIDTH),
        freq,
        head_bias,
        w_query,
        w_key,
        w_value,
        w_out.T,
        w_gate,
        w_up,
        w_down.T,
    )
    finals = pl.pallas_call(
        finish_kernel,
        out_shape=(
            shape(half3, BF),
            shape(half3, BF),
            shape((1, WIDTH), F32),
            shape((SHARD, LOCAL), F32),
            shape((SHARD, LOCAL), F32),
            shape((SHARD, LOCAL), F32),
            shape((2, 16), F32),
            shape((SHARD, LOCAL), F32),
            shape((1, WIDTH), F32),
            shape((SHARD, HIDDEN), F32),
            shape((SHARD, HIDDEN), F32),
            shape((SHARD, HIDDEN), F32),
        ),
        in_specs=[anym] * 9,
        out_specs=[anym] * 12,
        scratch_shapes=[
            bf(*half3),
            bf(*half3),
            fl(SHARD, HIDDEN),
            fl(SHARD, HIDDEN),
            fl(SHARD, HIDDEN),
            fl(SHARD, HIDDEN),
            fl(1, WIDTH),
            fl(1, WIDTH),
            fl(2, 16),
            dma((9,)),
            dma((12,)),
        ],
        name="finish",
    )(*outs)
    layer_out, tokens_grad, ga, gq, gk, gv, gb, go, gf, gg, gu, gd = finals
    return (
        layer_out,
        tokens_grad,
        ga.reshape(WIDTH),
        gq,
        gk,
        gv,
        gb,
        go.T,
        gf.reshape(WIDTH),
        gg,
        gu,
        gd.T,
    )


def fits(mesh, tokens, w_query, w_gate):
    sizes = dict(mesh.shape)
    return (
        sizes["fsdp"] == 16
        and sizes["tensor"] == 2
        and tokens.shape == (2, 16 * SEQ_LEN, WIDTH)
        and w_query.shape == (WIDTH, 2 * LOCAL)
        and w_gate.shape == (WIDTH, 2 * HIDDEN)
    )


def solution(mesh):
    placed = (
        P(None, ("fsdp", "tensor"), None),
        P(None, "fsdp"),
        P(None, "fsdp"),
        P(None, "fsdp"),
        P(),
        P("fsdp", "tensor"),
        P("fsdp", "tensor"),
        P("fsdp", "tensor"),
        P(),
        P("tensor", "fsdp"),
        P(),
        P("fsdp", "tensor"),
        P("fsdp", "tensor"),
        P("tensor", "fsdp"),
        P(None, ("fsdp", "tensor"), None),
    )
    outs = (
        P(None, ("fsdp", "tensor"), None),
        P(None, ("fsdp", "tensor"), None),
        P(),
        P("fsdp", "tensor"),
        P("fsdp", "tensor"),
        P("fsdp", "tensor"),
        P(),
        P("tensor", "fsdp"),
        P(),
        P("fsdp", "tensor"),
        P("fsdp", "tensor"),
        P("tensor", "fsdp"),
    )

    def whole(*args):
        body = fused_local if fits(mesh, args[0], args[5], args[11]) else local
        return jax.shard_map(
            body, mesh=mesh, in_specs=placed, out_specs=outs, check_vma=False
        )(*args)

    return whole
```

```python
from functools import partial
from functools import reduce

import jax
import jax.numpy as jnp
import numpy as np
from jax import lax
from jax.experimental import pallas as pl
from jax.experimental.pallas import tpu as pltpu
from jax.sharding import PartitionSpec as P

HEAD_DIM = 64
SEQ_MAX = 1024


EPS = 1e-06


def product(left, right):
    return jnp.dot(left, right, preferred_element_type=jnp.float32)


def product_back(left, right):
    return lax.dot_general(
        left, right, (((1,), (1,)), ((), ())), preferred_element_type=jnp.float32
    )


def outer_sum(left, right):
    return lax.dot_general(
        left, right, (((0,), (0,)), ((), ())), preferred_element_type=jnp.float32
    )


def norm_forward(resid, gain):
    inverse = lax.rsqrt(jnp.mean(resid * resid, axis=-1, keepdims=True) + EPS)
    return (resid * inverse * gain, inverse)


def norm_backward(resid, inverse, gain, upstream):
    scaled = resid * inverse
    weighted = upstream * gain
    back = inverse * (weighted - scaled * jnp.mean(weighted * scaled, axis=-1, keepdims=True))
    return (back, jnp.sum(upstream * scaled, axis=0))


def rope_tables(moments, half_width):
    inverse = 10000.0 ** (-(jnp.arange(half_width, dtype=jnp.float32) / half_width))
    angles = moments.astype(jnp.float32)[:, None] * inverse[None, :]
    return (jnp.cos(angles), jnp.sin(angles))


def rotate(values, cosine, sine):
    half_width = values.shape[-1] // 2
    leading = values[..., :half_width]
    trailing = values[..., half_width:]
    cosine = cosine[:, None, :]
    sine = sine[:, None, :]
    return jnp.concatenate(
        [leading * cosine - trailing * sine, trailing * cosine + leading * sine], axis=-1
    )


def rotate_back(grads, cosine, sine):
    half_width = grads.shape[-1] // 2
    leading = grads[..., :half_width]
    trailing = grads[..., half_width:]
    cosine = cosine[:, None, :]
    sine = sine[:, None, :]
    return jnp.concatenate(
        [leading * cosine + trailing * sine, trailing * cosine - leading * sine], axis=-1
    )


def masked_scores(query, keys, segment, variate, bias_pair):
    scores = jnp.einsum(
        "qhd,khd->hqk", query, keys, preferred_element_type=jnp.float32
    ) * HEAD_DIM ** (-0.5)
    same_variate = variate[:, None] == variate[None, :]
    scores = scores + jnp.where(
        same_variate[None], bias_pair[0][:, None, None], bias_pair[1][:, None, None]
    )
    allowed = segment[:, None] == segment[None, :]
    return (jnp.where(allowed[None], scores, -1e30), same_variate)


def attend_forward(bias_pair, item):
    query, keys, values, segment, variate = item
    scores, unused = masked_scores(query, keys, segment, variate, bias_pair)
    highest = jnp.max(scores, axis=-1, keepdims=True)
    expo = jnp.exp(scores - highest)
    total = jnp.sum(expo, axis=-1, keepdims=True)
    probs = (expo / total).astype(jnp.bfloat16)
    attended = jnp.einsum("hqk,khd->qhd", probs, values, preferred_element_type=jnp.float32)
    return (attended.astype(jnp.bfloat16), (highest + jnp.log(total))[..., 0])


def attend_backward(bias_pair, item):
    query, keys, values, dattended, segment, variate, logsum = item
    scores, same_variate = masked_scores(query, keys, segment, variate, bias_pair)
    probs = jnp.exp(scores - logsum[..., None])
    probs_low = probs.astype(jnp.bfloat16)
    dprobs = jnp.einsum("qhd,khd->hqk", dattended, values, preferred_element_type=jnp.float32)
    dvalues = jnp.einsum("hqk,qhd->khd", probs_low, dattended, preferred_element_type=jnp.float32)
    dscores = (probs * (dprobs - jnp.sum(probs * dprobs, axis=-1, keepdims=True))).astype(
        jnp.bfloat16
    )
    widened = dscores.astype(jnp.float32)
    same_sum = jnp.sum(jnp.where(same_variate[None], widened, 0.0), axis=(1, 2))
    other_sum = jnp.sum(jnp.where(same_variate[None], 0.0, widened), axis=(1, 2))
    dquery = jnp.einsum(
        "hqk,khd->qhd", dscores, keys, preferred_element_type=jnp.float32
    ) * HEAD_DIM ** (-0.5)
    dkeys = jnp.einsum(
        "hqk,qhd->khd", dscores, query, preferred_element_type=jnp.float32
    ) * HEAD_DIM ** (-0.5)
    return (dquery, dkeys, dvalues, jnp.stack([same_sum, other_sum]))


def local(
    tokens,
    segment_ids,
    variate_ids,
    time_ids,
    attn_gain,
    w_query,
    w_key,
    w_value,
    head_bias,
    w_out,
    ffn_gain,
    w_gate,
    w_up,
    w_down,
    cotangent,
):
    micro_count, row_count, model_width = tokens.shape
    group_rows = segment_ids.shape[1]
    seq_len = min(SEQ_MAX, group_rows)
    seq_count = group_rows // seq_len
    local_width = w_query.shape[1]
    local_heads = local_width // HEAD_DIM
    head_start = lax.axis_index("tensor") * local_heads
    bias_pair = lax.dynamic_slice_in_dim(head_bias, head_start, local_heads, 1)
    shards = (w_query, w_key, w_value, w_out, w_gate, w_up, w_down)
    heads_shape = (group_rows, local_heads, HEAD_DIM)
    seq_shape = (seq_count, seq_len, local_heads, HEAD_DIM)

    def spread_normed(block):
        return lax.all_gather(block, "tensor", axis=0, tiled=True)

    def spread_grads(block):
        return lax.all_gather(block, "tensor", axis=0, tiled=True)

    def branch_rows(left, right):
        return lax.psum_scatter(product(left, right), "tensor", scatter_dimension=0, tiled=True)

    def back_rows(lefts, rights):
        pieces = [product_back(left, right) for left, right in zip(lefts, rights)]
        return lax.psum_scatter(reduce(jnp.add, pieces), "tensor", scatter_dimension=0, tiled=True)

    outputs = []
    input_grads = []
    grad_shards = None
    gain_first = jnp.zeros((model_width,), jnp.float32)
    gain_second = jnp.zeros((model_width,), jnp.float32)
    bias_grad = jnp.zeros((2, local_heads), jnp.float32)
    for micro_index in range(micro_count):
        full_weights = (
            lax.all_gather(shards[0], "fsdp", axis=0, tiled=True),
            lax.all_gather(shards[1], "fsdp", axis=0, tiled=True),
            lax.all_gather(shards[2], "fsdp", axis=0, tiled=True),
            lax.all_gather(shards[3], "fsdp", axis=1, tiled=True),
            lax.all_gather(shards[4], "fsdp", axis=0, tiled=True),
            lax.all_gather(shards[5], "fsdp", axis=0, tiled=True),
            lax.all_gather(shards[6], "fsdp", axis=1, tiled=True),
        )
        query_full, key_full, value_full, out_full, gate_full, up_full, down_full = full_weights
        resid = tokens[micro_index].astype(jnp.float32)
        segment = segment_ids[micro_index].reshape(seq_count, seq_len)
        variate = variate_ids[micro_index].reshape(seq_count, seq_len)
        cosine, sine = rope_tables(time_ids[micro_index], HEAD_DIM // 2)
        normed, inverse_first = norm_forward(resid, attn_gain)
        normed_all = spread_normed(normed.astype(jnp.bfloat16))
        query = rotate(product(normed_all, query_full).reshape(heads_shape), cosine, sine).astype(
            jnp.bfloat16
        )
        keys = rotate(product(normed_all, key_full).reshape(heads_shape), cosine, sine).astype(
            jnp.bfloat16
        )
        values = product(normed_all, value_full).astype(jnp.bfloat16)
        query_seq = query.reshape(seq_shape)
        keys_seq = keys.reshape(seq_shape)
        values_seq = values.reshape(seq_shape)
        attended, logsum = lax.map(
            partial(attend_forward, bias_pair), (query_seq, keys_seq, values_seq, segment, variate)
        )
        attended = attended.reshape(group_rows, local_width)
        middle = resid + branch_rows(attended, out_full)
        normed_ffn, inverse_second = norm_forward(middle, ffn_gain)
        normed_ffn_all = spread_normed(normed_ffn.astype(jnp.bfloat16))
        gate = product(normed_ffn_all, gate_full)
        upward = product(normed_ffn_all, up_full)
        sigmoid = jax.nn.sigmoid(gate)
        hidden = (gate * sigmoid * upward).astype(jnp.bfloat16)
        outputs.append((middle + branch_rows(hidden, down_full)).astype(jnp.bfloat16))
        full_weights = (
            lax.all_gather(shards[0], "fsdp", axis=0, tiled=True),
            lax.all_gather(shards[1], "fsdp", axis=0, tiled=True),
            lax.all_gather(shards[2], "fsdp", axis=0, tiled=True),
            lax.all_gather(shards[3], "fsdp", axis=1, tiled=True),
            lax.all_gather(shards[4], "fsdp", axis=0, tiled=True),
            lax.all_gather(shards[5], "fsdp", axis=0, tiled=True),
            lax.all_gather(shards[6], "fsdp", axis=1, tiled=True),
        )
        query_full, key_full, value_full, out_full, gate_full, up_full, down_full = full_weights
        grad_out = cotangent[micro_index].astype(jnp.float32)
        grad_ffn_all = spread_grads(cotangent[micro_index])
        dhidden = product_back(grad_ffn_all, down_full)
        dgate = (dhidden * upward * (sigmoid + gate * sigmoid * (1.0 - sigmoid))).astype(
            jnp.bfloat16
        )
        dupward = (dhidden * gate * sigmoid).astype(jnp.bfloat16)
        dnormed_ffn = back_rows((dgate, dupward), (gate_full, up_full))
        grad_gate = outer_sum(normed_ffn_all, dgate)
        grad_up = outer_sum(normed_ffn_all, dupward)
        grad_down = outer_sum(hidden, grad_ffn_all)
        dmiddle, gain_term = norm_backward(middle, inverse_second, ffn_gain, dnormed_ffn)
        gain_second = gain_second + gain_term
        dmiddle = dmiddle + grad_out
        grad_attn_all = spread_grads(dmiddle.astype(jnp.bfloat16))
        dattended = product_back(grad_attn_all, out_full).astype(jnp.bfloat16)
        grad_out_proj = outer_sum(attended, grad_attn_all)
        back_items = (
            query_seq,
            keys_seq,
            values_seq,
            dattended.reshape(seq_shape),
            segment,
            variate,
            logsum,
        )
        dquery, dkeys, dvalues, bias_terms = lax.map(
            partial(attend_backward, bias_pair), back_items
        )
        bias_grad = bias_grad + jnp.sum(bias_terms, axis=0)
        dquery = (
            rotate_back(dquery.reshape(heads_shape), cosine, sine)
            .astype(jnp.bfloat16)
            .reshape(group_rows, local_width)
        )
        dkeys = (
            rotate_back(dkeys.reshape(heads_shape), cosine, sine)
            .astype(jnp.bfloat16)
            .reshape(group_rows, local_width)
        )
        dvalues = dvalues.astype(jnp.bfloat16).reshape(group_rows, local_width)
        dnormed = back_rows((dquery, dkeys, dvalues), (query_full, key_full, value_full))
        grad_query = outer_sum(normed_all, dquery)
        grad_key = outer_sum(normed_all, dkeys)
        grad_value = outer_sum(normed_all, dvalues)
        dresid, gain_term = norm_backward(resid, inverse_first, attn_gain, dnormed)
        gain_first = gain_first + gain_term
        input_grads.append((dresid + dmiddle).astype(jnp.bfloat16))
        summed = (
            lax.psum_scatter(
                grad_query.astype(jnp.bfloat16), "fsdp", scatter_dimension=0, tiled=True
            ).astype(jnp.float32),
            lax.psum_scatter(
                grad_key.astype(jnp.bfloat16), "fsdp", scatter_dimension=0, tiled=True
            ).astype(jnp.float32),
            lax.psum_scatter(
                grad_value.astype(jnp.bfloat16), "fsdp", scatter_dimension=0, tiled=True
            ).astype(jnp.float32),
            lax.psum_scatter(
                grad_out_proj.astype(jnp.bfloat16), "fsdp", scatter_dimension=1, tiled=True
            ).astype(jnp.float32),
            lax.psum_scatter(
                grad_gate.astype(jnp.bfloat16), "fsdp", scatter_dimension=0, tiled=True
            ).astype(jnp.float32),
            lax.psum_scatter(
                grad_up.astype(jnp.bfloat16), "fsdp", scatter_dimension=0, tiled=True
            ).astype(jnp.float32),
            lax.psum_scatter(
                grad_down.astype(jnp.bfloat16), "fsdp", scatter_dimension=1, tiled=True
            ).astype(jnp.float32),
        )
        grad_shards = summed if grad_shards is None else jax.tree.map(jnp.add, grad_shards, summed)
    bias_full = lax.dynamic_update_slice_in_dim(
        jnp.zeros((2, head_bias.shape[1]), jnp.float32), bias_grad, head_start, 1
    )
    gain_first, gain_second, bias_full = lax.psum(
        (gain_first, gain_second, bias_full), ("fsdp", "tensor")
    )
    return (
        jnp.stack(outputs),
        jnp.stack(input_grads),
        gain_first,
        grad_shards[0],
        grad_shards[1],
        grad_shards[2],
        bias_full,
        grad_shards[3],
        gain_second,
        grad_shards[4],
        grad_shards[5],
        grad_shards[6],
    )


BF = jnp.bfloat16
F32 = jnp.float32
MESH = pl.DeviceIdType.MESH
SHARD = 64
SEQ_LEN = 256
HALF = 128
WIDTH = 1024
LOCAL = 512
HIDDEN = 2048
PAIRS = 4
COL_QKV, COL_OUT, COL_GATE, COL_UP, COL_DOWN = 0, 1536, 2048, 4096, 6144
ALL_COLS = 8192
GATHER = (
    (0, 512, False),
    (512, 512, False),
    (1024, 512, False),
    (1536, 512, False),
    (2048, 512, False),
    (2560, 512, False),
    (3072, 512, False),
    (3584, 512, False),
    (4096, 512, False),
    (4608, 512, False),
    (5120, 512, False),
    (5632, 512, False),
    (6144, 512, True),
    (6656, 512, True),
    (7168, 512, True),
    (7680, 512, True),
)
CHUNK = 2048
SCATTER = (
    (0, 0, 512, False, False),
    (0, 512, 512, False, False),
    (0, 1024, 512, False, False),
    (0, 1536, 512, False, False),
    (1, 0, 512, False, False),
    (1, 512, 512, False, False),
    (1, 1024, 512, False, False),
    (1, 1536, 512, True, False),
    (2, 0, 512, False, False),
    (2, 512, 512, False, False),
    (2, 1024, 512, False, False),
    (2, 1536, 512, False, False),
    (3, 0, 512, False, False),
    (3, 512, 512, False, False),
    (3, 1024, 512, False, False),
    (3, 1536, 512, False, True),
)
NORMAL_COLS = sum(piece[2] for piece in SCATTER if not piece[3])
TURNED_COLS = max(128, sum(piece[2] for piece in SCATTER if piece[3]))
DEPTH = 4
PROGRAM = (
    "start", "gz0", "gz1", "gz2", "gz3", "gc0", "gc1", "gz4", "gz5", "gc2", "norm", "value",
    "tables", "query", "gc3", "gz6", "key", "att0", "proj0", "gz7", "gc4", "att1", "proj1",
    "gz8", "gz9", "gc5", "gc6", "gz10", "mid0", "gc7", "mid1", "tcot", "gz11", "gate0", "gc8",
    "gc9", "up0", "gz12", "wg0", "gc10", "wg1", "gate1", "sx0", "gz13", "tffn", "sx1", "gc11",
    "hid0", "gz14", "up1", "wg2", "gz15", "wg3", "gend", "sz0", "sx2", "hid1", "sx3", "sz1",
    "dffn0", "down", "sz2", "wg4", "wg6", "wg7", "sx4", "sx6", "sp0", "sx7", "wg5", "dffn1",
    "sp1", "dmid0", "wg11", "sx5", "wg9", "wg10", "sz4", "sx9", "sz3", "wg8", "sz6", "back0",
    "sx11", "sp7", "dnorm0", "tnorm", "dmid1", "sz5", "sx8", "sz9", "back1", "sp2", "wg14",
    "sp4", "sx10", "dnorm1", "se4", "tok0", "sz11", "sx14", "wg13", "sp6", "sz8", "sp3", "wg12",
    "tok1", "sz10", "sp9", "sx13", "yout", "se6", "sz14", "tmid", "sum0", "se0", "wg15", "sx12",
    "sp5", "sp11", "sp10", "sx15", "sz13", "sp8", "fx7", "sum1", "sp14", "sum2", "sz12", "se10",
    "sz15", "se9", "sum3", "se11", "out", "se3", "sp13", "se5", "sp12", "se1", "sp15", "se13",
    "sum4", "se2", "fe7", "se14", "se12", "se8", "se15",
)
WEIGHT_ORDER = [int(name[2:]) for name in PROGRAM if name[:2] == "wg"]
CORE_ORDER = [int(name[2:]) for name in PROGRAM if name[:2] == "sx"]
FIRST_QUERY = [p for p in WEIGHT_ORDER if SCATTER[p][0] == 3][0]
LAST_DOWN = [p for p in CORE_ORDER if SCATTER[p][0] == 0][-1]


NEGATIVE = -1e30


def mm(left, right):
    return jnp.dot(left, right, preferred_element_type=F32)


def mm_nt(left, right):
    return lax.dot_general(left, right, (((1,), (1,)), ((), ())), preferred_element_type=F32)


def mm_tn(left, right):
    return lax.dot_general(left, right, (((0,), (0,)), ((), ())), preferred_element_type=F32)


def layer_kernel(
    tok_ref,
    cot_in,
    seg_ref,
    var_ref,
    time_ref,
    again_ref,
    fgain_ref,
    freq_ref,
    bias_ref,
    wq_ref,
    wk_ref,
    wv_ref,
    wo_ref,
    wg_ref,
    wu_ref,
    wd_ref,
    out_ref,
    tgrad_ref,
    gqkvo_ref,
    gg_ref,
    gu_ref,
    gd_ref,
    ga_ref,
    gf_ref,
    gb_ref,
    W,
    GD,
    RC,
    RX,
    RZ,
    RL,
    RXS,
    RZS,
    RLS,
    X,
    COT,
    N1,
    NF,
    Q,
    K,
    V,
    ATT,
    PT,
    MID,
    GT,
    UP,
    HID,
    YS,
    YR,
    YDS,
    YDR,
    YNR,
    T,
    T2,
    OUTM,
    DML,
    SAME,
    NEGM,
    COS,
    SIN,
    GF,
    GA,
    BS,
    SV,
    SR,
    local_sem,
    ag_send,
    ag_recv,
    rs_send,
    rs_recv,
    y_send,
    y_recv,
    sv_send,
    sv_recv,
    credit,
    core_credit,
):
    f = lax.axis_index("fsdp")
    y = lax.axis_index("tensor")
    z, x, c = f // 4, (f // 2) % 2, f % 2
    zs = (z + 1 - 2 * (z % 2), (z + 2) % 4, 3 - z)
    z_devs = [(zk * 4 + x * 2 + c, y) for zk in zs]
    x_dev = (z * 4 + (1 - x) * 2 + c, y)
    c_dev = (z * 4 + x * 2 + 1 - c, y)
    y_dev = (f, 1 - y)
    partners = z_devs + [x_dev, c_dev, y_dev]

    def remote(src, dst, send, recv, dev):
        return pltpu.make_async_remote_copy(
            src_ref=src, dst_ref=dst, send_sem=send, recv_sem=recv, device_id=dev, device_id_type=MESH
        )

    barrier = pltpu.get_barrier_semaphore()
    for dev in partners:
        pl.semaphore_signal(barrier, inc=1, device_id=dev, device_id_type=MESH)
    own_rows = pl.ds(pl.multiple_of(y * HALF, HALF), HALF)
    other_rows = pl.ds(pl.multiple_of((1 - y) * HALF, HALF), HALF)
    loads = [
        (tok_ref, X.at[:, own_rows]),
        (cot_in, COT.at[:, own_rows]),
        (wq_ref, W.at[z, x, c, :, pl.ds(0, LOCAL)]),
        (wk_ref, W.at[z, x, c, :, pl.ds(LOCAL, LOCAL)]),
        (wv_ref, W.at[z, x, c, :, pl.ds(2 * LOCAL, LOCAL)]),
        (wo_ref, W.at[z, x, c, :, pl.ds(COL_OUT, LOCAL)]),
        (wg_ref, W.at[z, x, c, :, pl.ds(COL_GATE, HIDDEN)]),
        (wu_ref, W.at[z, x, c, :, pl.ds(COL_UP, HIDDEN)]),
        (wd_ref, W.at[z, x, c, :, pl.ds(COL_DOWN, HIDDEN)]),
    ]
    loads = [
        pltpu.make_async_copy(src, dst, local_sem.at[i]) for i, (src, dst) in enumerate(loads)
    ]
    for load in loads:
        load.start()
    for load in loads:
        load.wait()
    pl.semaphore_wait(barrier, len(partners))

    middle = ((z + 1) // 2) % 2 == 1
    edge = ((z + 1) // 2) % 2 == 0

    ag_own, ag_pass, ag_x, ag_c = [], [], [], []
    for i, (c0, n, turned) in enumerate(GATHER):
        cols = pl.ds(c0, n)

        def block(zi):
            if turned:
                return W.at[zi, :, c, :, cols]
            return W.at[zi, x, c, :, cols]

        at = i * 6
        ag_own.append(
            [
                remote(block(z), block(z), ag_send.at[at + k], ag_recv.at[at + k], z_devs[k])
                for k in range(3)
            ]
        )
        ag_pass.append(
            remote(block(zs[1]), block(zs[1]), ag_send.at[at + 3], ag_recv.at[at + 2], z_devs[0])
        )
        part = W.at[z, x, c, :, cols] if turned else W.at[:, x, c, :, cols]
        ag_x.append(remote(part, part, ag_send.at[at + 4], ag_recv.at[at + 4], x_dev))
        part = W.at[:, :, c, :, cols]
        ag_c.append(remote(part, part, ag_send.at[at + 5], ag_recv.at[at + 5], c_dev))

    def gather_own(i):
        if GATHER[i][2]:
            ag_x[i].wait_recv()
        ag_own[i][0].start()
        ag_own[i][1].start()

        @pl.when(middle)
        def _():
            ag_own[i][2].start()

    def gather_z(i):
        ag_own[i][1].wait_recv()

        @pl.when(middle)
        def _():
            ag_pass[i].start()

        if i + DEPTH < len(GATHER):
            gather_own(i + DEPTH)
        ag_own[i][0].wait_recv()
        ag_own[i][2].wait_recv()
        if GATHER[i][2]:
            ag_c[i].start()
        else:
            ag_x[i].start()

    def gather_c(i):
        ag_x[i].wait_recv()
        ag_c[i].start()

    ended = set()

    def gather_end(c0, n):
        for i, (start_col, size, _) in enumerate(GATHER):
            if start_col < c0 + n and c0 < start_col + size and i not in ended:
                ended.add(i)
                ag_c[i].wait_recv()

    y_tok = remote(X.at[:, own_rows], X.at[:, own_rows], y_send.at[0], y_recv.at[0], y_dev)
    y_cot = remote(COT.at[:, own_rows], COT.at[:, own_rows], y_send.at[1], y_recv.at[1], y_dev)

    def start():
        for i in range(DEPTH):
            gather_own(i)
        for i, (_, _, turned) in enumerate(GATHER):
            if turned:
                ag_x[i].start()
        y_tok.start()
        y_cot.start()

        @pl.when(edge)
        def _():
            for p, (_, _, n, turned, straight) in enumerate(SCATTER):
                spot = sum(piece[2] for piece in SCATTER[:p] if piece[3] == turned)
                if turned and not straight:
                    RZS[2, :, :, pl.ds(spot, n)] = jnp.zeros((2, SHARD, n), BF)
                elif not straight:
                    RZ[2, :, pl.ds(spot, n)] = jnp.zeros((SHARD, n), BF)

    lane = lax.broadcasted_iota(jnp.int32, (1, 128), 1)
    low_lane = lane < 64
    lead_lane = (lane % 64) < 32

    def column(row):
        return jnp.transpose(jnp.broadcast_to(row.astype(F32), (128, SEQ_LEN)))

    def tables():
        for s in range(2):
            moments = column(time_ref[s : s + 1, :])
            angles = moments * freq_ref[...]
            COS[s] = jnp.cos(angles)
            sine = jnp.sin(angles)
            SIN[s] = jnp.where(lead_lane, -sine, sine)
            seg_row = seg_ref[s : s + 1, :].astype(F32)
            var_row = var_ref[s : s + 1, :].astype(F32)
            seg_col = column(seg_ref[s : s + 1, :])
            var_col = column(var_ref[s : s + 1, :])
            for h in range(2):
                part = slice(h * 128, (h + 1) * 128)
                SAME[s, :, part] = jnp.where(var_col == var_row[:, part], 1.0, 0.0)
                NEGM[s, :, part] = jnp.where(seg_col == seg_row[:, part], 0.0, NEGATIVE)

    def swap(values):
        return jnp.where(
            lead_lane, pltpu.roll(values, 96, axis=1), pltpu.roll(values, 32, axis=1)
        )

    ROWS = 64
    BLOCKS = SEQ_LEN // ROWS

    def row_loop(body):
        def step(b, carry):
            body(b, pl.ds(pl.multiple_of(b * ROWS, ROWS), ROWS))
            return carry

        lax.fori_loop(0, BLOCKS, step, 0)

    def tile_loop(count, body):
        def step(j, carry):
            body(j)
            return carry

        lax.fori_loop(0, count, step, 0)

    def tile_cols(base, j, size=256):
        return pl.ds(pl.multiple_of(base + j * size, size), size)

    def w_tile(cols):
        return W[:, :, :, :, cols].reshape(WIDTH, 256)

    def w_rows(zi, c0, n):
        return W[zi, :, :, :, pl.ds(c0, n)].reshape(256, n)

    def transpose_into(src, T):
        for s in range(2):

            def body(j):
                cols = tile_cols(0, j)
                T[cols, s * SEQ_LEN : (s + 1) * SEQ_LEN] = jnp.transpose(src[s, :, cols])

            tile_loop(4, body)

    def norm():
        y_tok.wait_recv()
        for s in range(2):

            def body(b, rows):
                v = X[s, rows, :].astype(F32)
                inv = lax.rsqrt(jnp.mean(v * v, axis=-1, keepdims=True) + EPS)
                N1[s, rows, :] = (v * inv * again_ref[...]).astype(BF)

            row_loop(body)

    def project(kind):
        gather_end(kind * LOCAL, LOCAL)
        dest = (Q, K, V)[kind]

        def body(j):
            r = mm(N1[...].reshape(2 * SEQ_LEN, WIDTH), w_tile(tile_cols(kind * LOCAL, j)))
            for h in range(2):
                part = r[:, h * 128 : (h + 1) * 128]
                if kind < 2:
                    cosine = COS[...].reshape(2 * SEQ_LEN, 128)
                    sine = SIN[...].reshape(2 * SEQ_LEN, 128)
                    part = part * cosine + swap(part) * sine
                dest[:, :, pl.ds(pl.multiple_of(j * 256 + h * 128, 128), 128)] = part.astype(
                    BF
                ).reshape(2, SEQ_LEN, 128)

        tile_loop(2, body)

    def stacked(values):
        zero = jnp.zeros_like(values)
        return jnp.concatenate(
            [jnp.where(low_lane, values, zero), jnp.where(low_lane, zero, values)], axis=0
        )

    def pair_cols(p):
        return pl.ds(pl.multiple_of(p * 128, 128), 128)

    y_att = [
        remote(YS.at[s], YR.at[s], y_send.at[2 + s], y_recv.at[2 + s], y_dev) for s in range(2)
    ]
    def attend(s):
        def body(p):
            cols = pair_cols(p)
            keys = stacked(K[s, :, cols] * jnp.asarray(0.125, BF))
            scores = mm_nt(keys, Q[s, :, cols])
            parts = []
            for h in range(2):
                head = y * 8 + p * 2 + h
                same_bias = bias_ref[0, head]
                other_bias = bias_ref[1, head]
                sc = scores[h * SEQ_LEN : (h + 1) * SEQ_LEN]
                sc = sc + (SAME[s] * (same_bias - other_bias) + (NEGM[s] + other_bias))
                top = jnp.max(sc, axis=0, keepdims=True)
                expo = jnp.exp(sc - top)
                total = jnp.sum(expo, axis=0, keepdims=True)
                parts.append((expo * (1.0 / total)).astype(BF))
            probs = jnp.concatenate(parts, axis=0)
            PT[s * PAIRS + p] = probs
            ATT[s, :, cols] = mm_tn(probs, stacked(V[s, :, cols])).astype(BF)

        tile_loop(PAIRS, body)

    def project_out(s):
        if s == 0:
            gather_end(COL_OUT, LOCAL)
        for zi in range(4):
            YS[s, :, zi * 256 : (zi + 1) * 256] = mm_nt(
                ATT[s], w_rows(zi, COL_OUT, LOCAL)
            ).astype(BF)
        y_att[s].start()

    def middle_rows(s):
        y_att[s].wait_recv()

        def body(b, rows):
            v = X[s, rows, :].astype(F32) + (YS[s, rows, :].astype(F32) + YR[s, rows, :].astype(F32))
            MID[s, rows, :] = v
            inv = lax.rsqrt(jnp.mean(v * v, axis=-1, keepdims=True) + EPS)
            NF[s, rows, :] = (v * inv * fgain_ref[...]).astype(BF)

        row_loop(body)
        if s == 1:
            for k in range(2):
                y_att[k].wait_send()
            pl.semaphore_signal(credit, inc=1, device_id=y_dev, device_id_type=MESH)

    def gate_tiles(half):
        gather_end(COL_GATE + half * 1024, 1024)

        def body(j):
            cols = tile_cols(half * 1024, j)
            GT[:, cols] = mm(
                NF[...].reshape(2 * SEQ_LEN, WIDTH), w_tile(tile_cols(COL_GATE + half * 1024, j))
            ).astype(BF)

        tile_loop(4, body)

    def up_tiles(half):
        gather_end(COL_UP + half * 1024, 1024)

        def body(j):
            cols = tile_cols(half * 1024, j)
            up = mm(
                NF[...].reshape(2 * SEQ_LEN, WIDTH), w_tile(tile_cols(COL_UP + half * 1024, j))
            )
            UP[:, cols] = up.astype(BF)
            gate = GT[:, cols].astype(F32)
            HID[:, cols] = (gate * jax.nn.sigmoid(gate) * up).astype(BF)

        tile_loop(4, body)

    def turn_cotangent():
        y_cot.wait_recv()
        transpose_into(COT, T)

    homes = ((GD, 0), (W, COL_DOWN), (W, COL_GATE), (W, COL_UP))
    results = (gd_ref, gg_ref, gu_ref, gqkvo_ref)

    def home(ch, *index, c0=0, n=CHUNK):
        ref, base = homes[ch]
        return ref.at[index + (slice(None), pl.ds(base + c0, n))]

    every = slice(None)
    slots = (0, 1, 2, 0)
    rs_c, rs_x, rs_z, rs_relay = [], [], [], []
    spots = []
    for p, (ch, c0, n, turned, straight) in enumerate(SCATTER):
        spot = sum(piece[2] for piece in SCATTER[:p] if piece[3] == turned)
        spots.append(spot)
        at = p * 6

        def sems(k):
            return rs_send.at[at + k], rs_recv.at[at + k]

        rs_c.append(
            remote(
                home(ch, every, every, 1 - c, c0=c0, n=n),
                RC.at[slots[ch], :, :, :, pl.ds(c0, n)],
                *sems(0),
                c_dev,
            )
        )
        cols = pl.ds(spot, n)
        if turned:
            rs_x.append(
                remote(home(ch, z, 1 - x, c, c0=c0, n=n), RXS.at[:, cols], *sems(1), x_dev)
            )
            views = [home(ch, zk, every, c, c0=c0, n=n) for zk in zs]
            boxes, relay = [RZS.at[k, :, :, cols] for k in range(3)], RLS.at[:, :, cols]
        else:
            rs_x.append(
                remote(
                    home(ch, every, 1 - x, c, c0=c0, n=n), RX.at[:, :, cols], *sems(1), x_dev
                )
            )
            views = [home(ch, zk, x, c, c0=c0, n=n) for zk in zs]
            boxes, relay = [RZ.at[k, :, cols] for k in range(3)], RL.at[:, cols]
        rs_z.append(
            [remote(views[k], boxes[k], *sems(2 + k), z_devs[k]) for k in range(3)]
        )
        rs_relay.append(remote(views[2], relay, *sems(5), z_devs[0]))

    def add_core(p, xi):
        ch, c0, n, turned, straight = SCATTER[p]

        def body(zi):
            view = home(ch, zi, xi, c, c0=c0, n=n)
            view[...] = view[...] + RC[slots[ch], zi, xi, :, pl.ds(c0, n)]

        tile_loop(4, body)

    def send_z(p):
        rs_z[p][0].start()
        if SCATTER[p][4]:
            rs_z[p][1].start()
            rs_z[p][2].start()
            return

        @pl.when(middle)
        def _():
            rs_z[p][2].start()

        @pl.when(edge)
        def _():
            rs_z[p][1].start()
            rs_relay[p].start()

    def scatter_x(p):
        rs_c[p].wait_recv()
        add_core(p, 1 - x)
        if SCATTER[p][3]:
            add_core(p, x)
            send_z(p)
        else:
            rs_x[p].start()
            add_core(p, x)
        if p == LAST_DOWN:
            pl.semaphore_signal(core_credit, inc=1, device_id=c_dev, device_id_type=MESH)

    def scatter_z(p):
        ch, c0, n, turned, straight = SCATTER[p]
        rs_x[p].wait_recv()

        def body(zi):
            view = home(ch, zi, x, c, c0=c0, n=n)
            view[...] = view[...] + RX[zi, :, pl.ds(spots[p], n)]

        tile_loop(4, body)
        send_z(p)

    def scatter_pass(p):
        ch, c0, n, turned, straight = SCATTER[p]
        if straight:
            return

        @pl.when(middle)
        def _():
            rs_relay[p].wait_recv()
            if turned:
                view = home(ch, zs[1], every, c, c0=c0, n=n)
                view[...] = view[...] + RLS[:, :, pl.ds(spots[p], n)]
            else:
                view = home(ch, zs[1], x, c, c0=c0, n=n)
                view[...] = view[...] + RL[:, pl.ds(spots[p], n)]
            rs_z[p][1].start()

    def wait_z(p):
        rs_z[p][0].wait_recv()
        rs_z[p][1].wait_recv()
        if SCATTER[p][4]:
            rs_z[p][2].wait_recv()
            return

        @pl.when(middle)
        def _():
            rs_z[p][2].wait_recv()

    def scatter_end(p):
        ch, c0, n, turned, straight = SCATTER[p]
        wait_z(p)

        def body(j):
            total = home(ch, z, x, c)[:, tile_cols(c0, j)].astype(F32)
            for k in range(3):
                total = total + RZ[k, :, tile_cols(spots[p], j)].astype(F32)
            results[ch][:, tile_cols(c0, j)] = total

        tile_loop(n // 256, body)

    def turned_x(p):
        ch, c0, n, turned, straight = SCATTER[p]
        wait_z(p)
        for xi in range(2):
            view = home(ch, z, xi, c, c0=c0, n=n)
            total = view[...].astype(F32)
            for k in range(3):
                total = total + RZS[k, xi, :, pl.ds(spots[p], n)].astype(F32)
            view[...] = total.astype(BF)
        rs_x[p].start()

    def turned_end(p):
        ch, c0, n, turned, straight = SCATTER[p]
        rs_x[p].wait_recv()
        own = home(ch, z, x, c, c0=c0, n=n)[...].astype(F32)
        results[ch][:, c0 : c0 + n] = own + RXS[:, pl.ds(spots[p], n)].astype(F32)

    def weight_tiles(ch, c0, n):
        ref, base = homes[ch]

        def body(j):
            cols = tile_cols(c0, j)
            if ch == 0:
                left, right = T, HID[:, cols]
            elif ch == 1:
                left, right = T2, GT[:, cols]
            elif ch == 2:
                left, right = T2, UP[:, cols]
            elif c0 < 3 * LOCAL:
                left, right = T2, DQKV[:, cols]
            else:
                left, right = T, ATT[:, :, tile_cols(c0 - 3 * LOCAL, j)].reshape(2 * SEQ_LEN, 256)
            r = mm(left[...], right)
            ref[:, :, :, :, tile_cols(base + c0, j)] = r.astype(BF).reshape(4, 2, 2, SHARD, 256)

        tile_loop(n // 256, body)

    def weight_grad(p):
        ch, c0, n, turned, straight = SCATTER[p]
        if p == FIRST_QUERY:
            pl.semaphore_wait(core_credit, 1)
        if ch == 3 and c0 < 3 * LOCAL < c0 + n:
            weight_tiles(ch, c0, 3 * LOCAL - c0)
            weight_tiles(ch, 3 * LOCAL, c0 + n - 3 * LOCAL)
        else:
            weight_tiles(ch, c0, n)
        rs_c[p].start()

    def hidden_back(half):
        gather_end(COL_DOWN + half * 1024, 1024)

        def body(j):
            cols = tile_cols(half * 1024, j)
            dhid = mm(
                COT[...].reshape(2 * SEQ_LEN, WIDTH), w_tile(tile_cols(COL_DOWN + half * 1024, j))
            )
            gate = GT[:, cols].astype(F32)
            up = UP[:, cols].astype(F32)
            sig = jax.nn.sigmoid(gate)
            GT[:, cols] = (dhid * up * (sig + gate * sig * (1.0 - sig))).astype(BF)
            UP[:, cols] = (dhid * gate * sig).astype(BF)

        tile_loop(4, body)

    def gather_sent():
        for i in range(len(GATHER)):
            ag_own[i][0].wait_send()
            ag_own[i][1].wait_send()
            ag_x[i].wait_send()
            ag_c[i].wait_send()

            @pl.when(middle)
            def _():
                ag_own[i][2].wait_send()
                ag_pass[i].wait_send()

    def last_product():
        def body(zi):
            cols = tile_cols(0, zi)
            r = mm_nt(HID[...], w_rows(zi, COL_DOWN, HIDDEN)).reshape(2, 2, HALF, 256)
            mine = jnp.where(y == 0, r[:, 0], r[:, 1])
            OUTM[:, :, cols] = MID[:, own_rows, cols] + mine
            YDS[:, :, cols] = jnp.where(y == 0, r[:, 1], r[:, 0]).astype(BF)

        tile_loop(4, body)

    y_dnf = [
        remote(YS.at[s], YR.at[s], y_send.at[4 + s], y_recv.at[4 + s], y_dev) for s in range(2)
    ]
    y_out = remote(YDS, YDR, y_send.at[6], y_recv.at[6], y_dev)

    def ffn_back(s):
        if s == 0:
            pl.semaphore_wait(credit, 1)
        rows = slice(s * SEQ_LEN, (s + 1) * SEQ_LEN)

        def body(zi):
            r = mm_nt(GT[rows, :], w_rows(zi, COL_GATE, HIDDEN))
            r = r + mm_nt(UP[rows, :], w_rows(zi, COL_UP, HIDDEN))
            YS[s, :, tile_cols(0, zi)] = r.astype(BF)

        tile_loop(4, body)
        y_dnf[s].start()

    DAT = HID.at[:, 3 * LOCAL : 4 * LOCAL]
    DQKV = HID

    def middle_back(s):
        if s == 0:
            GF[...] = jnp.zeros_like(GF)
            GA[...] = jnp.zeros_like(GA)
        y_dnf[s].wait_recv()

        def body(b, rows):
            v = MID[s, rows, :]
            inv = lax.rsqrt(jnp.mean(v * v, axis=-1, keepdims=True) + EPS)
            scaled = v * inv
            dn = YS[s, rows, :].astype(F32) + YR[s, rows, :].astype(F32)
            flag = jnp.where(b // (HALF // ROWS) == y, 1.0, 0.0)
            GF[...] += flag * jnp.sum((dn * scaled).reshape(ROWS // 8, 8, WIDTH), axis=0)
            u = dn * fgain_ref[...]
            dm = COT[s, rows, :].astype(F32) + inv * (
                u - scaled * jnp.mean(u * scaled, axis=-1, keepdims=True)
            )
            MID[s, rows, :] = dm
            DML[s, rows, :] = dm.astype(BF)

        row_loop(body)
        seq_rows = slice(s * SEQ_LEN, (s + 1) * SEQ_LEN)

        def body(j):
            DAT[seq_rows, tile_cols(0, j)] = mm(DML[s], w_tile(tile_cols(COL_OUT, j))).astype(BF)

        tile_loop(2, body)

    def attend_back(s):
        seq_rows = slice(s * SEQ_LEN, (s + 1) * SEQ_LEN)

        def body(p):
            cols = pair_cols(p)
            do = DAT[seq_rows, cols]
            dprobs = mm_nt(stacked(V[s, :, cols]), do)
            probs_low = PT[s * PAIRS + p]
            parts = []
            for h in range(2):
                part = slice(h * SEQ_LEN, (h + 1) * SEQ_LEN)
                pr = probs_low[part].astype(F32)
                dp = dprobs[part]
                dot = jnp.sum(pr * dp, axis=0, keepdims=True)
                ds = (pr * (dp - dot)).astype(BF)
                wide = ds.astype(F32)
                same = wide * SAME[s]
                same_sum = jnp.sum(same, axis=0, keepdims=True)
                other_sum = jnp.sum(wide - same, axis=0, keepdims=True)
                if s == 0:
                    BS[0, p * 2 + h] = same_sum
                    BS[1, p * 2 + h] = other_sum
                else:
                    BS[0, p * 2 + h] += same_sum
                    BS[1, p * 2 + h] += other_sum
                parts.append(ds)
            dsc = jnp.concatenate(parts, axis=0)
            dv = mm(probs_low, do)
            dv = jnp.where(low_lane, dv[:SEQ_LEN], dv[SEQ_LEN:])
            dk = mm(dsc, Q[s, :, cols])
            dk = jnp.where(low_lane, dk[:SEQ_LEN], dk[SEQ_LEN:]) * 0.125
            dq = mm_tn(dsc, stacked(K[s, :, cols] * jnp.asarray(0.125, BF)))
            dq = dq * COS[s] - swap(dq) * SIN[s]
            dk = dk * COS[s] - swap(dk) * SIN[s]
            DQKV[seq_rows, cols] = dq.astype(BF)
            DQKV[seq_rows, pl.ds(pl.multiple_of(LOCAL + p * 128, 128), 128)] = dk.astype(BF)
            DQKV[seq_rows, pl.ds(pl.multiple_of(2 * LOCAL + p * 128, 128), 128)] = dv.astype(BF)

        tile_loop(PAIRS, body)

    y_dn = [
        remote(YS.at[s, other_rows], YNR.at[s], y_send.at[7 + s], y_recv.at[7 + s], y_dev)
        for s in range(2)
    ]

    def norm_back(s):
        if s == 0:
            for k in range(2):
                y_dnf[k].wait_send()
        seq_rows = slice(s * SEQ_LEN, (s + 1) * SEQ_LEN)

        def body(zi):
            r = mm_nt(DQKV[seq_rows, 0 : 3 * LOCAL], w_rows(zi, COL_QKV, 3 * LOCAL))
            YS[s, :, tile_cols(0, zi)] = r.astype(BF)

        tile_loop(4, body)
        y_dn[s].start()

    def finish_out():
        y_out.wait_recv()
        for s in range(2):

            def body(b, carry):
                rows = pl.ds(pl.multiple_of(b * ROWS, ROWS), ROWS)
                out_ref[s, rows, :] = (OUTM[s, rows, :] + YDR[s, rows, :].astype(F32)).astype(BF)
                return carry

            lax.fori_loop(0, HALF // ROWS, body, 0)

    def token_rows(s):
        y_dn[s].wait_recv()

        def body(b, carry):
            rows = pl.ds(pl.multiple_of(b * ROWS, ROWS), ROWS)
            mine = pl.ds(pl.multiple_of(y * HALF + b * ROWS, ROWS), ROWS)
            v = X[s, mine, :].astype(F32)
            inv = lax.rsqrt(jnp.mean(v * v, axis=-1, keepdims=True) + EPS)
            scaled = v * inv
            dn = YS[s, mine, :].astype(F32) + YNR[s, rows, :].astype(F32)
            GA[...] += jnp.sum((dn * scaled).reshape(ROWS // 8, 8, WIDTH), axis=0)
            u = dn * again_ref[...]
            dx = MID[s, mine, :] + inv * (
                u - scaled * jnp.mean(u * scaled, axis=-1, keepdims=True)
            )
            tgrad_ref[s, rows, :] = dx.astype(BF)
            return carry

        lax.fori_loop(0, HALF // ROWS, body, 0)

    def sum_start():
        SV[0] = jnp.zeros((24, 128), F32)
        first_sum = jnp.sum(GA[...], axis=0, keepdims=True)
        second_sum = jnp.sum(GF[...], axis=0, keepdims=True)
        for j in range(8):
            SV[0, j : j + 1, :] = first_sum[:, j * 128 : (j + 1) * 128]
            SV[0, 8 + j : 9 + j, :] = second_sum[:, j * 128 : (j + 1) * 128]
        for kind in range(2):
            row = jnp.zeros((1, 128), F32)
            for h in range(8):
                head_sum = jnp.sum(BS[kind, h], axis=1, keepdims=True)
                row = row + jnp.where(lane == y * 8 + h, head_sum, 0.0)
            SV[0, 16 + kind : 17 + kind, :] = row
        sums[0][0].start()

    sums = [
        [remote(SV.at[0], SR.at[0], sv_send.at[0], sv_recv.at[0], c_dev)],
        [remote(SV.at[1], SR.at[1], sv_send.at[1], sv_recv.at[1], y_dev)],
        [
            remote(SV.at[2], SR.at[2 + k], sv_send.at[2 + k], sv_recv.at[2 + k], z_devs[k])
            for k in range(3)
        ],
        [remote(SV.at[3], SR.at[5], sv_send.at[5], sv_recv.at[5], x_dev)],
    ]

    def sum_stage(i):
        total = SV[i]
        for copy in sums[i]:
            copy.wait_recv()
        first = (0, 1, 2, 5)[i]
        for k in range(len(sums[i])):
            total = total + SR[first + k]
        if i < 3:
            SV[i + 1] = total
            for copy in sums[i + 1]:
                copy.start()
        else:
            for j in range(8):
                cols = slice(j * 128, (j + 1) * 128)
                ga_ref[:, cols] = total[j : j + 1]
                gf_ref[:, cols] = total[8 + j : 9 + j]
            gb_ref[...] = total[16:18, 0:16]

    steps = {
        "start": start,
        "tables": tables,
        "norm": norm,
        "query": partial(project, 0),
        "key": partial(project, 1),
        "value": partial(project, 2),
        "tcot": turn_cotangent,
        "tffn": partial(transpose_into, NF, T2),
        "tnorm": partial(transpose_into, N1, T2),
        "tmid": partial(transpose_into, DML, T),
        "down": last_product,
        "gend": gather_sent,
        "yout": y_out.start,
        "out": finish_out,
        "sum0": sum_start,
    }
    for s in range(2):
        steps[f"att{s}"] = partial(attend, s)
        steps[f"proj{s}"] = partial(project_out, s)
        steps[f"mid{s}"] = partial(middle_rows, s)
        steps[f"gate{s}"] = partial(gate_tiles, s)
        steps[f"up{s}"] = partial(up_tiles, s)
        steps[f"hid{s}"] = partial(hidden_back, s)
        steps[f"dffn{s}"] = partial(ffn_back, s)
        steps[f"dmid{s}"] = partial(middle_back, s)
        steps[f"back{s}"] = partial(attend_back, s)
        steps[f"dnorm{s}"] = partial(norm_back, s)
        steps[f"tok{s}"] = partial(token_rows, s)
    for i in range(len(GATHER)):
        steps[f"gz{i}"] = partial(gather_z, i)
        steps[f"gc{i}"] = partial(gather_c, i)
    for i in range(4):
        steps[f"sum{i + 1}"] = partial(sum_stage, i)
    for p in range(len(SCATTER)):
        steps[f"wg{p}"] = partial(weight_grad, p)
        steps[f"sx{p}"] = partial(scatter_x, p)
        steps[f"sz{p}"] = partial(scatter_z, p)
        steps[f"sp{p}"] = partial(scatter_pass, p)
        steps[f"se{p}"] = partial(scatter_end, p)
        steps[f"fx{p}"] = partial(turned_x, p)
        steps[f"fe{p}"] = partial(turned_end, p)
    for name in PROGRAM:
        steps[name]()

    y_out.wait_send()
    for s in range(2):
        y_dn[s].wait_send()
    y_tok.wait_send()
    y_cot.wait_send()
    for group in sums:
        for copy in group:
            copy.wait_send()
    for p in range(len(SCATTER)):
        rs_c[p].wait_send()
        rs_x[p].wait_send()
        rs_z[p][0].wait_send()
        rs_z[p][1].wait_send()
        if SCATTER[p][4]:
            rs_z[p][2].wait_send()
            continue

        @pl.when(middle)
        def _():
            rs_z[p][2].wait_send()

        @pl.when(edge)
        def _():
            rs_relay[p].wait_send()


def finish_kernel(*refs):
    sources, dests, boxes = refs[:9], refs[9:21], refs[21:30]
    in_sem, out_sem = refs[30], refs[31]
    order = (0, 1, 5, 4, 3, 2, 6, 7, 8)
    loads = {k: pltpu.make_async_copy(sources[k], boxes[k], in_sem.at[k]) for k in order}
    for k in order:
        loads[k].start()
    places = {0: (0,), 1: (1,), 2: (3, 4, 5, 7), 3: (9,), 4: (10,), 5: (11,), 6: (2,), 7: (8,), 8: (6,)}
    stores = []
    for k in order:
        loads[k].wait()
        for i, place in enumerate(places[k]):
            box = boxes[k].at[:, pl.ds(i * LOCAL, LOCAL)] if k == 2 else boxes[k]
            store = pltpu.make_async_copy(box, dests[place], out_sem.at[place])
            store.start()
            stores.append(store)
    for store in stores:
        store.wait()


def fused_local(
    tokens,
    segment_ids,
    variate_ids,
    time_ids,
    attn_gain,
    w_query,
    w_key,
    w_value,
    head_bias,
    w_out,
    ffn_gain,
    w_gate,
    w_up,
    w_down,
    cotangent,
):
    inverse = 10000.0 ** (-(np.arange(32, dtype=np.float32) / np.float32(32)))
    freq = jnp.asarray(np.tile(inverse.astype(np.float32), 4)[None, :])
    vmem = pl.BlockSpec(memory_space=pltpu.VMEM)
    anym = pl.BlockSpec(memory_space=pl.ANY)
    smem = pl.BlockSpec(memory_space=pltpu.SMEM)
    bf = lambda *shape: pltpu.VMEM(shape, BF)
    fl = lambda *shape: pltpu.VMEM(shape, F32)
    seq3 = (2, SEQ_LEN, WIDTH)
    half3 = (2, HALF, WIDTH)
    dma = pltpu.SemaphoreType.DMA
    scratch = [
        bf(4, 2, 2, SHARD, ALL_COLS),
        bf(4, 2, 2, SHARD, CHUNK),
        bf(3, 4, 2, SHARD, CHUNK),
        bf(4, SHARD, NORMAL_COLS),
        bf(3, SHARD, NORMAL_COLS),
        bf(SHARD, NORMAL_COLS),
        bf(SHARD, TURNED_COLS),
        bf(3, 2, SHARD, TURNED_COLS),
        bf(2, SHARD, TURNED_COLS),
        bf(*seq3),
        bf(*seq3),
        bf(*seq3),
        bf(*seq3),
        bf(2, SEQ_LEN, LOCAL),
        bf(2, SEQ_LEN, LOCAL),
        bf(2, SEQ_LEN, LOCAL),
        bf(2, SEQ_LEN, LOCAL),
        bf(2 * PAIRS, 2 * SEQ_LEN, SEQ_LEN),
        fl(*seq3),
        bf(2 * SEQ_LEN, HIDDEN),
        bf(2 * SEQ_LEN, HIDDEN),
        bf(2 * SEQ_LEN, HIDDEN),
        bf(*seq3),
        bf(*seq3),
        bf(*half3),
        bf(*half3),
        bf(*half3),
        bf(WIDTH, 2 * SEQ_LEN),
        bf(WIDTH, 2 * SEQ_LEN),
        fl(*half3),
        bf(*seq3),
        fl(2, SEQ_LEN, SEQ_LEN),
        fl(2, SEQ_LEN, SEQ_LEN),
        fl(2, SEQ_LEN, 128),
        fl(2, SEQ_LEN, 128),
        fl(8, WIDTH),
        fl(8, WIDTH),
        fl(2, 8, 1, SEQ_LEN),
        fl(4, 24, 128),
        fl(6, 24, 128),
        dma((9,)),
        dma((6 * len(GATHER),)),
        dma((6 * len(GATHER),)),
        dma((6 * len(SCATTER),)),
        dma((6 * len(SCATTER),)),
        dma((9,)),
        dma((9,)),
        dma((6,)),
        dma((6,)),
        pltpu.SemaphoreType.REGULAR,
        pltpu.SemaphoreType.REGULAR,
    ]
    shape = jax.ShapeDtypeStruct
    outs = pl.pallas_call(
        layer_kernel,
        out_shape=(
            shape(half3, BF),
            shape(half3, BF),
            shape((SHARD, HIDDEN), F32),
            shape((SHARD, HIDDEN), F32),
            shape((SHARD, HIDDEN), F32),
            shape((SHARD, HIDDEN), F32),
            shape((1, WIDTH), F32),
            shape((1, WIDTH), F32),
            shape((2, 16), F32),
        ),
        in_specs=[anym, anym, vmem, vmem, vmem, vmem, vmem, vmem, smem] + [anym] * 7,
        out_specs=(vmem,) * 9,
        scratch_shapes=scratch,
        compiler_params=pltpu.CompilerParams(
            collective_id=0, has_side_effects=True, vmem_limit_bytes=67043328
        ),
        name="layer",
    )(
        tokens,
        cotangent,
        segment_ids,
        variate_ids,
        time_ids,
        attn_gain.reshape(1, WIDTH),
        ffn_gain.reshape(1, WIDTH),
        freq,
        head_bias,
        w_query,
        w_key,
        w_value,
        w_out.T,
        w_gate,
        w_up,
        w_down.T,
    )
    finals = pl.pallas_call(
        finish_kernel,
        out_shape=(
            shape(half3, BF),
            shape(half3, BF),
            shape((1, WIDTH), F32),
            shape((SHARD, LOCAL), F32),
            shape((SHARD, LOCAL), F32),
            shape((SHARD, LOCAL), F32),
            shape((2, 16), F32),
            shape((SHARD, LOCAL), F32),
            shape((1, WIDTH), F32),
            shape((SHARD, HIDDEN), F32),
            shape((SHARD, HIDDEN), F32),
            shape((SHARD, HIDDEN), F32),
        ),
        in_specs=[anym] * 9,
        out_specs=[anym] * 12,
        scratch_shapes=[
            bf(*half3),
            bf(*half3),
            fl(SHARD, HIDDEN),
            fl(SHARD, HIDDEN),
            fl(SHARD, HIDDEN),
            fl(SHARD, HIDDEN),
            fl(1, WIDTH),
            fl(1, WIDTH),
            fl(2, 16),
            dma((9,)),
            dma((12,)),
        ],
        name="finish",
    )(*outs)
    layer_out, tokens_grad, ga, gq, gk, gv, gb, go, gf, gg, gu, gd = finals
    return (
        layer_out,
        tokens_grad,
        ga.reshape(WIDTH),
        gq,
        gk,
        gv,
        gb,
        go.T,
        gf.reshape(WIDTH),
        gg,
        gu,
        gd.T,
    )


def fits(mesh, tokens, w_query, w_gate):
    sizes = dict(mesh.shape)
    return (
        sizes["fsdp"] == 16
        and sizes["tensor"] == 2
        and tokens.shape == (2, 16 * SEQ_LEN, WIDTH)
        and w_query.shape == (WIDTH, 2 * LOCAL)
        and w_gate.shape == (WIDTH, 2 * HIDDEN)
    )


def solution(mesh):
    placed = (
        P(None, ("fsdp", "tensor"), None),
        P(None, "fsdp"),
        P(None, "fsdp"),
        P(None, "fsdp"),
        P(),
        P("fsdp", "tensor"),
        P("fsdp", "tensor"),
        P("fsdp", "tensor"),
        P(),
        P("tensor", "fsdp"),
        P(),
        P("fsdp", "tensor"),
        P("fsdp", "tensor"),
        P("tensor", "fsdp"),
        P(None, ("fsdp", "tensor"), None),
    )
    outs = (
        P(None, ("fsdp", "tensor"), None),
        P(None, ("fsdp", "tensor"), None),
        P(),
        P("fsdp", "tensor"),
        P("fsdp", "tensor"),
        P("fsdp", "tensor"),
        P(),
        P("tensor", "fsdp"),
        P(),
        P("fsdp", "tensor"),
        P("fsdp", "tensor"),
        P("tensor", "fsdp"),
    )

    def whole(*args):
        body = fused_local if fits(mesh, args[0], args[5], args[11]) else local
        return jax.shard_map(
            body, mesh=mesh, in_specs=placed, out_specs=outs, check_vma=False
        )(*args)

    return whole
```

```python
from functools import partial
from functools import reduce

import jax
import jax.numpy as jnp
import numpy as np
from jax import lax
from jax.experimental import pallas as pl
from jax.experimental.pallas import tpu as pltpu
from jax.sharding import PartitionSpec as P

HEAD_DIM = 64
SEQ_MAX = 1024


EPS = 1e-06


def product(left, right):
    return jnp.dot(left, right, preferred_element_type=jnp.float32)


def product_back(left, right):
    return lax.dot_general(
        left, right, (((1,), (1,)), ((), ())), preferred_element_type=jnp.float32
    )


def outer_sum(left, right):
    return lax.dot_general(
        left, right, (((0,), (0,)), ((), ())), preferred_element_type=jnp.float32
    )


def norm_forward(resid, gain):
    inverse = lax.rsqrt(jnp.mean(resid * resid, axis=-1, keepdims=True) + EPS)
    return (resid * inverse * gain, inverse)


def norm_backward(resid, inverse, gain, upstream):
    scaled = resid * inverse
    weighted = upstream * gain
    back = inverse * (weighted - scaled * jnp.mean(weighted * scaled, axis=-1, keepdims=True))
    return (back, jnp.sum(upstream * scaled, axis=0))


def rope_tables(moments, half_width):
    inverse = 10000.0 ** (-(jnp.arange(half_width, dtype=jnp.float32) / half_width))
    angles = moments.astype(jnp.float32)[:, None] * inverse[None, :]
    return (jnp.cos(angles), jnp.sin(angles))


def rotate(values, cosine, sine):
    half_width = values.shape[-1] // 2
    leading = values[..., :half_width]
    trailing = values[..., half_width:]
    cosine = cosine[:, None, :]
    sine = sine[:, None, :]
    return jnp.concatenate(
        [leading * cosine - trailing * sine, trailing * cosine + leading * sine], axis=-1
    )


def rotate_back(grads, cosine, sine):
    half_width = grads.shape[-1] // 2
    leading = grads[..., :half_width]
    trailing = grads[..., half_width:]
    cosine = cosine[:, None, :]
    sine = sine[:, None, :]
    return jnp.concatenate(
        [leading * cosine + trailing * sine, trailing * cosine - leading * sine], axis=-1
    )


def masked_scores(query, keys, segment, variate, bias_pair):
    scores = jnp.einsum(
        "qhd,khd->hqk", query, keys, preferred_element_type=jnp.float32
    ) * HEAD_DIM ** (-0.5)
    same_variate = variate[:, None] == variate[None, :]
    scores = scores + jnp.where(
        same_variate[None], bias_pair[0][:, None, None], bias_pair[1][:, None, None]
    )
    allowed = segment[:, None] == segment[None, :]
    return (jnp.where(allowed[None], scores, -1e30), same_variate)


def attend_forward(bias_pair, item):
    query, keys, values, segment, variate = item
    scores, unused = masked_scores(query, keys, segment, variate, bias_pair)
    highest = jnp.max(scores, axis=-1, keepdims=True)
    expo = jnp.exp(scores - highest)
    total = jnp.sum(expo, axis=-1, keepdims=True)
    probs = (expo / total).astype(jnp.bfloat16)
    attended = jnp.einsum("hqk,khd->qhd", probs, values, preferred_element_type=jnp.float32)
    return (attended.astype(jnp.bfloat16), (highest + jnp.log(total))[..., 0])


def attend_backward(bias_pair, item):
    query, keys, values, dattended, segment, variate, logsum = item
    scores, same_variate = masked_scores(query, keys, segment, variate, bias_pair)
    probs = jnp.exp(scores - logsum[..., None])
    probs_low = probs.astype(jnp.bfloat16)
    dprobs = jnp.einsum("qhd,khd->hqk", dattended, values, preferred_element_type=jnp.float32)
    dvalues = jnp.einsum("hqk,qhd->khd", probs_low, dattended, preferred_element_type=jnp.float32)
    dscores = (probs * (dprobs - jnp.sum(probs * dprobs, axis=-1, keepdims=True))).astype(
        jnp.bfloat16
    )
    widened = dscores.astype(jnp.float32)
    same_sum = jnp.sum(jnp.where(same_variate[None], widened, 0.0), axis=(1, 2))
    other_sum = jnp.sum(jnp.where(same_variate[None], 0.0, widened), axis=(1, 2))
    dquery = jnp.einsum(
        "hqk,khd->qhd", dscores, keys, preferred_element_type=jnp.float32
    ) * HEAD_DIM ** (-0.5)
    dkeys = jnp.einsum(
        "hqk,qhd->khd", dscores, query, preferred_element_type=jnp.float32
    ) * HEAD_DIM ** (-0.5)
    return (dquery, dkeys, dvalues, jnp.stack([same_sum, other_sum]))


def local(
    tokens,
    segment_ids,
    variate_ids,
    time_ids,
    attn_gain,
    w_query,
    w_key,
    w_value,
    head_bias,
    w_out,
    ffn_gain,
    w_gate,
    w_up,
    w_down,
    cotangent,
):
    micro_count, row_count, model_width = tokens.shape
    group_rows = segment_ids.shape[1]
    seq_len = min(SEQ_MAX, group_rows)
    seq_count = group_rows // seq_len
    local_width = w_query.shape[1]
    local_heads = local_width // HEAD_DIM
    head_start = lax.axis_index("tensor") * local_heads
    bias_pair = lax.dynamic_slice_in_dim(head_bias, head_start, local_heads, 1)
    shards = (w_query, w_key, w_value, w_out, w_gate, w_up, w_down)
    heads_shape = (group_rows, local_heads, HEAD_DIM)
    seq_shape = (seq_count, seq_len, local_heads, HEAD_DIM)

    def spread_normed(block):
        return lax.all_gather(block, "tensor", axis=0, tiled=True)

    def spread_grads(block):
        return lax.all_gather(block, "tensor", axis=0, tiled=True)

    def branch_rows(left, right):
        return lax.psum_scatter(product(left, right), "tensor", scatter_dimension=0, tiled=True)

    def back_rows(lefts, rights):
        pieces = [product_back(left, right) for left, right in zip(lefts, rights)]
        return lax.psum_scatter(reduce(jnp.add, pieces), "tensor", scatter_dimension=0, tiled=True)

    outputs = []
    input_grads = []
    grad_shards = None
    gain_first = jnp.zeros((model_width,), jnp.float32)
    gain_second = jnp.zeros((model_width,), jnp.float32)
    bias_grad = jnp.zeros((2, local_heads), jnp.float32)
    for micro_index in range(micro_count):
        full_weights = (
            lax.all_gather(shards[0], "fsdp", axis=0, tiled=True),
            lax.all_gather(shards[1], "fsdp", axis=0, tiled=True),
            lax.all_gather(shards[2], "fsdp", axis=0, tiled=True),
            lax.all_gather(shards[3], "fsdp", axis=1, tiled=True),
            lax.all_gather(shards[4], "fsdp", axis=0, tiled=True),
            lax.all_gather(shards[5], "fsdp", axis=0, tiled=True),
            lax.all_gather(shards[6], "fsdp", axis=1, tiled=True),
        )
        query_full, key_full, value_full, out_full, gate_full, up_full, down_full = full_weights
        resid = tokens[micro_index].astype(jnp.float32)
        segment = segment_ids[micro_index].reshape(seq_count, seq_len)
        variate = variate_ids[micro_index].reshape(seq_count, seq_len)
        cosine, sine = rope_tables(time_ids[micro_index], HEAD_DIM // 2)
        normed, inverse_first = norm_forward(resid, attn_gain)
        normed_all = spread_normed(normed.astype(jnp.bfloat16))
        query = rotate(product(normed_all, query_full).reshape(heads_shape), cosine, sine).astype(
            jnp.bfloat16
        )
        keys = rotate(product(normed_all, key_full).reshape(heads_shape), cosine, sine).astype(
            jnp.bfloat16
        )
        values = product(normed_all, value_full).astype(jnp.bfloat16)
        query_seq = query.reshape(seq_shape)
        keys_seq = keys.reshape(seq_shape)
        values_seq = values.reshape(seq_shape)
        attended, logsum = lax.map(
            partial(attend_forward, bias_pair), (query_seq, keys_seq, values_seq, segment, variate)
        )
        attended = attended.reshape(group_rows, local_width)
        middle = resid + branch_rows(attended, out_full)
        normed_ffn, inverse_second = norm_forward(middle, ffn_gain)
        normed_ffn_all = spread_normed(normed_ffn.astype(jnp.bfloat16))
        gate = product(normed_ffn_all, gate_full)
        upward = product(normed_ffn_all, up_full)
        sigmoid = jax.nn.sigmoid(gate)
        hidden = (gate * sigmoid * upward).astype(jnp.bfloat16)
        outputs.append((middle + branch_rows(hidden, down_full)).astype(jnp.bfloat16))
        full_weights = (
            lax.all_gather(shards[0], "fsdp", axis=0, tiled=True),
            lax.all_gather(shards[1], "fsdp", axis=0, tiled=True),
            lax.all_gather(shards[2], "fsdp", axis=0, tiled=True),
            lax.all_gather(shards[3], "fsdp", axis=1, tiled=True),
            lax.all_gather(shards[4], "fsdp", axis=0, tiled=True),
            lax.all_gather(shards[5], "fsdp", axis=0, tiled=True),
            lax.all_gather(shards[6], "fsdp", axis=1, tiled=True),
        )
        query_full, key_full, value_full, out_full, gate_full, up_full, down_full = full_weights
        grad_out = cotangent[micro_index].astype(jnp.float32)
        grad_ffn_all = spread_grads(cotangent[micro_index])
        dhidden = product_back(grad_ffn_all, down_full)
        dgate = (dhidden * upward * (sigmoid + gate * sigmoid * (1.0 - sigmoid))).astype(
            jnp.bfloat16
        )
        dupward = (dhidden * gate * sigmoid).astype(jnp.bfloat16)
        dnormed_ffn = back_rows((dgate, dupward), (gate_full, up_full))
        grad_gate = outer_sum(normed_ffn_all, dgate)
        grad_up = outer_sum(normed_ffn_all, dupward)
        grad_down = outer_sum(hidden, grad_ffn_all)
        dmiddle, gain_term = norm_backward(middle, inverse_second, ffn_gain, dnormed_ffn)
        gain_second = gain_second + gain_term
        dmiddle = dmiddle + grad_out
        grad_attn_all = spread_grads(dmiddle.astype(jnp.bfloat16))
        dattended = product_back(grad_attn_all, out_full).astype(jnp.bfloat16)
        grad_out_proj = outer_sum(attended, grad_attn_all)
        back_items = (
            query_seq,
            keys_seq,
            values_seq,
            dattended.reshape(seq_shape),
            segment,
            variate,
            logsum,
        )
        dquery, dkeys, dvalues, bias_terms = lax.map(
            partial(attend_backward, bias_pair), back_items
        )
        bias_grad = bias_grad + jnp.sum(bias_terms, axis=0)
        dquery = (
            rotate_back(dquery.reshape(heads_shape), cosine, sine)
            .astype(jnp.bfloat16)
            .reshape(group_rows, local_width)
        )
        dkeys = (
            rotate_back(dkeys.reshape(heads_shape), cosine, sine)
            .astype(jnp.bfloat16)
            .reshape(group_rows, local_width)
        )
        dvalues = dvalues.astype(jnp.bfloat16).reshape(group_rows, local_width)
        dnormed = back_rows((dquery, dkeys, dvalues), (query_full, key_full, value_full))
        grad_query = outer_sum(normed_all, dquery)
        grad_key = outer_sum(normed_all, dkeys)
        grad_value = outer_sum(normed_all, dvalues)
        dresid, gain_term = norm_backward(resid, inverse_first, attn_gain, dnormed)
        gain_first = gain_first + gain_term
        input_grads.append((dresid + dmiddle).astype(jnp.bfloat16))
        summed = (
            lax.psum_scatter(
                grad_query.astype(jnp.bfloat16), "fsdp", scatter_dimension=0, tiled=True
            ).astype(jnp.float32),
            lax.psum_scatter(
                grad_key.astype(jnp.bfloat16), "fsdp", scatter_dimension=0, tiled=True
            ).astype(jnp.float32),
            lax.psum_scatter(
                grad_value.astype(jnp.bfloat16), "fsdp", scatter_dimension=0, tiled=True
            ).astype(jnp.float32),
            lax.psum_scatter(
                grad_out_proj.astype(jnp.bfloat16), "fsdp", scatter_dimension=1, tiled=True
            ).astype(jnp.float32),
            lax.psum_scatter(
                grad_gate.astype(jnp.bfloat16), "fsdp", scatter_dimension=0, tiled=True
            ).astype(jnp.float32),
            lax.psum_scatter(
                grad_up.astype(jnp.bfloat16), "fsdp", scatter_dimension=0, tiled=True
            ).astype(jnp.float32),
            lax.psum_scatter(
                grad_down.astype(jnp.bfloat16), "fsdp", scatter_dimension=1, tiled=True
            ).astype(jnp.float32),
        )
        grad_shards = summed if grad_shards is None else jax.tree.map(jnp.add, grad_shards, summed)
    bias_full = lax.dynamic_update_slice_in_dim(
        jnp.zeros((2, head_bias.shape[1]), jnp.float32), bias_grad, head_start, 1
    )
    gain_first, gain_second, bias_full = lax.psum(
        (gain_first, gain_second, bias_full), ("fsdp", "tensor")
    )
    return (
        jnp.stack(outputs),
        jnp.stack(input_grads),
        gain_first,
        grad_shards[0],
        grad_shards[1],
        grad_shards[2],
        bias_full,
        grad_shards[3],
        gain_second,
        grad_shards[4],
        grad_shards[5],
        grad_shards[6],
    )


BF = jnp.bfloat16
F32 = jnp.float32
MESH = pl.DeviceIdType.MESH
SHARD = 64
SEQ_LEN = 256
HALF = 128
WIDTH = 1024
LOCAL = 512
HIDDEN = 2048
PAIRS = 4
COL_QKV, COL_OUT, COL_GATE, COL_UP, COL_DOWN = 0, 1536, 2048, 4096, 6144
ALL_COLS = 8192
LOAD_COLS = (0, 512, 1024, COL_OUT, COL_GATE, COL_UP, COL_DOWN)
LOAD_ENDS = LOAD_COLS[1:] + (ALL_COLS,)
GATHER = (
    (0, 512, False, False, True),
    (512, 512, False, False, True),
    (1024, 512, False, False, True),
    (1536, 512, False, False, False),
    (2048, 512, False, False, False),
    (2560, 512, False, False, False),
    (3072, 512, False, False, False),
    (3584, 512, False, False, False),
    (4096, 512, False, False, False),
    (4608, 512, False, False, False),
    (5120, 512, False, False, False),
    (5632, 512, False, False, False),
    (6144, 512, True, False, False),
    (6656, 512, True, False, False),
    (7168, 512, True, False, False),
    (7680, 512, True, False, False),
)
CHUNK = 2048
SCATTER = (
    (0, 0, 512, False, False, False),
    (0, 512, 512, False, False, False),
    (0, 1024, 512, False, False, False),
    (0, 1536, 512, False, False, False),
    (1, 0, 512, False, False, False),
    (1, 512, 512, False, False, False),
    (1, 1024, 512, False, False, False),
    (1, 1536, 512, True, False, False),
    (2, 0, 512, False, False, True),
    (2, 512, 512, False, False, True),
    (2, 1024, 512, False, False, True),
    (2, 1536, 512, False, False, True),
    (3, 0, 512, False, False, True),
    (3, 512, 512, False, False, True),
    (3, 1024, 512, False, False, True),
    (3, 1536, 512, False, True, True),
)
NORMAL_COLS = sum(piece[2] for piece in SCATTER if not piece[3])
TURNED_COLS = max(128, sum(piece[2] for piece in SCATTER if piece[3]))
FIRST = 4
DEPTH = 4
(
    START,
    TABLES,
    NORM,
    PROJECT,
    ATTEND,
    PROJECT_OUT,
    MIDDLE,
    GATE_TILES,
    UP_TILES,
    TURN_COTANGENT,
    TURN_FFN,
    TURN_NORMED,
    TURN_MIDDLE,
    HIDDEN_BACK,
    LAST_PRODUCT,
    GATHER_SENT,
    FFN_BACK,
    OUT_SEND,
    MIDDLE_BACK,
    ATTEND_BACK,
    NORM_BACK,
    OUT_ROWS,
    TOKEN_ROWS,
    SUM_START,
    SUM_STAGE,
    GATHER_Z,
    GATHER_CORE,
    WEIGHT_GRAD,
    SCATTER_X,
    SCATTER_Z,
    SCATTER_PASS,
    SCATTER_END,
    TURNED_X,
    TURNED_END,
    SCATTER_OWN,
) = range(35)
PROGRAM = (
    (START, 0),
    (GATHER_Z, 0),
    (GATHER_Z, 1),
    (GATHER_Z, 2),
    (NORM, 0),
    (GATHER_CORE, 0),
    (TABLES, 0),
    (GATHER_Z, 3),
    (GATHER_CORE, 1),
    (PROJECT, 0),
    (PROJECT, 1),
    (GATHER_CORE, 2),
    (GATHER_Z, 4),
    (GATHER_Z, 5),
    (PROJECT, 2),
    (ATTEND, 0),
    (GATHER_CORE, 3),
    (PROJECT_OUT, 0),
    (GATHER_Z, 6),
    (ATTEND, 1),
    (TURN_COTANGENT, 0),
    (GATHER_Z, 7),
    (PROJECT_OUT, 1),
    (GATHER_CORE, 4),
    (GATHER_Z, 8),
    (GATHER_CORE, 5),
    (GATHER_Z, 9),
    (GATHER_Z, 10),
    (GATHER_CORE, 6),
    (GATHER_CORE, 7),
    (GATHER_Z, 11),
    (MIDDLE, 0),
    (MIDDLE, 1),
    (TURN_FFN, 0),
    (GATHER_CORE, 8),
    (GATE_TILES, 0),
    (GATHER_CORE, 9),
    (GATHER_Z, 12),
    (UP_TILES, 0),
    (WEIGHT_GRAD, 0),
    (WEIGHT_GRAD, 1),
    (GATHER_Z, 13),
    (SCATTER_X, 1),
    (GATE_TILES, 1),
    (GATHER_CORE, 10),
    (HIDDEN_BACK, 0),
    (GATHER_CORE, 11),
    (GATHER_Z, 14),
    (SCATTER_X, 0),
    (UP_TILES, 1),
    (WEIGHT_GRAD, 2),
    (WEIGHT_GRAD, 3),
    (GATHER_Z, 15),
    (SCATTER_X, 3),
    (SCATTER_X, 2),
    (GATHER_SENT, 0),
    (SCATTER_Z, 1),
    (HIDDEN_BACK, 1),
    (SCATTER_Z, 0),
    (FFN_BACK, 0),
    (FFN_BACK, 1),
    (SCATTER_Z, 3),
    (WEIGHT_GRAD, 9),
    (LAST_PRODUCT, 0),
    (SCATTER_PASS, 1),
    (SCATTER_X, 9),
    (WEIGHT_GRAD, 7),
    (SCATTER_Z, 2),
    (WEIGHT_GRAD, 10),
    (SCATTER_X, 7),
    (WEIGHT_GRAD, 5),
    (SCATTER_PASS, 0),
    (SCATTER_X, 10),
    (WEIGHT_GRAD, 6),
    (WEIGHT_GRAD, 11),
    (SCATTER_X, 6),
    (WEIGHT_GRAD, 8),
    (SCATTER_X, 11),
    (WEIGHT_GRAD, 4),
    (SCATTER_Z, 10),
    (SCATTER_Z, 9),
    (MIDDLE_BACK, 0),
    (SCATTER_X, 5),
    (OUT_SEND, 0),
    (SCATTER_PASS, 2),
    (ATTEND_BACK, 0),
    (SCATTER_OWN, 11),
    (MIDDLE_BACK, 1),
    (SCATTER_PASS, 3),
    (SCATTER_Z, 11),
    (NORM_BACK, 0),
    (TURN_MIDDLE, 0),
    (SCATTER_X, 8),
    (SCATTER_Z, 6),
    (SCATTER_PASS, 7),
    (ATTEND_BACK, 1),
    (SCATTER_X, 4),
    (SCATTER_Z, 5),
    (TURN_NORMED, 0),
    (NORM_BACK, 1),
    (SCATTER_PASS, 10),
    (WEIGHT_GRAD, 12),
    (SCATTER_OWN, 9),
    (SCATTER_X, 12),
    (SCATTER_END, 2),
    (SCATTER_Z, 8),
    (WEIGHT_GRAD, 14),
    (SCATTER_PASS, 9),
    (SCATTER_OWN, 10),
    (WEIGHT_GRAD, 15),
    (OUT_ROWS, 0),
    (SCATTER_Z, 4),
    (SCATTER_PASS, 11),
    (TOKEN_ROWS, 0),
    (TOKEN_ROWS, 1),
    (SUM_START, 0),
    (SCATTER_X, 14),
    (WEIGHT_GRAD, 13),
    (SCATTER_Z, 12),
    (SCATTER_PASS, 6),
    (SCATTER_X, 13),
    (SCATTER_PASS, 5),
    (SUM_STAGE, 0),
    (SCATTER_X, 15),
    (SUM_STAGE, 1),
    (SCATTER_END, 5),
    (SCATTER_END, 1),
    (SCATTER_END, 0),
    (SCATTER_END, 10),
    (SCATTER_OWN, 15),
    (SCATTER_PASS, 8),
    (SCATTER_Z, 14),
    (SCATTER_Z, 13),
    (SCATTER_PASS, 4),
    (SCATTER_OWN, 8),
    (SCATTER_END, 3),
    (SCATTER_Z, 15),
    (SCATTER_PASS, 14),
    (TURNED_X, 7),
    (SCATTER_OWN, 12),
    (SCATTER_PASS, 12),
    (SCATTER_END, 8),
    (SCATTER_OWN, 14),
    (SUM_STAGE, 2),
    (SCATTER_END, 9),
    (SCATTER_PASS, 15),
    (SCATTER_OWN, 13),
    (SCATTER_END, 12),
    (SCATTER_END, 4),
    (SCATTER_END, 11),
    (SCATTER_END, 14),
    (TURNED_END, 7),
    (SUM_STAGE, 3),
    (SCATTER_END, 6),
    (SCATTER_PASS, 13),
    (SCATTER_END, 15),
    (SCATTER_END, 13),
)
WEIGHT_ORDER = [p for step, p in PROGRAM if step == WEIGHT_GRAD]
CORE_ORDER = [p for step, p in PROGRAM if step == SCATTER_X]
FIRST_QUERY = [p for p in WEIGHT_ORDER if SCATTER[p][0] == 3][0]
LAST_DOWN = [p for p in CORE_ORDER if SCATTER[p][0] == 0][-1]
PARTS = 1
NEGATIVE = -1e30


def mm(left, right):
    return jnp.dot(left, right, preferred_element_type=F32)


def mm_nt(left, right):
    return lax.dot_general(left, right, (((1,), (1,)), ((), ())), preferred_element_type=F32)


def mm_tn(left, right):
    return lax.dot_general(left, right, (((0,), (0,)), ((), ())), preferred_element_type=F32)


def layer_kernel(
    tok_ref,
    cot_in,
    seg_ref,
    var_ref,
    time_ref,
    again_ref,
    fgain_ref,
    freq_ref,
    bias_ref,
    wq_ref,
    wk_ref,
    wv_ref,
    wo_ref,
    wg_ref,
    wu_ref,
    wd_ref,
    out_hbm,
    tgrad_hbm,
    gqkvo_hbm,
    gg_hbm,
    gu_hbm,
    gd_hbm,
    ga_ref,
    gf_ref,
    gb_ref,
    out_ref,
    tgrad_ref,
    RES,
    W,
    GD,
    RC,
    RX,
    RZ,
    RL,
    RXS,
    RZS,
    RLS,
    X,
    COT,
    N1,
    NF,
    Q,
    K,
    V,
    ATT,
    PT,
    MID,
    GT,
    UP,
    HID,
    YS,
    YR,
    YDS,
    YDR,
    YNR,
    T,
    T2,
    OUTM,
    DML,
    SAME,
    NEGM,
    COS,
    SIN,
    GF,
    GA,
    BS,
    SV,
    SR,
    local_sem,
    ag_send,
    ag_recv,
    rs_send,
    rs_recv,
    y_send,
    y_recv,
    sv_send,
    sv_recv,
    credit,
    core_credit,
    flush_sem,
):
    f = lax.axis_index("fsdp")
    y = lax.axis_index("tensor")
    z, x, c = f // 4, (f // 2) % 2, f % 2
    zs = (z + 1 - 2 * (z % 2), (z + 2) % 4, 3 - z)
    z_devs = [(zk * 4 + x * 2 + c, y) for zk in zs]
    x_dev = (z * 4 + (1 - x) * 2 + c, y)
    c_dev = (z * 4 + x * 2 + 1 - c, y)
    y_dev = (f, 1 - y)
    partners = z_devs + [x_dev, c_dev, y_dev]

    def remote(src, dst, send, recv, dev):
        return pltpu.make_async_remote_copy(
            src_ref=src, dst_ref=dst, send_sem=send, recv_sem=recv, device_id=dev, device_id_type=MESH
        )

    barrier = pltpu.get_barrier_semaphore()
    for dev in partners:
        pl.semaphore_signal(barrier, inc=1, device_id=dev, device_id_type=MESH)
    own_rows = pl.ds(pl.multiple_of(y * HALF, HALF), HALF)
    other_rows = pl.ds(pl.multiple_of((1 - y) * HALF, HALF), HALF)
    loads = [
        (tok_ref, X.at[:, own_rows]),
        (cot_in, COT.at[:, own_rows]),
        (wq_ref, W.at[z, x, c, :, pl.ds(0, LOCAL)]),
        (wk_ref, W.at[z, x, c, :, pl.ds(LOCAL, LOCAL)]),
        (wv_ref, W.at[z, x, c, :, pl.ds(2 * LOCAL, LOCAL)]),
        (wo_ref, W.at[z, x, c, :, pl.ds(COL_OUT, LOCAL)]),
        (wg_ref, W.at[z, x, c, :, pl.ds(COL_GATE, HIDDEN)]),
        (wu_ref, W.at[z, x, c, :, pl.ds(COL_UP, HIDDEN)]),
        (wd_ref, W.at[z, x, c, :, pl.ds(COL_DOWN, HIDDEN)]),
    ]
    loads = [
        pltpu.make_async_copy(src, dst, local_sem.at[i]) for i, (src, dst) in enumerate(loads)
    ]
    for load in loads:
        load.start()
    loaded = set()

    def load_wait(*which):
        for i in which:
            if i not in loaded:
                loaded.add(i)
                loads[i].wait()

    pl.semaphore_wait(barrier, len(partners))
    middle = ((z + 1) // 2) % 2 == 1
    edge = ((z + 1) // 2) % 2 == 0

    ag_own, ag_pass, ag_x, ag_c = [], [], [], []
    for i, (c0, n, turned, straight, early) in enumerate(GATHER):
        cols = pl.ds(c0, n)

        def block(zi):
            if turned:
                return W.at[zi, :, c, :, cols]
            return W.at[zi, x, c, :, cols]

        at = i * 9
        ag_own.append(
            [
                remote(block(z), block(z), ag_send.at[at + k], ag_recv.at[at + k], z_devs[k])
                for k in range(3)
            ]
        )
        ag_pass.append(
            [
                remote(
                    block(zs[k]),
                    block(zs[k]),
                    ag_send.at[at + (0, 3, 1)[k]],
                    ag_recv.at[at + 3 - k],
                    z_devs[0],
                )
                for k in (1, 2)
            ]
        )
        part = W.at[z, x, c, :, cols] if turned else W.at[:, x, c, :, cols]
        if early:
            parts = [block(zi) for zi in (z, *zs)]
        else:
            parts = [part]
        ag_x.append(
            [
                remote(part, part, ag_send.at[at + k], ag_recv.at[at + k], x_dev)
                for k, part in zip((4, 6, 7, 8), parts)
            ]
        )
        part = W.at[:, :, c, :, cols]
        ag_c.append(remote(part, part, ag_send.at[at + 5], ag_recv.at[at + 5], c_dev))

    def own_load(i):
        c0, n = GATHER[i][:2]
        for k, base in enumerate(LOAD_COLS):
            if base < c0 + n and c0 < LOAD_ENDS[k]:
                load_wait(2 + k)

    def gather_own(i):
        own_load(i)
        if GATHER[i][2]:
            ag_x[i][0].wait_recv()
        ag_own[i][0].start()
        if GATHER[i][3]:
            ag_own[i][1].start()
            ag_own[i][2].start()
            return

        @pl.when(edge)
        def _():
            ag_own[i][1].start()

        @pl.when(middle)
        def _():
            ag_own[i][2].start()

    def gather_z(i):
        if GATHER[i][3]:
            ag_own[i][1].wait_recv()
        else:

            @pl.when(middle)
            def _():
                for k in (1, 2):
                    ag_own[i][k].wait_recv()
                    ag_pass[i][k - 1].start()

        for k in range(max(FIRST, i + DEPTH if i else FIRST), min(i + DEPTH + 1, len(GATHER))):
            gather_own(k)
        ag_own[i][0].wait_recv()
        if GATHER[i][3]:
            ag_own[i][2].wait_recv()
        else:

            @pl.when(edge)
            def _():
                ag_own[i][1].wait_recv()
                ag_own[i][2].wait_recv()

        if GATHER[i][2]:
            ag_c[i].start()
        else:
            for copy in ag_x[i][1 if GATHER[i][4] else 0 :]:
                copy.start()

    def gather_c(i):
        for copy in ag_x[i]:
            copy.wait_recv()
        ag_c[i].start()

    ended = set()

    def gather_end(c0, n):
        for i, (start_col, size, *_) in enumerate(GATHER):
            if start_col < c0 + n and c0 < start_col + size and i not in ended:
                ended.add(i)
                ag_c[i].wait_recv()

    y_tok = remote(X.at[:, own_rows], X.at[:, own_rows], y_send.at[0], y_recv.at[0], y_dev)
    y_cot = remote(COT.at[:, own_rows], COT.at[:, own_rows], y_send.at[1], y_recv.at[1], y_dev)

    def start():
        load_wait(0)
        y_tok.start()
        for i in range(FIRST):
            gather_own(i)
        for i in range(len(GATHER)):
            if GATHER[i][2] or GATHER[i][4]:
                own_load(i)
                ag_x[i][0].start()
        load_wait(1)
        y_cot.start()

        @pl.when(edge)
        def _():
            for p, (_, _, n, turned, straight, _) in enumerate(SCATTER):
                spot = sum(piece[2] for piece in SCATTER[:p] if piece[3] == turned)
                if turned and not straight:
                    RZS[2, :, :, pl.ds(spot, n)] = jnp.zeros((2, SHARD, n), BF)
                elif not straight:
                    RZ[2, :, pl.ds(spot, n)] = jnp.zeros((SHARD, n), BF)

    lane = lax.broadcasted_iota(jnp.int32, (1, 128), 1)
    low_lane = lane < 64
    lead_lane = (lane % 64) < 32

    def column(row):
        return jnp.transpose(jnp.broadcast_to(row.astype(F32), (128, SEQ_LEN)))

    def tables():
        for s in range(2):
            moments = column(time_ref[s : s + 1, :])
            angles = moments * freq_ref[...]
            COS[s] = jnp.cos(angles)
            sine = jnp.sin(angles)
            SIN[s] = jnp.where(lead_lane, -sine, sine)
            seg_row = seg_ref[s : s + 1, :].astype(F32)
            var_row = var_ref[s : s + 1, :].astype(F32)
            seg_col = column(seg_ref[s : s + 1, :])
            var_col = column(var_ref[s : s + 1, :])
            for h in range(2):
                part = slice(h * 128, (h + 1) * 128)
                SAME[s, :, part] = jnp.where(var_col == var_row[:, part], 1.0, 0.0)
                NEGM[s, :, part] = jnp.where(seg_col == seg_row[:, part], 0.0, NEGATIVE)

    def swap(values):
        return jnp.where(
            lead_lane, pltpu.roll(values, 96, axis=1), pltpu.roll(values, 32, axis=1)
        )

    ROWS = 64
    BLOCKS = SEQ_LEN // ROWS

    def row_loop(body):
        def step(b, carry):
            body(b, pl.ds(pl.multiple_of(b * ROWS, ROWS), ROWS))
            return carry

        lax.fori_loop(0, BLOCKS, step, 0)

    def tile_loop(count, body):
        def step(j, carry):
            body(j)
            return carry

        lax.fori_loop(0, count, step, 0)

    def tile_cols(base, j, size=256):
        return pl.ds(pl.multiple_of(base + j * size, size), size)

    def w_tile(cols):
        return W[:, :, :, :, cols].reshape(WIDTH, 256)

    def w_rows(zi, c0, n):
        return W[zi, :, :, :, pl.ds(c0, n)].reshape(256, n)

    def transpose_into(src, T):
        for s in range(2):

            def body(j):
                cols = tile_cols(0, j)
                T[cols, s * SEQ_LEN : (s + 1) * SEQ_LEN] = jnp.transpose(src[s, :, cols])

            tile_loop(4, body)

    def norm():
        y_tok.wait_recv()
        for s in range(2):

            def body(b, rows):
                v = X[s, rows, :].astype(F32)
                inv = lax.rsqrt(jnp.mean(v * v, axis=-1, keepdims=True) + EPS)
                N1[s, rows, :] = (v * inv * again_ref[...]).astype(BF)

            row_loop(body)

    def project(kind):
        gather_end(kind * LOCAL, LOCAL)
        dest = (Q, K, V)[kind]

        def body(j):
            r = mm(N1[...].reshape(2 * SEQ_LEN, WIDTH), w_tile(tile_cols(kind * LOCAL, j)))
            for h in range(2):
                part = r[:, h * 128 : (h + 1) * 128]
                if kind < 2:
                    cosine = COS[...].reshape(2 * SEQ_LEN, 128)
                    sine = SIN[...].reshape(2 * SEQ_LEN, 128)
                    part = part * cosine + swap(part) * sine
                dest[:, :, pl.ds(pl.multiple_of(j * 256 + h * 128, 128), 128)] = part.astype(
                    BF
                ).reshape(2, SEQ_LEN, 128)

        tile_loop(2, body)

    def stacked(values):
        zero = jnp.zeros_like(values)
        return jnp.concatenate(
            [jnp.where(low_lane, values, zero), jnp.where(low_lane, zero, values)], axis=0
        )

    def pair_cols(p):
        return pl.ds(pl.multiple_of(p * 128, 128), 128)

    y_att = [
        remote(YS.at[s], YR.at[s], y_send.at[2 + s], y_recv.at[2 + s], y_dev) for s in range(2)
    ]
    def attend(s):
        def body(p):
            cols = pair_cols(p)
            keys = stacked(K[s, :, cols] * jnp.asarray(0.125, BF))
            scores = mm_nt(keys, Q[s, :, cols])
            parts = []
            for h in range(2):
                head = y * 8 + p * 2 + h
                same_bias = bias_ref[0, head]
                other_bias = bias_ref[1, head]
                sc = scores[h * SEQ_LEN : (h + 1) * SEQ_LEN]
                sc = sc + (SAME[s] * (same_bias - other_bias) + (NEGM[s] + other_bias))
                top = jnp.max(sc, axis=0, keepdims=True)
                expo = jnp.exp(sc - top)
                total = jnp.sum(expo, axis=0, keepdims=True)
                parts.append((expo * (1.0 / total)).astype(BF))
            probs = jnp.concatenate(parts, axis=0)
            PT[s * PAIRS + p] = probs
            ATT[s, :, cols] = mm_tn(probs, stacked(V[s, :, cols])).astype(BF)

        tile_loop(PAIRS, body)

    def project_out(s):
        if s == 0:
            gather_end(COL_OUT, LOCAL)
        for zi in range(4):
            YS[s, :, zi * 256 : (zi + 1) * 256] = mm_nt(
                ATT[s], w_rows(zi, COL_OUT, LOCAL)
            ).astype(BF)
        y_att[s].start()

    def middle_rows(s):
        y_att[s].wait_recv()

        def body(b, rows):
            v = X[s, rows, :].astype(F32) + (YS[s, rows, :].astype(F32) + YR[s, rows, :].astype(F32))
            MID[s, rows, :] = v
            inv = lax.rsqrt(jnp.mean(v * v, axis=-1, keepdims=True) + EPS)
            NF[s, rows, :] = (v * inv * fgain_ref[...]).astype(BF)

        row_loop(body)
        if s == 1:
            for k in range(2):
                y_att[k].wait_send()
            pl.semaphore_signal(credit, inc=1, device_id=y_dev, device_id_type=MESH)

    def gate_tiles(half):
        gather_end(COL_GATE + half * 1024, 1024)

        def body(j):
            cols = tile_cols(half * 1024, j)
            GT[:, cols] = mm(
                NF[...].reshape(2 * SEQ_LEN, WIDTH), w_tile(tile_cols(COL_GATE + half * 1024, j))
            ).astype(BF)

        tile_loop(4, body)

    def up_tiles(half):
        gather_end(COL_UP + half * 1024, 1024)

        def body(j):
            cols = tile_cols(half * 1024, j)
            up = mm(
                NF[...].reshape(2 * SEQ_LEN, WIDTH), w_tile(tile_cols(COL_UP + half * 1024, j))
            )
            UP[:, cols] = up.astype(BF)
            gate = GT[:, cols].astype(F32)
            HID[:, cols] = (gate * jax.nn.sigmoid(gate) * up).astype(BF)

        tile_loop(4, body)

    def turn_cotangent():
        y_cot.wait_recv()
        transpose_into(COT, T)

    homes = ((GD, 0), (W, COL_DOWN), (W, COL_GATE), (W, COL_UP))
    results = tuple(RES.at[ch] for ch in range(4))
    result_homes = (gd_hbm, gg_hbm, gu_hbm, gqkvo_hbm)
    flushes = []

    def flush(src, dst):
        copy = pltpu.make_async_copy(src, dst, flush_sem.at[len(flushes)])
        copy.start()
        flushes.append(copy)

    def flush_result(p):
        ch, c0, n = SCATTER[p][:3]
        cols = pl.ds(c0, n)
        flush(results[ch].at[:, cols], result_homes[ch].at[:, cols])


    def home(ch, *index, c0=0, n=CHUNK):
        ref, base = homes[ch]
        return ref.at[index + (slice(None), pl.ds(base + c0, n))]

    every = slice(None)
    slots = (0, 1, 2, 0)
    rs_c, rs_x, rs_z, rs_relay = [], [], [], []
    spots = []
    for p, (ch, c0, n, turned, straight, late) in enumerate(SCATTER):
        spot = sum(piece[2] for piece in SCATTER[:p] if piece[3] == turned)
        spots.append(spot)
        at = p * 9

        def sems(k):
            return rs_send.at[at + k], rs_recv.at[at + k]

        rs_c.append(
            remote(
                home(ch, every, every, 1 - c, c0=c0, n=n),
                RC.at[slots[ch], :, :, :, pl.ds(c0, n)],
                *sems(0),
                c_dev,
            )
        )
        cols = pl.ds(spot, n)
        if turned:
            rs_x.append(
                [remote(home(ch, z, 1 - x, c, c0=c0, n=n), RXS.at[:, cols], *sems(1), x_dev)]
            )
            views = [home(ch, zk, every, c, c0=c0, n=n) for zk in zs]
            boxes, relay = [RZS.at[k, :, :, cols] for k in range(3)], RLS.at[:, :, cols]
        else:
            blocks = (*zs, z) if late else (every,)
            rs_x.append(
                [
                    remote(
                        home(ch, zi, 1 - x, c, c0=c0, n=n), RX.at[zi, :, cols], *sems(k), x_dev
                    )
                    for k, zi in zip((1, 6, 7, 8), blocks)
                ]
            )
            views = [home(ch, zk, x, c, c0=c0, n=n) for zk in zs]
            boxes, relay = [RZ.at[k, :, cols] for k in range(3)], RL.at[:, cols]
        rs_z.append(
            [remote(views[k], boxes[k], *sems(2 + k), z_devs[k]) for k in range(3)]
        )
        rs_relay.append(remote(views[2], relay, *sems(5), z_devs[0]))

    def add_core(p, xi):
        ch, c0, n, turned, straight, late = SCATTER[p]

        def body(zi):
            view = home(ch, zi, xi, c, c0=c0, n=n)
            view[...] = view[...] + RC[slots[ch], zi, xi, :, pl.ds(c0, n)]

        tile_loop(4, body)

    def send_z(p):
        rs_z[p][0].start()
        if SCATTER[p][4]:
            rs_z[p][1].start()
            rs_z[p][2].start()
            return

        @pl.when(middle)
        def _():
            rs_z[p][2].start()

        @pl.when(edge)
        def _():
            rs_z[p][1].start()
            rs_relay[p].start()

    def scatter_x(p):
        rs_c[p].wait_recv()
        add_core(p, 1 - x)
        if SCATTER[p][3]:
            add_core(p, x)
            send_z(p)
        else:
            for copy in rs_x[p][:3]:
                copy.start()
            add_core(p, x)
        if p == LAST_DOWN:
            pl.semaphore_signal(core_credit, inc=1, device_id=c_dev, device_id_type=MESH)

    def scatter_z(p):
        ch, c0, n, turned, straight, late = SCATTER[p]
        for copy in rs_x[p][:3]:
            copy.wait_recv()

        def body(zi):
            view = home(ch, zi, x, c, c0=c0, n=n)
            view[...] = view[...] + RX[zi, :, pl.ds(spots[p], n)]

        if late:
            for zi in zs:
                body(zi)
        else:
            tile_loop(4, body)
        send_z(p)

    def scatter_own(p):
        rs_x[p][3].start()

    def scatter_pass(p):
        ch, c0, n, turned, straight, late = SCATTER[p]
        if straight:
            return

        @pl.when(middle)
        def _():
            rs_relay[p].wait_recv()
            if turned:
                view = home(ch, zs[1], every, c, c0=c0, n=n)
                view[...] = view[...] + RLS[:, :, pl.ds(spots[p], n)]
            else:
                view = home(ch, zs[1], x, c, c0=c0, n=n)
                view[...] = view[...] + RL[:, pl.ds(spots[p], n)]
            rs_z[p][1].start()

    def wait_z(p):
        rs_z[p][0].wait_recv()
        rs_z[p][1].wait_recv()
        if SCATTER[p][4]:
            rs_z[p][2].wait_recv()
            return

        @pl.when(middle)
        def _():
            rs_z[p][2].wait_recv()

    def scatter_end(p):
        ch, c0, n, turned, straight, late = SCATTER[p]
        wait_z(p)
        if late:
            rs_x[p][3].wait_recv()

        def body(j):
            total = home(ch, z, x, c)[:, tile_cols(c0, j)].astype(F32)
            if late:
                total = total + RX[z, :, tile_cols(spots[p], j)].astype(F32)
            for k in range(3):
                total = total + RZ[k, :, tile_cols(spots[p], j)].astype(F32)
            results[ch][:, tile_cols(c0, j)] = total

        tile_loop(n // 256, body)
        flush_result(p)

    def turned_x(p):
        ch, c0, n, turned, straight, late = SCATTER[p]
        wait_z(p)
        for xi in range(2):
            view = home(ch, z, xi, c, c0=c0, n=n)
            total = view[...].astype(F32)
            for k in range(3):
                total = total + RZS[k, xi, :, pl.ds(spots[p], n)].astype(F32)
            view[...] = total.astype(BF)
        rs_x[p][0].start()

    def turned_end(p):
        ch, c0, n, turned, straight, late = SCATTER[p]
        rs_x[p][0].wait_recv()
        own = home(ch, z, x, c, c0=c0, n=n)[...].astype(F32)
        results[ch][:, c0 : c0 + n] = own + RXS[:, pl.ds(spots[p], n)].astype(F32)
        flush_result(p)

    def weight_tiles(ch, c0, n):
        ref, base = homes[ch]

        def body(j):
            cols = tile_cols(c0, j)
            if ch == 0:
                left, right = T, HID[:, cols]
            elif ch == 1:
                left, right = T2, GT[:, cols]
            elif ch == 2:
                left, right = T2, UP[:, cols]
            elif c0 < 3 * LOCAL:
                left, right = T2, DQKV[:, cols]
            else:
                left, right = T, ATT[:, :, tile_cols(c0 - 3 * LOCAL, j)].reshape(2 * SEQ_LEN, 256)
            r = mm(left[...], right)
            ref[:, :, :, :, tile_cols(base + c0, j)] = r.astype(BF).reshape(4, 2, 2, SHARD, 256)

        tile_loop(n // 256, body)

    def weight_grad(p):
        ch, c0, n, turned, straight, late = SCATTER[p]
        if p == FIRST_QUERY:
            pl.semaphore_wait(core_credit, 1)
        if ch == 3 and c0 < 3 * LOCAL < c0 + n:
            weight_tiles(ch, c0, 3 * LOCAL - c0)
            weight_tiles(ch, 3 * LOCAL, c0 + n - 3 * LOCAL)
        else:
            weight_tiles(ch, c0, n)
        rs_c[p].start()

    def hidden_back(half):
        gather_end(COL_DOWN + half * 1024, 1024)

        def body(j):
            cols = tile_cols(half * 1024, j)
            dhid = mm(
                COT[...].reshape(2 * SEQ_LEN, WIDTH), w_tile(tile_cols(COL_DOWN + half * 1024, j))
            )
            gate = GT[:, cols].astype(F32)
            up = UP[:, cols].astype(F32)
            sig = jax.nn.sigmoid(gate)
            GT[:, cols] = (dhid * up * (sig + gate * sig * (1.0 - sig))).astype(BF)
            UP[:, cols] = (dhid * gate * sig).astype(BF)

        tile_loop(4, body)

    def gather_sent():
        for i in range(len(GATHER)):
            ag_own[i][0].wait_send()
            for copy in ag_x[i]:
                copy.wait_send()
            ag_c[i].wait_send()
            if GATHER[i][3]:
                ag_own[i][1].wait_send()
                ag_own[i][2].wait_send()
                continue

            @pl.when(edge)
            def _():
                ag_own[i][1].wait_send()

            @pl.when(middle)
            def _():
                ag_own[i][2].wait_send()
                for copy in ag_pass[i]:
                    copy.wait_send()

    def last_product():
        def body(zi):
            cols = tile_cols(0, zi)
            r = mm_nt(HID[...], w_rows(zi, COL_DOWN, HIDDEN)).reshape(2, 2, HALF, 256)
            mine = jnp.where(y == 0, r[:, 0], r[:, 1])
            OUTM[:, :, cols] = MID[:, own_rows, cols] + mine
            YDS[:, :, cols] = jnp.where(y == 0, r[:, 1], r[:, 0]).astype(BF)

        tile_loop(4, body)

    y_dnf = [
        remote(YS.at[s], YR.at[s], y_send.at[4 + s], y_recv.at[4 + s], y_dev) for s in range(2)
    ]
    y_out = remote(YDS, YDR, y_send.at[6], y_recv.at[6], y_dev)

    def ffn_back(s):
        if s == 0:
            pl.semaphore_wait(credit, 1)
        rows = slice(s * SEQ_LEN, (s + 1) * SEQ_LEN)

        def body(zi):
            r = mm_nt(GT[rows, :], w_rows(zi, COL_GATE, HIDDEN))
            r = r + mm_nt(UP[rows, :], w_rows(zi, COL_UP, HIDDEN))
            YS[s, :, tile_cols(0, zi)] = r.astype(BF)

        tile_loop(4, body)
        y_dnf[s].start()

    DAT = HID.at[:, 3 * LOCAL : 4 * LOCAL]
    DQKV = HID

    def middle_back(s):
        if s == 0:
            GF[...] = jnp.zeros_like(GF)
            GA[...] = jnp.zeros_like(GA)
        y_dnf[s].wait_recv()

        def body(b, rows):
            v = MID[s, rows, :]
            inv = lax.rsqrt(jnp.mean(v * v, axis=-1, keepdims=True) + EPS)
            scaled = v * inv
            dn = YS[s, rows, :].astype(F32) + YR[s, rows, :].astype(F32)
            flag = jnp.where(b // (HALF // ROWS) == y, 1.0, 0.0)
            GF[...] += flag * jnp.sum((dn * scaled).reshape(ROWS // 8, 8, WIDTH), axis=0)
            u = dn * fgain_ref[...]
            dm = COT[s, rows, :].astype(F32) + inv * (
                u - scaled * jnp.mean(u * scaled, axis=-1, keepdims=True)
            )
            MID[s, rows, :] = dm
            DML[s, rows, :] = dm.astype(BF)

        row_loop(body)
        seq_rows = slice(s * SEQ_LEN, (s + 1) * SEQ_LEN)

        def body(j):
            DAT[seq_rows, tile_cols(0, j)] = mm(DML[s], w_tile(tile_cols(COL_OUT, j))).astype(BF)

        tile_loop(2, body)

    def attend_back(s):
        seq_rows = slice(s * SEQ_LEN, (s + 1) * SEQ_LEN)

        def body(p):
            cols = pair_cols(p)
            do = DAT[seq_rows, cols]
            dprobs = mm_nt(stacked(V[s, :, cols]), do)
            probs_low = PT[s * PAIRS + p]
            parts = []
            for h in range(2):
                part = slice(h * SEQ_LEN, (h + 1) * SEQ_LEN)
                pr = probs_low[part].astype(F32)
                dp = dprobs[part]
                dot = jnp.sum(pr * dp, axis=0, keepdims=True)
                ds = (pr * (dp - dot)).astype(BF)
                wide = ds.astype(F32)
                same = wide * SAME[s]
                same_sum = jnp.sum(same, axis=0, keepdims=True)
                other_sum = jnp.sum(wide - same, axis=0, keepdims=True)
                if s == 0:
                    BS[0, p * 2 + h] = same_sum
                    BS[1, p * 2 + h] = other_sum
                else:
                    BS[0, p * 2 + h] += same_sum
                    BS[1, p * 2 + h] += other_sum
                parts.append(ds)
            dsc = jnp.concatenate(parts, axis=0)
            dv = mm(probs_low, do)
            dv = jnp.where(low_lane, dv[:SEQ_LEN], dv[SEQ_LEN:])
            dk = mm(dsc, Q[s, :, cols])
            dk = jnp.where(low_lane, dk[:SEQ_LEN], dk[SEQ_LEN:]) * 0.125
            dq = mm_tn(dsc, stacked(K[s, :, cols] * jnp.asarray(0.125, BF)))
            dq = dq * COS[s] - swap(dq) * SIN[s]
            dk = dk * COS[s] - swap(dk) * SIN[s]
            DQKV[seq_rows, cols] = dq.astype(BF)
            DQKV[seq_rows, pl.ds(pl.multiple_of(LOCAL + p * 128, 128), 128)] = dk.astype(BF)
            DQKV[seq_rows, pl.ds(pl.multiple_of(2 * LOCAL + p * 128, 128), 128)] = dv.astype(BF)

        tile_loop(PAIRS, body)

    y_dn = [
        remote(YS.at[s, other_rows], YNR.at[s], y_send.at[7 + s], y_recv.at[7 + s], y_dev)
        for s in range(2)
    ]

    def norm_back(s):
        if s == 0:
            for k in range(2):
                y_dnf[k].wait_send()
        seq_rows = slice(s * SEQ_LEN, (s + 1) * SEQ_LEN)

        def body(zi):
            r = mm_nt(DQKV[seq_rows, 0 : 3 * LOCAL], w_rows(zi, COL_QKV, 3 * LOCAL))
            YS[s, :, tile_cols(0, zi)] = r.astype(BF)

        tile_loop(4, body)
        y_dn[s].start()

    def finish_out():
        y_out.wait_recv()
        for s in range(2):

            def body(b, carry):
                rows = pl.ds(pl.multiple_of(b * ROWS, ROWS), ROWS)
                out_ref[s, rows, :] = (OUTM[s, rows, :] + YDR[s, rows, :].astype(F32)).astype(BF)
                return carry

            lax.fori_loop(0, HALF // ROWS, body, 0)
        flush(out_ref, out_hbm)

    def token_rows(s):
        y_dn[s].wait_recv()

        def body(b, carry):
            rows = pl.ds(pl.multiple_of(b * ROWS, ROWS), ROWS)
            mine = pl.ds(pl.multiple_of(y * HALF + b * ROWS, ROWS), ROWS)
            v = X[s, mine, :].astype(F32)
            inv = lax.rsqrt(jnp.mean(v * v, axis=-1, keepdims=True) + EPS)
            scaled = v * inv
            dn = YS[s, mine, :].astype(F32) + YNR[s, rows, :].astype(F32)
            GA[...] += jnp.sum((dn * scaled).reshape(ROWS // 8, 8, WIDTH), axis=0)
            u = dn * again_ref[...]
            dx = MID[s, mine, :] + inv * (
                u - scaled * jnp.mean(u * scaled, axis=-1, keepdims=True)
            )
            tgrad_ref[s, rows, :] = dx.astype(BF)
            return carry

        lax.fori_loop(0, HALF // ROWS, body, 0)
        flush(tgrad_ref.at[s], tgrad_hbm.at[s])

    def sum_start():
        SV[0] = jnp.zeros((24, 128), F32)
        first_sum = jnp.sum(GA[...], axis=0, keepdims=True)
        second_sum = jnp.sum(GF[...], axis=0, keepdims=True)
        for j in range(8):
            SV[0, j : j + 1, :] = first_sum[:, j * 128 : (j + 1) * 128]
            SV[0, 8 + j : 9 + j, :] = second_sum[:, j * 128 : (j + 1) * 128]
        for kind in range(2):
            row = jnp.zeros((1, 128), F32)
            for h in range(8):
                head_sum = jnp.sum(BS[kind, h], axis=1, keepdims=True)
                row = row + jnp.where(lane == y * 8 + h, head_sum, 0.0)
            SV[0, 16 + kind : 17 + kind, :] = row
        sums[0][0].start()

    sums = [
        [remote(SV.at[0], SR.at[0], sv_send.at[0], sv_recv.at[0], c_dev)],
        [remote(SV.at[1], SR.at[1], sv_send.at[1], sv_recv.at[1], y_dev)],
        [
            remote(SV.at[2], SR.at[2 + k], sv_send.at[2 + k], sv_recv.at[2 + k], z_devs[k])
            for k in range(3)
        ],
        [remote(SV.at[3], SR.at[5], sv_send.at[5], sv_recv.at[5], x_dev)],
    ]

    def sum_stage(i):
        total = SV[i]
        for copy in sums[i]:
            copy.wait_recv()
        first = (0, 1, 2, 5)[i]
        for k in range(len(sums[i])):
            total = total + SR[first + k]
        if i < 3:
            SV[i + 1] = total
            for copy in sums[i + 1]:
                copy.start()
        else:
            for j in range(8):
                cols = slice(j * 128, (j + 1) * 128)
                ga_ref[:, cols] = total[j : j + 1]
                gf_ref[:, cols] = total[8 + j : 9 + j]
            gb_ref[...] = total[16:18, 0:16]

    transposes = {
        TURN_FFN: (NF, T2),
        TURN_NORMED: (N1, T2),
        TURN_MIDDLE: (DML, T),
    }
    plain = {
        START: start,
        TABLES: tables,
        NORM: norm,
        TURN_COTANGENT: turn_cotangent,
        LAST_PRODUCT: last_product,
        GATHER_SENT: gather_sent,
        OUT_SEND: y_out.start,
        OUT_ROWS: finish_out,
        SUM_START: sum_start,
    }
    indexed = {
        PROJECT: project,
        ATTEND: attend,
        PROJECT_OUT: project_out,
        MIDDLE: middle_rows,
        GATE_TILES: gate_tiles,
        UP_TILES: up_tiles,
        HIDDEN_BACK: hidden_back,
        FFN_BACK: ffn_back,
        MIDDLE_BACK: middle_back,
        ATTEND_BACK: attend_back,
        NORM_BACK: norm_back,
        TOKEN_ROWS: token_rows,
        SUM_STAGE: sum_stage,
        GATHER_Z: gather_z,
        GATHER_CORE: gather_c,
        WEIGHT_GRAD: weight_grad,
        SCATTER_X: scatter_x,
        SCATTER_Z: scatter_z,
        SCATTER_PASS: scatter_pass,
        SCATTER_END: scatter_end,
        TURNED_X: turned_x,
        TURNED_END: turned_end,
        SCATTER_OWN: scatter_own,
    }
    for step, index in PROGRAM:
        if step in transposes:
            transpose_into(*transposes[step])
        elif step in plain:
            plain[step]()
        else:
            indexed[step](index)

    y_out.wait_send()
    for copy in flushes:
        copy.wait()
    for s in range(2):
        y_dn[s].wait_send()
    y_tok.wait_send()
    y_cot.wait_send()
    for group in sums:
        for copy in group:
            copy.wait_send()
    for p in range(len(SCATTER)):
        rs_c[p].wait_send()
        for copy in rs_x[p]:
            copy.wait_send()
        rs_z[p][0].wait_send()
        rs_z[p][1].wait_send()
        if SCATTER[p][4]:
            rs_z[p][2].wait_send()
            continue

        @pl.when(middle)
        def _():
            rs_z[p][2].wait_send()

        @pl.when(edge)
        def _():
            rs_relay[p].wait_send()


def finish_kernel(*refs):
    sources, dests, boxes = refs[:9], refs[9:21], refs[21:30]
    in_sem, out_sem = refs[30], refs[31]
    moves = []
    for k, places in ((0, (0,)), (1, (1,)), (5, (11,)), (4, (10,)), (3, (9,)), (2, (3, 4, 5, 7))):
        rows = sources[k].shape[-2] // PARTS
        for part in range(PARTS):
            cut = (slice(None),) * (len(sources[k].shape) - 2) + (pl.ds(part * rows, rows),)
            moves.append((sources[k].at[cut], boxes[k].at[cut], places, cut))
    for k, place in ((6, 2), (7, 8), (8, 6)):
        moves.append((sources[k], boxes[k], (place,), ()))
    loads = [
        pltpu.make_async_copy(source, box, in_sem.at[i])
        for i, (source, box, _, _) in enumerate(moves)
    ]
    for load in loads:
        load.start()
    stores = []
    for load, (_, box, places, cut) in zip(loads, moves):
        load.wait()
        for i, place in enumerate(places):
            part = box if len(places) == 1 else box.at[:, pl.ds(i * LOCAL, LOCAL)]
            dest = dests[place].at[cut] if cut else dests[place]
            store = pltpu.make_async_copy(part, dest, out_sem.at[len(stores)])
            store.start()
            stores.append(store)
    for store in stores:
        store.wait()


def fused_local(
    tokens,
    segment_ids,
    variate_ids,
    time_ids,
    attn_gain,
    w_query,
    w_key,
    w_value,
    head_bias,
    w_out,
    ffn_gain,
    w_gate,
    w_up,
    w_down,
    cotangent,
):
    inverse = 10000.0 ** (-(np.arange(32, dtype=np.float32) / np.float32(32)))
    freq = jnp.asarray(np.tile(inverse.astype(np.float32), 4)[None, :])
    vmem = pl.BlockSpec(memory_space=pltpu.VMEM)
    anym = pl.BlockSpec(memory_space=pl.ANY)
    smem = pl.BlockSpec(memory_space=pltpu.SMEM)
    bf = lambda *shape: pltpu.VMEM(shape, BF)
    fl = lambda *shape: pltpu.VMEM(shape, F32)
    seq3 = (2, SEQ_LEN, WIDTH)
    half3 = (2, HALF, WIDTH)
    dma = pltpu.SemaphoreType.DMA
    scratch = [
        bf(*half3),
        bf(*half3),
        fl(4, SHARD, CHUNK),
        bf(4, 2, 2, SHARD, ALL_COLS),
        bf(4, 2, 2, SHARD, CHUNK),
        bf(3, 4, 2, SHARD, CHUNK),
        bf(4, SHARD, NORMAL_COLS),
        bf(3, SHARD, NORMAL_COLS),
        bf(SHARD, NORMAL_COLS),
        bf(SHARD, TURNED_COLS),
        bf(3, 2, SHARD, TURNED_COLS),
        bf(2, SHARD, TURNED_COLS),
        bf(*seq3),
        bf(*seq3),
        bf(*seq3),
        bf(*seq3),
        bf(2, SEQ_LEN, LOCAL),
        bf(2, SEQ_LEN, LOCAL),
        bf(2, SEQ_LEN, LOCAL),
        bf(2, SEQ_LEN, LOCAL),
        bf(2 * PAIRS, 2 * SEQ_LEN, SEQ_LEN),
        fl(*seq3),
        bf(2 * SEQ_LEN, HIDDEN),
        bf(2 * SEQ_LEN, HIDDEN),
        bf(2 * SEQ_LEN, HIDDEN),
        bf(*seq3),
        bf(*seq3),
        bf(*half3),
        bf(*half3),
        bf(*half3),
        bf(WIDTH, 2 * SEQ_LEN),
        bf(WIDTH, 2 * SEQ_LEN),
        fl(*half3),
        bf(*seq3),
        fl(2, SEQ_LEN, SEQ_LEN),
        fl(2, SEQ_LEN, SEQ_LEN),
        fl(2, SEQ_LEN, 128),
        fl(2, SEQ_LEN, 128),
        fl(8, WIDTH),
        fl(8, WIDTH),
        fl(2, 8, 1, SEQ_LEN),
        fl(4, 24, 128),
        fl(6, 24, 128),
        dma((9,)),
        dma((9 * len(GATHER),)),
        dma((9 * len(GATHER),)),
        dma((9 * len(SCATTER),)),
        dma((9 * len(SCATTER),)),
        dma((9,)),
        dma((9,)),
        dma((6,)),
        dma((6,)),
        pltpu.SemaphoreType.REGULAR,
        pltpu.SemaphoreType.REGULAR,
        dma((len(SCATTER) + 3,)),
    ]
    shape = jax.ShapeDtypeStruct
    outs = pl.pallas_call(
        layer_kernel,
        out_shape=(
            shape(half3, BF),
            shape(half3, BF),
            shape((SHARD, HIDDEN), F32),
            shape((SHARD, HIDDEN), F32),
            shape((SHARD, HIDDEN), F32),
            shape((SHARD, HIDDEN), F32),
            shape((1, WIDTH), F32),
            shape((1, WIDTH), F32),
            shape((2, 16), F32),
        ),
        in_specs=[anym, anym, vmem, vmem, vmem, vmem, vmem, vmem, smem] + [anym] * 7,
        out_specs=(anym,) * 6 + (vmem,) * 3,
        scratch_shapes=scratch,
        compiler_params=pltpu.CompilerParams(
            collective_id=0, has_side_effects=True, vmem_limit_bytes=67043328
        ),
        name="layer",
    )(
        tokens,
        cotangent,
        segment_ids,
        variate_ids,
        time_ids,
        attn_gain.reshape(1, WIDTH),
        ffn_gain.reshape(1, WIDTH),
        freq,
        head_bias,
        w_query,
        w_key,
        w_value,
        w_out.T,
        w_gate,
        w_up,
        w_down.T,
    )
    finals = pl.pallas_call(
        finish_kernel,
        out_shape=(
            shape(half3, BF),
            shape(half3, BF),
            shape((1, WIDTH), F32),
            shape((SHARD, LOCAL), F32),
            shape((SHARD, LOCAL), F32),
            shape((SHARD, LOCAL), F32),
            shape((2, 16), F32),
            shape((SHARD, LOCAL), F32),
            shape((1, WIDTH), F32),
            shape((SHARD, HIDDEN), F32),
            shape((SHARD, HIDDEN), F32),
            shape((SHARD, HIDDEN), F32),
        ),
        in_specs=[anym] * 9,
        out_specs=[anym] * 12,
        scratch_shapes=[
            bf(*half3),
            bf(*half3),
            fl(SHARD, HIDDEN),
            fl(SHARD, HIDDEN),
            fl(SHARD, HIDDEN),
            fl(SHARD, HIDDEN),
            fl(1, WIDTH),
            fl(1, WIDTH),
            fl(2, 16),
            dma((6 * PARTS + 3,)),
            dma((9 * PARTS + 3,)),
        ],
        name="finish",
    )(*outs)
    layer_out, tokens_grad, ga, gq, gk, gv, gb, go, gf, gg, gu, gd = finals
    return (
        layer_out,
        tokens_grad,
        ga.reshape(WIDTH),
        gq,
        gk,
        gv,
        gb,
        go.T,
        gf.reshape(WIDTH),
        gg,
        gu,
        gd.T,
    )


def fits(mesh, tokens, w_query, w_gate):
    sizes = dict(mesh.shape)
    return (
        sizes["fsdp"] == 16
        and sizes["tensor"] == 2
        and tokens.shape == (2, 16 * SEQ_LEN, WIDTH)
        and w_query.shape == (WIDTH, 2 * LOCAL)
        and w_gate.shape == (WIDTH, 2 * HIDDEN)
    )


def solution(mesh):
    placed = (
        P(None, ("fsdp", "tensor"), None),
        P(None, "fsdp"),
        P(None, "fsdp"),
        P(None, "fsdp"),
        P(),
        P("fsdp", "tensor"),
        P("fsdp", "tensor"),
        P("fsdp", "tensor"),
        P(),
        P("tensor", "fsdp"),
        P(),
        P("fsdp", "tensor"),
        P("fsdp", "tensor"),
        P("tensor", "fsdp"),
        P(None, ("fsdp", "tensor"), None),
    )
    outs = (
        P(None, ("fsdp", "tensor"), None),
        P(None, ("fsdp", "tensor"), None),
        P(),
        P("fsdp", "tensor"),
        P("fsdp", "tensor"),
        P("fsdp", "tensor"),
        P(),
        P("tensor", "fsdp"),
        P(),
        P("fsdp", "tensor"),
        P("fsdp", "tensor"),
        P("tensor", "fsdp"),
    )

    def whole(*args):
        body = fused_local if fits(mesh, args[0], args[5], args[11]) else local
        return jax.shard_map(
            body, mesh=mesh, in_specs=placed, out_specs=outs, check_vma=False
        )(*args)

    return whole
```

```python
from functools import partial
from functools import reduce

import jax
import jax.numpy as jnp
import numpy as np
from jax import lax
from jax.experimental import pallas as pl
from jax.experimental.pallas import tpu as pltpu
from jax.sharding import PartitionSpec as P

HEAD_DIM = 64
SEQ_MAX = 1024


EPS = 1e-06


def product(left, right):
    return jnp.dot(left, right, preferred_element_type=jnp.float32)


def product_back(left, right):
    return lax.dot_general(
        left, right, (((1,), (1,)), ((), ())), preferred_element_type=jnp.float32
    )


def outer_sum(left, right):
    return lax.dot_general(
        left, right, (((0,), (0,)), ((), ())), preferred_element_type=jnp.float32
    )


def norm_forward(resid, gain):
    inverse = lax.rsqrt(jnp.mean(resid * resid, axis=-1, keepdims=True) + EPS)
    return (resid * inverse * gain, inverse)


def norm_backward(resid, inverse, gain, upstream):
    scaled = resid * inverse
    weighted = upstream * gain
    back = inverse * (weighted - scaled * jnp.mean(weighted * scaled, axis=-1, keepdims=True))
    return (back, jnp.sum(upstream * scaled, axis=0))


def rope_tables(moments, half_width):
    inverse = 10000.0 ** (-(jnp.arange(half_width, dtype=jnp.float32) / half_width))
    angles = moments.astype(jnp.float32)[:, None] * inverse[None, :]
    return (jnp.cos(angles), jnp.sin(angles))


def rotate(values, cosine, sine):
    half_width = values.shape[-1] // 2
    leading = values[..., :half_width]
    trailing = values[..., half_width:]
    cosine = cosine[:, None, :]
    sine = sine[:, None, :]
    return jnp.concatenate(
        [leading * cosine - trailing * sine, trailing * cosine + leading * sine], axis=-1
    )


def rotate_back(grads, cosine, sine):
    half_width = grads.shape[-1] // 2
    leading = grads[..., :half_width]
    trailing = grads[..., half_width:]
    cosine = cosine[:, None, :]
    sine = sine[:, None, :]
    return jnp.concatenate(
        [leading * cosine + trailing * sine, trailing * cosine - leading * sine], axis=-1
    )


def masked_scores(query, keys, segment, variate, bias_pair):
    scores = jnp.einsum(
        "qhd,khd->hqk", query, keys, preferred_element_type=jnp.float32
    ) * HEAD_DIM ** (-0.5)
    same_variate = variate[:, None] == variate[None, :]
    scores = scores + jnp.where(
        same_variate[None], bias_pair[0][:, None, None], bias_pair[1][:, None, None]
    )
    allowed = segment[:, None] == segment[None, :]
    return (jnp.where(allowed[None], scores, -1e30), same_variate)


def attend_forward(bias_pair, item):
    query, keys, values, segment, variate = item
    scores, unused = masked_scores(query, keys, segment, variate, bias_pair)
    highest = jnp.max(scores, axis=-1, keepdims=True)
    expo = jnp.exp(scores - highest)
    total = jnp.sum(expo, axis=-1, keepdims=True)
    probs = (expo / total).astype(jnp.bfloat16)
    attended = jnp.einsum("hqk,khd->qhd", probs, values, preferred_element_type=jnp.float32)
    return (attended.astype(jnp.bfloat16), (highest + jnp.log(total))[..., 0])


def attend_backward(bias_pair, item):
    query, keys, values, dattended, segment, variate, logsum = item
    scores, same_variate = masked_scores(query, keys, segment, variate, bias_pair)
    probs = jnp.exp(scores - logsum[..., None])
    probs_low = probs.astype(jnp.bfloat16)
    dprobs = jnp.einsum("qhd,khd->hqk", dattended, values, preferred_element_type=jnp.float32)
    dvalues = jnp.einsum("hqk,qhd->khd", probs_low, dattended, preferred_element_type=jnp.float32)
    dscores = (probs * (dprobs - jnp.sum(probs * dprobs, axis=-1, keepdims=True))).astype(
        jnp.bfloat16
    )
    widened = dscores.astype(jnp.float32)
    same_sum = jnp.sum(jnp.where(same_variate[None], widened, 0.0), axis=(1, 2))
    other_sum = jnp.sum(jnp.where(same_variate[None], 0.0, widened), axis=(1, 2))
    dquery = jnp.einsum(
        "hqk,khd->qhd", dscores, keys, preferred_element_type=jnp.float32
    ) * HEAD_DIM ** (-0.5)
    dkeys = jnp.einsum(
        "hqk,qhd->khd", dscores, query, preferred_element_type=jnp.float32
    ) * HEAD_DIM ** (-0.5)
    return (dquery, dkeys, dvalues, jnp.stack([same_sum, other_sum]))


def local(
    tokens,
    segment_ids,
    variate_ids,
    time_ids,
    attn_gain,
    w_query,
    w_key,
    w_value,
    head_bias,
    w_out,
    ffn_gain,
    w_gate,
    w_up,
    w_down,
    cotangent,
):
    micro_count, row_count, model_width = tokens.shape
    group_rows = segment_ids.shape[1]
    seq_len = min(SEQ_MAX, group_rows)
    seq_count = group_rows // seq_len
    local_width = w_query.shape[1]
    local_heads = local_width // HEAD_DIM
    head_start = lax.axis_index("tensor") * local_heads
    bias_pair = lax.dynamic_slice_in_dim(head_bias, head_start, local_heads, 1)
    shards = (w_query, w_key, w_value, w_out, w_gate, w_up, w_down)
    heads_shape = (group_rows, local_heads, HEAD_DIM)
    seq_shape = (seq_count, seq_len, local_heads, HEAD_DIM)

    def spread_normed(block):
        return lax.all_gather(block, "tensor", axis=0, tiled=True)

    def spread_grads(block):
        return lax.all_gather(block, "tensor", axis=0, tiled=True)

    def branch_rows(left, right):
        return lax.psum_scatter(product(left, right), "tensor", scatter_dimension=0, tiled=True)

    def back_rows(lefts, rights):
        pieces = [product_back(left, right) for left, right in zip(lefts, rights)]
        return lax.psum_scatter(reduce(jnp.add, pieces), "tensor", scatter_dimension=0, tiled=True)

    outputs = []
    input_grads = []
    grad_shards = None
    gain_first = jnp.zeros((model_width,), jnp.float32)
    gain_second = jnp.zeros((model_width,), jnp.float32)
    bias_grad = jnp.zeros((2, local_heads), jnp.float32)
    for micro_index in range(micro_count):
        full_weights = (
            lax.all_gather(shards[0], "fsdp", axis=0, tiled=True),
            lax.all_gather(shards[1], "fsdp", axis=0, tiled=True),
            lax.all_gather(shards[2], "fsdp", axis=0, tiled=True),
            lax.all_gather(shards[3], "fsdp", axis=1, tiled=True),
            lax.all_gather(shards[4], "fsdp", axis=0, tiled=True),
            lax.all_gather(shards[5], "fsdp", axis=0, tiled=True),
            lax.all_gather(shards[6], "fsdp", axis=1, tiled=True),
        )
        query_full, key_full, value_full, out_full, gate_full, up_full, down_full = full_weights
        resid = tokens[micro_index].astype(jnp.float32)
        segment = segment_ids[micro_index].reshape(seq_count, seq_len)
        variate = variate_ids[micro_index].reshape(seq_count, seq_len)
        cosine, sine = rope_tables(time_ids[micro_index], HEAD_DIM // 2)
        normed, inverse_first = norm_forward(resid, attn_gain)
        normed_all = spread_normed(normed.astype(jnp.bfloat16))
        query = rotate(product(normed_all, query_full).reshape(heads_shape), cosine, sine).astype(
            jnp.bfloat16
        )
        keys = rotate(product(normed_all, key_full).reshape(heads_shape), cosine, sine).astype(
            jnp.bfloat16
        )
        values = product(normed_all, value_full).astype(jnp.bfloat16)
        query_seq = query.reshape(seq_shape)
        keys_seq = keys.reshape(seq_shape)
        values_seq = values.reshape(seq_shape)
        attended, logsum = lax.map(
            partial(attend_forward, bias_pair), (query_seq, keys_seq, values_seq, segment, variate)
        )
        attended = attended.reshape(group_rows, local_width)
        middle = resid + branch_rows(attended, out_full)
        normed_ffn, inverse_second = norm_forward(middle, ffn_gain)
        normed_ffn_all = spread_normed(normed_ffn.astype(jnp.bfloat16))
        gate = product(normed_ffn_all, gate_full)
        upward = product(normed_ffn_all, up_full)
        sigmoid = jax.nn.sigmoid(gate)
        hidden = (gate * sigmoid * upward).astype(jnp.bfloat16)
        outputs.append((middle + branch_rows(hidden, down_full)).astype(jnp.bfloat16))
        full_weights = (
            lax.all_gather(shards[0], "fsdp", axis=0, tiled=True),
            lax.all_gather(shards[1], "fsdp", axis=0, tiled=True),
            lax.all_gather(shards[2], "fsdp", axis=0, tiled=True),
            lax.all_gather(shards[3], "fsdp", axis=1, tiled=True),
            lax.all_gather(shards[4], "fsdp", axis=0, tiled=True),
            lax.all_gather(shards[5], "fsdp", axis=0, tiled=True),
            lax.all_gather(shards[6], "fsdp", axis=1, tiled=True),
        )
        query_full, key_full, value_full, out_full, gate_full, up_full, down_full = full_weights
        grad_out = cotangent[micro_index].astype(jnp.float32)
        grad_ffn_all = spread_grads(cotangent[micro_index])
        dhidden = product_back(grad_ffn_all, down_full)
        dgate = (dhidden * upward * (sigmoid + gate * sigmoid * (1.0 - sigmoid))).astype(
            jnp.bfloat16
        )
        dupward = (dhidden * gate * sigmoid).astype(jnp.bfloat16)
        dnormed_ffn = back_rows((dgate, dupward), (gate_full, up_full))
        grad_gate = outer_sum(normed_ffn_all, dgate)
        grad_up = outer_sum(normed_ffn_all, dupward)
        grad_down = outer_sum(hidden, grad_ffn_all)
        dmiddle, gain_term = norm_backward(middle, inverse_second, ffn_gain, dnormed_ffn)
        gain_second = gain_second + gain_term
        dmiddle = dmiddle + grad_out
        grad_attn_all = spread_grads(dmiddle.astype(jnp.bfloat16))
        dattended = product_back(grad_attn_all, out_full).astype(jnp.bfloat16)
        grad_out_proj = outer_sum(attended, grad_attn_all)
        back_items = (
            query_seq,
            keys_seq,
            values_seq,
            dattended.reshape(seq_shape),
            segment,
            variate,
            logsum,
        )
        dquery, dkeys, dvalues, bias_terms = lax.map(
            partial(attend_backward, bias_pair), back_items
        )
        bias_grad = bias_grad + jnp.sum(bias_terms, axis=0)
        dquery = (
            rotate_back(dquery.reshape(heads_shape), cosine, sine)
            .astype(jnp.bfloat16)
            .reshape(group_rows, local_width)
        )
        dkeys = (
            rotate_back(dkeys.reshape(heads_shape), cosine, sine)
            .astype(jnp.bfloat16)
            .reshape(group_rows, local_width)
        )
        dvalues = dvalues.astype(jnp.bfloat16).reshape(group_rows, local_width)
        dnormed = back_rows((dquery, dkeys, dvalues), (query_full, key_full, value_full))
        grad_query = outer_sum(normed_all, dquery)
        grad_key = outer_sum(normed_all, dkeys)
        grad_value = outer_sum(normed_all, dvalues)
        dresid, gain_term = norm_backward(resid, inverse_first, attn_gain, dnormed)
        gain_first = gain_first + gain_term
        input_grads.append((dresid + dmiddle).astype(jnp.bfloat16))
        summed = (
            lax.psum_scatter(
                grad_query.astype(jnp.bfloat16), "fsdp", scatter_dimension=0, tiled=True
            ).astype(jnp.float32),
            lax.psum_scatter(
                grad_key.astype(jnp.bfloat16), "fsdp", scatter_dimension=0, tiled=True
            ).astype(jnp.float32),
            lax.psum_scatter(
                grad_value.astype(jnp.bfloat16), "fsdp", scatter_dimension=0, tiled=True
            ).astype(jnp.float32),
            lax.psum_scatter(
                grad_out_proj.astype(jnp.bfloat16), "fsdp", scatter_dimension=1, tiled=True
            ).astype(jnp.float32),
            lax.psum_scatter(
                grad_gate.astype(jnp.bfloat16), "fsdp", scatter_dimension=0, tiled=True
            ).astype(jnp.float32),
            lax.psum_scatter(
                grad_up.astype(jnp.bfloat16), "fsdp", scatter_dimension=0, tiled=True
            ).astype(jnp.float32),
            lax.psum_scatter(
                grad_down.astype(jnp.bfloat16), "fsdp", scatter_dimension=1, tiled=True
            ).astype(jnp.float32),
        )
        grad_shards = summed if grad_shards is None else jax.tree.map(jnp.add, grad_shards, summed)
    bias_full = lax.dynamic_update_slice_in_dim(
        jnp.zeros((2, head_bias.shape[1]), jnp.float32), bias_grad, head_start, 1
    )
    gain_first, gain_second, bias_full = lax.psum(
        (gain_first, gain_second, bias_full), ("fsdp", "tensor")
    )
    return (
        jnp.stack(outputs),
        jnp.stack(input_grads),
        gain_first,
        grad_shards[0],
        grad_shards[1],
        grad_shards[2],
        bias_full,
        grad_shards[3],
        gain_second,
        grad_shards[4],
        grad_shards[5],
        grad_shards[6],
    )


BF = jnp.bfloat16
F32 = jnp.float32
MESH = pl.DeviceIdType.MESH
SHARD = 64
SEQ_LEN = 256
HALF = 128
WIDTH = 1024
LOCAL = 512
HIDDEN = 2048
PAIRS = 4
COL_QKV, COL_OUT, COL_GATE, COL_UP, COL_DOWN = 0, 1536, 2048, 4096, 6144
ALL_COLS = 8192
LOAD_COLS = (0, 512, 1024, COL_OUT, COL_GATE, COL_UP, COL_DOWN)
LOAD_ENDS = LOAD_COLS[1:] + (ALL_COLS,)
GATHER = (
    (0, 512, False, False, True),
    (512, 512, False, False, True),
    (1024, 512, False, False, True),
    (1536, 512, False, False, True),
    (2048, 512, False, False, True),
    (2560, 512, False, False, False),
    (3072, 512, False, False, False),
    (3584, 512, False, False, False),
    (4096, 512, False, False, False),
    (4608, 512, False, False, False),
    (5120, 512, False, False, False),
    (5632, 512, False, False, False),
    (6144, 512, True, False, False),
    (6656, 512, True, False, False),
    (7168, 512, True, False, False),
    (7680, 512, True, False, False),
)
CHUNK = 2048
SCATTER = (
    (0, 0, 512, False, False, False),
    (0, 512, 512, False, False, False),
    (0, 1024, 512, False, False, False),
    (0, 1536, 512, False, False, False),
    (1, 0, 512, False, False, False),
    (1, 512, 512, False, False, False),
    (1, 1024, 512, False, False, False),
    (1, 1536, 512, True, False, False),
    (2, 0, 512, False, False, True),
    (2, 512, 512, False, False, True),
    (2, 1024, 512, False, False, True),
    (2, 1536, 512, False, False, True),
    (3, 0, 512, False, False, True),
    (3, 512, 512, False, False, True),
    (3, 1024, 512, False, False, True),
    (3, 1536, 512, False, True, True),
)
NORMAL_COLS = sum(piece[2] for piece in SCATTER if not piece[3])
TURNED_COLS = max(128, sum(piece[2] for piece in SCATTER if piece[3]))
FIRST = 5
DEPTH = 5
(
    START,
    TABLES,
    NORM,
    PROJECT,
    ATTEND,
    PROJECT_OUT,
    MIDDLE,
    GATE_TILES,
    UP_TILES,
    TURN_COTANGENT,
    TURN_FFN,
    TURN_NORMED,
    TURN_MIDDLE,
    HIDDEN_BACK,
    LAST_PRODUCT,
    GATHER_SENT,
    FFN_BACK,
    OUT_SEND,
    MIDDLE_BACK,
    ATTEND_BACK,
    NORM_BACK,
    OUT_ROWS,
    TOKEN_ROWS,
    SUM_START,
    SUM_STAGE,
    GATHER_Z,
    GATHER_CORE,
    WEIGHT_GRAD,
    SCATTER_X,
    SCATTER_Z,
    SCATTER_PASS,
    SCATTER_END,
    TURNED_X,
    TURNED_END,
    SCATTER_OWN,
) = range(35)
PROGRAM = (
    (START, 0),
    (GATHER_Z, 0),
    (GATHER_Z, 1),
    (NORM, 0),
    (TABLES, 0),
    (GATHER_Z, 2),
    (GATHER_Z, 3),
    (GATHER_CORE, 0),
    (GATHER_Z, 4),
    (TURN_COTANGENT, 0),
    (PROJECT, 0),
    (GATHER_CORE, 1),
    (GATHER_Z, 5),
    (GATHER_CORE, 2),
    (PROJECT, 2),
    (GATHER_Z, 6),
    (PROJECT, 1),
    (GATHER_CORE, 3),
    (GATHER_Z, 7),
    (ATTEND, 0),
    (PROJECT_OUT, 0),
    (GATHER_CORE, 4),
    (ATTEND, 1),
    (PROJECT_OUT, 1),
    (GATHER_CORE, 5),
    (GATHER_Z, 8),
    (GATHER_Z, 9),
    (GATHER_CORE, 6),
    (GATHER_Z, 10),
    (GATHER_CORE, 7),
    (GATHER_CORE, 8),
    (GATHER_Z, 11),
    (MIDDLE, 0),
    (MIDDLE, 1),
    (GATE_TILES, 1),
    (GATHER_Z, 12),
    (GATE_TILES, 0),
    (GATHER_CORE, 9),
    (TURN_FFN, 0),
    (UP_TILES, 0),
    (WEIGHT_GRAD, 1),
    (GATHER_CORE, 10),
    (GATHER_Z, 13),
    (WEIGHT_GRAD, 0),
    (SCATTER_X, 1),
    (SCATTER_X, 0),
    (GATHER_Z, 14),
    (GATHER_CORE, 11),
    (HIDDEN_BACK, 0),
    (UP_TILES, 1),
    (GATHER_Z, 15),
    (WEIGHT_GRAD, 2),
    (SCATTER_Z, 1),
    (WEIGHT_GRAD, 3),
    (HIDDEN_BACK, 1),
    (SCATTER_X, 2),
    (FFN_BACK, 0),
    (SCATTER_Z, 0),
    (SCATTER_X, 3),
    (GATHER_SENT, 0),
    (LAST_PRODUCT, 0),
    (WEIGHT_GRAD, 4),
    (SCATTER_Z, 2),
    (WEIGHT_GRAD, 7),
    (SCATTER_X, 4),
    (WEIGHT_GRAD, 5),
    (SCATTER_X, 7),
    (FFN_BACK, 1),
    (SCATTER_X, 5),
    (WEIGHT_GRAD, 11),
    (SCATTER_PASS, 1),
    (WEIGHT_GRAD, 8),
    (MIDDLE_BACK, 0),
    (SCATTER_X, 8),
    (SCATTER_Z, 3),
    (WEIGHT_GRAD, 10),
    (SCATTER_PASS, 0),
    (WEIGHT_GRAD, 9),
    (WEIGHT_GRAD, 6),
    (SCATTER_Z, 4),
    (SCATTER_X, 11),
    (ATTEND_BACK, 0),
    (SCATTER_X, 10),
    (SCATTER_X, 9),
    (SCATTER_Z, 5),
    (MIDDLE_BACK, 1),
    (SCATTER_Z, 8),
    (SCATTER_PASS, 7),
    (TURN_NORMED, 0),
    (NORM_BACK, 0),
    (SCATTER_X, 6),
    (SCATTER_Z, 11),
    (ATTEND_BACK, 1),
    (SCATTER_PASS, 3),
    (WEIGHT_GRAD, 14),
    (SCATTER_PASS, 2),
    (TURN_MIDDLE, 0),
    (SCATTER_X, 14),
    (SCATTER_OWN, 11),
    (SCATTER_OWN, 9),
    (SCATTER_Z, 10),
    (SCATTER_Z, 9),
    (SCATTER_PASS, 4),
    (NORM_BACK, 1),
    (SCATTER_PASS, 5),
    (WEIGHT_GRAD, 15),
    (WEIGHT_GRAD, 12),
    (SCATTER_END, 0),
    (SCATTER_Z, 6),
    (WEIGHT_GRAD, 13),
    (TOKEN_ROWS, 0),
    (SCATTER_X, 15),
    (SCATTER_X, 13),
    (SCATTER_Z, 14),
    (SCATTER_PASS, 8),
    (SCATTER_X, 12),
    (TOKEN_ROWS, 1),
    (SCATTER_PASS, 10),
    (SCATTER_END, 4),
    (SCATTER_END, 5),
    (SCATTER_END, 3),
    (SCATTER_END, 1),
    (SUM_START, 0),
    (SCATTER_PASS, 11),
    (OUT_SEND, 0),
    (SCATTER_OWN, 10),
    (SUM_STAGE, 0),
    (SCATTER_OWN, 8),
    (SCATTER_Z, 15),
    (SCATTER_Z, 13),
    (OUT_ROWS, 0),
    (SCATTER_OWN, 15),
    (SCATTER_PASS, 6),
    (SCATTER_PASS, 14),
    (SCATTER_PASS, 9),
    (SCATTER_Z, 12),
    (TURNED_X, 7),
    (SCATTER_OWN, 14),
    (SUM_STAGE, 1),
    (SCATTER_END, 10),
    (SCATTER_PASS, 13),
    (SCATTER_END, 11),
    (SCATTER_END, 8),
    (SCATTER_PASS, 15),
    (SCATTER_OWN, 13),
    (SCATTER_END, 2),
    (SCATTER_OWN, 12),
    (SCATTER_END, 6),
    (SCATTER_PASS, 12),
    (SCATTER_END, 15),
    (SUM_STAGE, 2),
    (SCATTER_END, 14),
    (SCATTER_END, 13),
    (SCATTER_END, 9),
    (TURNED_END, 7),
    (SUM_STAGE, 3),
    (SCATTER_END, 12),
)
WEIGHT_ORDER = [p for step, p in PROGRAM if step == WEIGHT_GRAD]
CORE_ORDER = [p for step, p in PROGRAM if step == SCATTER_X]
FIRST_QUERY = [p for p in WEIGHT_ORDER if SCATTER[p][0] == 3][0]
LAST_DOWN = [p for p in CORE_ORDER if SCATTER[p][0] == 0][-1]
PARTS = 1
NEGATIVE = -1e30


def mm(left, right):
    return jnp.dot(left, right, preferred_element_type=F32)


def mm_nt(left, right):
    return lax.dot_general(left, right, (((1,), (1,)), ((), ())), preferred_element_type=F32)


def mm_tn(left, right):
    return lax.dot_general(left, right, (((0,), (0,)), ((), ())), preferred_element_type=F32)


def layer_kernel(
    tok_ref,
    cot_in,
    seg_ref,
    var_ref,
    time_ref,
    again_ref,
    fgain_ref,
    freq_ref,
    bias_ref,
    wq_ref,
    wk_ref,
    wv_ref,
    wo_ref,
    wg_ref,
    wu_ref,
    wd_ref,
    out_hbm,
    tgrad_hbm,
    gqkvo_hbm,
    gg_hbm,
    gu_hbm,
    gd_hbm,
    ga_ref,
    gf_ref,
    gb_ref,
    out_ref,
    tgrad_ref,
    RES,
    W,
    GD,
    RC,
    RX,
    RZ,
    RL,
    RXS,
    RZS,
    RLS,
    X,
    COT,
    N1,
    NF,
    Q,
    K,
    V,
    ATT,
    PT,
    MID,
    GT,
    UP,
    HID,
    YS,
    YR,
    YDS,
    YDR,
    YNR,
    T,
    T2,
    OUTM,
    DML,
    SAME,
    NEGM,
    COS,
    SIN,
    GF,
    GA,
    BS,
    SV,
    SR,
    local_sem,
    ag_send,
    ag_recv,
    rs_send,
    rs_recv,
    y_send,
    y_recv,
    sv_send,
    sv_recv,
    credit,
    core_credit,
    flush_sem,
):
    f = lax.axis_index("fsdp")
    y = lax.axis_index("tensor")
    z, x, c = f // 4, (f // 2) % 2, f % 2
    zs = (z + 1 - 2 * (z % 2), (z + 2) % 4, 3 - z)
    z_devs = [(zk * 4 + x * 2 + c, y) for zk in zs]
    x_dev = (z * 4 + (1 - x) * 2 + c, y)
    c_dev = (z * 4 + x * 2 + 1 - c, y)
    y_dev = (f, 1 - y)
    partners = z_devs + [x_dev, c_dev, y_dev]

    def remote(src, dst, send, recv, dev):
        return pltpu.make_async_remote_copy(
            src_ref=src, dst_ref=dst, send_sem=send, recv_sem=recv, device_id=dev, device_id_type=MESH
        )

    barrier = pltpu.get_barrier_semaphore()
    for dev in partners:
        pl.semaphore_signal(barrier, inc=1, device_id=dev, device_id_type=MESH)
    own_rows = pl.ds(pl.multiple_of(y * HALF, HALF), HALF)
    other_rows = pl.ds(pl.multiple_of((1 - y) * HALF, HALF), HALF)
    loads = [
        (tok_ref, X.at[:, own_rows]),
        (cot_in, COT.at[:, own_rows]),
        (wq_ref, W.at[z, x, c, :, pl.ds(0, LOCAL)]),
        (wk_ref, W.at[z, x, c, :, pl.ds(LOCAL, LOCAL)]),
        (wv_ref, W.at[z, x, c, :, pl.ds(2 * LOCAL, LOCAL)]),
        (wo_ref, W.at[z, x, c, :, pl.ds(COL_OUT, LOCAL)]),
        (wg_ref, W.at[z, x, c, :, pl.ds(COL_GATE, HIDDEN)]),
        (wu_ref, W.at[z, x, c, :, pl.ds(COL_UP, HIDDEN)]),
        (wd_ref, W.at[z, x, c, :, pl.ds(COL_DOWN, HIDDEN)]),
    ]
    loads = [
        pltpu.make_async_copy(src, dst, local_sem.at[i]) for i, (src, dst) in enumerate(loads)
    ]
    for load in loads:
        load.start()
    loaded = set()

    def load_wait(*which):
        for i in which:
            if i not in loaded:
                loaded.add(i)
                loads[i].wait()

    pl.semaphore_wait(barrier, len(partners))
    middle = ((z + 1) // 2) % 2 == 1
    edge = ((z + 1) // 2) % 2 == 0

    ag_own, ag_pass, ag_x, ag_c = [], [], [], []
    for i, (c0, n, turned, straight, early) in enumerate(GATHER):
        cols = pl.ds(c0, n)

        def block(zi):
            if turned:
                return W.at[zi, :, c, :, cols]
            return W.at[zi, x, c, :, cols]

        at = i * 9
        ag_own.append(
            [
                remote(block(z), block(z), ag_send.at[at + k], ag_recv.at[at + k], z_devs[k])
                for k in range(3)
            ]
        )
        ag_pass.append(
            [
                remote(
                    block(zs[k]),
                    block(zs[k]),
                    ag_send.at[at + (0, 3, 1)[k]],
                    ag_recv.at[at + 3 - k],
                    z_devs[0],
                )
                for k in (1, 2)
            ]
        )
        part = W.at[z, x, c, :, cols] if turned else W.at[:, x, c, :, cols]
        if early:
            parts = [block(zi) for zi in (z, *zs)]
        else:
            parts = [part]
        ag_x.append(
            [
                remote(part, part, ag_send.at[at + k], ag_recv.at[at + k], x_dev)
                for k, part in zip((4, 6, 7, 8), parts)
            ]
        )
        part = W.at[:, :, c, :, cols]
        ag_c.append(remote(part, part, ag_send.at[at + 5], ag_recv.at[at + 5], c_dev))

    def own_load(i):
        c0, n = GATHER[i][:2]
        for k, base in enumerate(LOAD_COLS):
            if base < c0 + n and c0 < LOAD_ENDS[k]:
                load_wait(2 + k)

    def gather_own(i):
        own_load(i)
        if GATHER[i][2]:
            ag_x[i][0].wait_recv()
        ag_own[i][0].start()
        if GATHER[i][3]:
            ag_own[i][1].start()
            ag_own[i][2].start()
            return

        @pl.when(edge)
        def _():
            ag_own[i][1].start()

        @pl.when(middle)
        def _():
            ag_own[i][2].start()

    def gather_z(i):
        if GATHER[i][3]:
            ag_own[i][1].wait_recv()
        else:

            @pl.when(middle)
            def _():
                for k in (1, 2):
                    ag_own[i][k].wait_recv()
                    ag_pass[i][k - 1].start()

        for k in range(max(FIRST, i + DEPTH if i else FIRST), min(i + DEPTH + 1, len(GATHER))):
            gather_own(k)
        ag_own[i][0].wait_recv()
        if GATHER[i][3]:
            ag_own[i][2].wait_recv()
        else:

            @pl.when(edge)
            def _():
                ag_own[i][1].wait_recv()
                ag_own[i][2].wait_recv()

        if GATHER[i][2]:
            ag_c[i].start()
        else:
            for copy in ag_x[i][1 if GATHER[i][4] else 0 :]:
                copy.start()

    def gather_c(i):
        for copy in ag_x[i]:
            copy.wait_recv()
        ag_c[i].start()

    ended = set()

    def gather_end(c0, n):
        for i, (start_col, size, *_) in enumerate(GATHER):
            if start_col < c0 + n and c0 < start_col + size and i not in ended:
                ended.add(i)
                ag_c[i].wait_recv()

    y_tok = remote(X.at[:, own_rows], X.at[:, own_rows], y_send.at[0], y_recv.at[0], y_dev)
    y_cot = remote(COT.at[:, own_rows], COT.at[:, own_rows], y_send.at[1], y_recv.at[1], y_dev)

    def start():
        load_wait(0)
        y_tok.start()
        for i in range(FIRST):
            gather_own(i)
        for i in range(len(GATHER)):
            if GATHER[i][2] or GATHER[i][4]:
                own_load(i)
                ag_x[i][0].start()
        load_wait(1)
        y_cot.start()

        @pl.when(edge)
        def _():
            for p, (_, _, n, turned, straight, _) in enumerate(SCATTER):
                spot = sum(piece[2] for piece in SCATTER[:p] if piece[3] == turned)
                if turned and not straight:
                    RZS[2, :, :, pl.ds(spot, n)] = jnp.zeros((2, SHARD, n), BF)
                elif not straight:
                    RZ[2, :, pl.ds(spot, n)] = jnp.zeros((SHARD, n), BF)

    lane = lax.broadcasted_iota(jnp.int32, (1, 128), 1)
    low_lane = lane < 64
    lead_lane = (lane % 64) < 32

    def column(row):
        return jnp.transpose(jnp.broadcast_to(row.astype(F32), (128, SEQ_LEN)))

    def tables():
        for s in range(2):
            moments = column(time_ref[s : s + 1, :])
            angles = moments * freq_ref[...]
            COS[s] = jnp.cos(angles)
            sine = jnp.sin(angles)
            SIN[s] = jnp.where(lead_lane, -sine, sine)
            seg_row = seg_ref[s : s + 1, :].astype(F32)
            var_row = var_ref[s : s + 1, :].astype(F32)
            seg_col = column(seg_ref[s : s + 1, :])
            var_col = column(var_ref[s : s + 1, :])
            for h in range(2):
                part = slice(h * 128, (h + 1) * 128)
                SAME[s, :, part] = jnp.where(var_col == var_row[:, part], 1.0, 0.0)
                NEGM[s, :, part] = jnp.where(seg_col == seg_row[:, part], 0.0, NEGATIVE)

    def swap(values):
        return jnp.where(
            lead_lane, pltpu.roll(values, 96, axis=1), pltpu.roll(values, 32, axis=1)
        )

    ROWS = 64
    BLOCKS = SEQ_LEN // ROWS

    def row_loop(body):
        def step(b, carry):
            body(b, pl.ds(pl.multiple_of(b * ROWS, ROWS), ROWS))
            return carry

        lax.fori_loop(0, BLOCKS, step, 0)

    def tile_loop(count, body):
        def step(j, carry):
            body(j)
            return carry

        lax.fori_loop(0, count, step, 0)

    def tile_cols(base, j, size=256):
        return pl.ds(pl.multiple_of(base + j * size, size), size)

    def w_tile(cols):
        return W[:, :, :, :, cols].reshape(WIDTH, 256)

    def w_rows(zi, c0, n):
        return W[zi, :, :, :, pl.ds(c0, n)].reshape(256, n)

    def transpose_into(src, T):
        for s in range(2):

            def body(j):
                cols = tile_cols(0, j)
                T[cols, s * SEQ_LEN : (s + 1) * SEQ_LEN] = jnp.transpose(src[s, :, cols])

            tile_loop(4, body)

    def norm():
        y_tok.wait_recv()
        for s in range(2):

            def body(b, rows):
                v = X[s, rows, :].astype(F32)
                inv = lax.rsqrt(jnp.mean(v * v, axis=-1, keepdims=True) + EPS)
                N1[s, rows, :] = (v * inv * again_ref[...]).astype(BF)

            row_loop(body)

    def project(kind):
        gather_end(kind * LOCAL, LOCAL)
        dest = (Q, K, V)[kind]

        def body(j):
            r = mm(N1[...].reshape(2 * SEQ_LEN, WIDTH), w_tile(tile_cols(kind * LOCAL, j)))
            for h in range(2):
                part = r[:, h * 128 : (h + 1) * 128]
                if kind < 2:
                    cosine = COS[...].reshape(2 * SEQ_LEN, 128)
                    sine = SIN[...].reshape(2 * SEQ_LEN, 128)
                    part = part * cosine + swap(part) * sine
                dest[:, :, pl.ds(pl.multiple_of(j * 256 + h * 128, 128), 128)] = part.astype(
                    BF
                ).reshape(2, SEQ_LEN, 128)

        tile_loop(2, body)

    def stacked(values):
        zero = jnp.zeros_like(values)
        return jnp.concatenate(
            [jnp.where(low_lane, values, zero), jnp.where(low_lane, zero, values)], axis=0
        )

    def pair_cols(p):
        return pl.ds(pl.multiple_of(p * 128, 128), 128)

    y_att = [
        remote(YS.at[s], YR.at[s], y_send.at[2 + s], y_recv.at[2 + s], y_dev) for s in range(2)
    ]
    def attend(s):
        def body(p):
            cols = pair_cols(p)
            keys = stacked(K[s, :, cols] * jnp.asarray(0.125, BF))
            scores = mm_nt(keys, Q[s, :, cols])
            parts = []
            for h in range(2):
                head = y * 8 + p * 2 + h
                same_bias = bias_ref[0, head]
                other_bias = bias_ref[1, head]
                sc = scores[h * SEQ_LEN : (h + 1) * SEQ_LEN]
                sc = sc + (SAME[s] * (same_bias - other_bias) + (NEGM[s] + other_bias))
                top = jnp.max(sc, axis=0, keepdims=True)
                expo = jnp.exp(sc - top)
                total = jnp.sum(expo, axis=0, keepdims=True)
                parts.append((expo * (1.0 / total)).astype(BF))
            probs = jnp.concatenate(parts, axis=0)
            PT[s * PAIRS + p] = probs
            ATT[s, :, cols] = mm_tn(probs, stacked(V[s, :, cols])).astype(BF)

        tile_loop(PAIRS, body)

    def project_out(s):
        if s == 0:
            gather_end(COL_OUT, LOCAL)
        for zi in range(4):
            YS[s, :, zi * 256 : (zi + 1) * 256] = mm_nt(
                ATT[s], w_rows(zi, COL_OUT, LOCAL)
            ).astype(BF)
        y_att[s].start()

    def middle_rows(s):
        y_att[s].wait_recv()

        def body(b, rows):
            v = X[s, rows, :].astype(F32) + (YS[s, rows, :].astype(F32) + YR[s, rows, :].astype(F32))
            MID[s, rows, :] = v
            inv = lax.rsqrt(jnp.mean(v * v, axis=-1, keepdims=True) + EPS)
            NF[s, rows, :] = (v * inv * fgain_ref[...]).astype(BF)

        row_loop(body)
        if s == 1:
            for k in range(2):
                y_att[k].wait_send()
            pl.semaphore_signal(credit, inc=1, device_id=y_dev, device_id_type=MESH)

    def gate_tiles(half):
        gather_end(COL_GATE + half * 1024, 1024)

        def body(j):
            cols = tile_cols(half * 1024, j)
            GT[:, cols] = mm(
                NF[...].reshape(2 * SEQ_LEN, WIDTH), w_tile(tile_cols(COL_GATE + half * 1024, j))
            ).astype(BF)

        tile_loop(4, body)

    def up_tiles(half):
        gather_end(COL_UP + half * 1024, 1024)

        def body(j):
            cols = tile_cols(half * 1024, j)
            up = mm(
                NF[...].reshape(2 * SEQ_LEN, WIDTH), w_tile(tile_cols(COL_UP + half * 1024, j))
            )
            UP[:, cols] = up.astype(BF)
            gate = GT[:, cols].astype(F32)
            HID[:, cols] = (gate * jax.nn.sigmoid(gate) * up).astype(BF)

        tile_loop(4, body)

    def turn_cotangent():
        y_cot.wait_recv()
        transpose_into(COT, T)

    homes = ((GD, 0), (W, COL_DOWN), (W, COL_GATE), (W, COL_UP))
    results = tuple(RES.at[ch] for ch in range(4))
    result_homes = (gd_hbm, gg_hbm, gu_hbm, gqkvo_hbm)
    flushes = []

    def flush(src, dst):
        copy = pltpu.make_async_copy(src, dst, flush_sem.at[len(flushes)])
        copy.start()
        flushes.append(copy)

    def flush_result(p):
        ch, c0, n = SCATTER[p][:3]
        cols = pl.ds(c0, n)
        flush(results[ch].at[:, cols], result_homes[ch].at[:, cols])


    def home(ch, *index, c0=0, n=CHUNK):
        ref, base = homes[ch]
        return ref.at[index + (slice(None), pl.ds(base + c0, n))]

    every = slice(None)
    slots = (0, 1, 2, 0)
    rs_c, rs_x, rs_z, rs_relay = [], [], [], []
    spots = []
    for p, (ch, c0, n, turned, straight, late) in enumerate(SCATTER):
        spot = sum(piece[2] for piece in SCATTER[:p] if piece[3] == turned)
        spots.append(spot)
        at = p * 9

        def sems(k):
            return rs_send.at[at + k], rs_recv.at[at + k]

        rs_c.append(
            remote(
                home(ch, every, every, 1 - c, c0=c0, n=n),
                RC.at[slots[ch], :, :, :, pl.ds(c0, n)],
                *sems(0),
                c_dev,
            )
        )
        cols = pl.ds(spot, n)
        if turned:
            rs_x.append(
                [remote(home(ch, z, 1 - x, c, c0=c0, n=n), RXS.at[:, cols], *sems(1), x_dev)]
            )
            views = [home(ch, zk, every, c, c0=c0, n=n) for zk in zs]
            boxes, relay = [RZS.at[k, :, :, cols] for k in range(3)], RLS.at[:, :, cols]
        else:
            blocks = (*zs, z) if late else (every,)
            rs_x.append(
                [
                    remote(
                        home(ch, zi, 1 - x, c, c0=c0, n=n), RX.at[zi, :, cols], *sems(k), x_dev
                    )
                    for k, zi in zip((1, 6, 7, 8), blocks)
                ]
            )
            views = [home(ch, zk, x, c, c0=c0, n=n) for zk in zs]
            boxes, relay = [RZ.at[k, :, cols] for k in range(3)], RL.at[:, cols]
        rs_z.append(
            [remote(views[k], boxes[k], *sems(2 + k), z_devs[k]) for k in range(3)]
        )
        rs_relay.append(remote(views[2], relay, *sems(5), z_devs[0]))

    def add_core(p, xi):
        ch, c0, n, turned, straight, late = SCATTER[p]

        def body(zi):
            view = home(ch, zi, xi, c, c0=c0, n=n)
            view[...] = view[...] + RC[slots[ch], zi, xi, :, pl.ds(c0, n)]

        tile_loop(4, body)

    def send_z(p):
        rs_z[p][0].start()
        if SCATTER[p][4]:
            rs_z[p][1].start()
            rs_z[p][2].start()
            return

        @pl.when(middle)
        def _():
            rs_z[p][2].start()

        @pl.when(edge)
        def _():
            rs_z[p][1].start()
            rs_relay[p].start()

    def scatter_x(p):
        rs_c[p].wait_recv()
        add_core(p, 1 - x)
        if SCATTER[p][3]:
            add_core(p, x)
            send_z(p)
        else:
            for copy in rs_x[p][:3]:
                copy.start()
            add_core(p, x)
        if p == LAST_DOWN:
            pl.semaphore_signal(core_credit, inc=1, device_id=c_dev, device_id_type=MESH)

    def scatter_z(p):
        ch, c0, n, turned, straight, late = SCATTER[p]
        for copy in rs_x[p][:3]:
            copy.wait_recv()

        def body(zi):
            view = home(ch, zi, x, c, c0=c0, n=n)
            view[...] = view[...] + RX[zi, :, pl.ds(spots[p], n)]

        if late:
            for zi in zs:
                body(zi)
        else:
            tile_loop(4, body)
        send_z(p)

    def scatter_own(p):
        rs_x[p][3].start()

    def scatter_pass(p):
        ch, c0, n, turned, straight, late = SCATTER[p]
        if straight:
            return

        @pl.when(middle)
        def _():
            rs_relay[p].wait_recv()
            if turned:
                view = home(ch, zs[1], every, c, c0=c0, n=n)
                view[...] = view[...] + RLS[:, :, pl.ds(spots[p], n)]
            else:
                view = home(ch, zs[1], x, c, c0=c0, n=n)
                view[...] = view[...] + RL[:, pl.ds(spots[p], n)]
            rs_z[p][1].start()

    def wait_z(p):
        rs_z[p][0].wait_recv()
        rs_z[p][1].wait_recv()
        if SCATTER[p][4]:
            rs_z[p][2].wait_recv()
            return

        @pl.when(middle)
        def _():
            rs_z[p][2].wait_recv()

    def scatter_end(p):
        ch, c0, n, turned, straight, late = SCATTER[p]
        wait_z(p)
        if late:
            rs_x[p][3].wait_recv()

        def body(j):
            total = home(ch, z, x, c)[:, tile_cols(c0, j)].astype(F32)
            if late:
                total = total + RX[z, :, tile_cols(spots[p], j)].astype(F32)
            for k in range(3):
                total = total + RZ[k, :, tile_cols(spots[p], j)].astype(F32)
            results[ch][:, tile_cols(c0, j)] = total

        tile_loop(n // 256, body)
        flush_result(p)

    def turned_x(p):
        ch, c0, n, turned, straight, late = SCATTER[p]
        wait_z(p)
        for xi in range(2):
            view = home(ch, z, xi, c, c0=c0, n=n)
            total = view[...].astype(F32)
            for k in range(3):
                total = total + RZS[k, xi, :, pl.ds(spots[p], n)].astype(F32)
            view[...] = total.astype(BF)
        rs_x[p][0].start()

    def turned_end(p):
        ch, c0, n, turned, straight, late = SCATTER[p]
        rs_x[p][0].wait_recv()
        own = home(ch, z, x, c, c0=c0, n=n)[...].astype(F32)
        results[ch][:, c0 : c0 + n] = own + RXS[:, pl.ds(spots[p], n)].astype(F32)
        flush_result(p)

    def weight_tiles(ch, c0, n):
        ref, base = homes[ch]

        def body(j):
            cols = tile_cols(c0, j)
            if ch == 0:
                left, right = T, HID[:, cols]
            elif ch == 1:
                left, right = T2, GT[:, cols]
            elif ch == 2:
                left, right = T2, UP[:, cols]
            elif c0 < 3 * LOCAL:
                left, right = T2, DQKV[:, cols]
            else:
                left, right = T, ATT[:, :, tile_cols(c0 - 3 * LOCAL, j)].reshape(2 * SEQ_LEN, 256)
            r = mm(left[...], right)
            ref[:, :, :, :, tile_cols(base + c0, j)] = r.astype(BF).reshape(4, 2, 2, SHARD, 256)

        tile_loop(n // 256, body)

    def weight_grad(p):
        ch, c0, n, turned, straight, late = SCATTER[p]
        if p == FIRST_QUERY:
            pl.semaphore_wait(core_credit, 1)
        if ch == 3 and c0 < 3 * LOCAL < c0 + n:
            weight_tiles(ch, c0, 3 * LOCAL - c0)
            weight_tiles(ch, 3 * LOCAL, c0 + n - 3 * LOCAL)
        else:
            weight_tiles(ch, c0, n)
        rs_c[p].start()

    def hidden_back(half):
        gather_end(COL_DOWN + half * 1024, 1024)

        def body(j):
            cols = tile_cols(half * 1024, j)
            dhid = mm(
                COT[...].reshape(2 * SEQ_LEN, WIDTH), w_tile(tile_cols(COL_DOWN + half * 1024, j))
            )
            gate = GT[:, cols].astype(F32)
            up = UP[:, cols].astype(F32)
            sig = jax.nn.sigmoid(gate)
            GT[:, cols] = (dhid * up * (sig + gate * sig * (1.0 - sig))).astype(BF)
            UP[:, cols] = (dhid * gate * sig).astype(BF)

        tile_loop(4, body)

    def gather_sent():
        for i in range(len(GATHER)):
            ag_own[i][0].wait_send()
            for copy in ag_x[i]:
                copy.wait_send()
            ag_c[i].wait_send()
            if GATHER[i][3]:
                ag_own[i][1].wait_send()
                ag_own[i][2].wait_send()
                continue

            @pl.when(edge)
            def _():
                ag_own[i][1].wait_send()

            @pl.when(middle)
            def _():
                ag_own[i][2].wait_send()
                for copy in ag_pass[i]:
                    copy.wait_send()

    def last_product():
        def body(zi):
            cols = tile_cols(0, zi)
            r = mm_nt(HID[...], w_rows(zi, COL_DOWN, HIDDEN)).reshape(2, 2, HALF, 256)
            mine = jnp.where(y == 0, r[:, 0], r[:, 1])
            OUTM[:, :, cols] = MID[:, own_rows, cols] + mine
            YDS[:, :, cols] = jnp.where(y == 0, r[:, 1], r[:, 0]).astype(BF)

        tile_loop(4, body)

    y_dnf = [
        remote(YS.at[s], YR.at[s], y_send.at[4 + s], y_recv.at[4 + s], y_dev) for s in range(2)
    ]
    y_out = remote(YDS, YDR, y_send.at[6], y_recv.at[6], y_dev)

    def ffn_back(s):
        if s == 0:
            pl.semaphore_wait(credit, 1)
        rows = slice(s * SEQ_LEN, (s + 1) * SEQ_LEN)

        def body(zi):
            r = mm_nt(GT[rows, :], w_rows(zi, COL_GATE, HIDDEN))
            r = r + mm_nt(UP[rows, :], w_rows(zi, COL_UP, HIDDEN))
            YS[s, :, tile_cols(0, zi)] = r.astype(BF)

        tile_loop(4, body)
        y_dnf[s].start()

    DAT = HID.at[:, 3 * LOCAL : 4 * LOCAL]
    DQKV = HID

    def middle_back(s):
        if s == 0:
            GF[...] = jnp.zeros_like(GF)
            GA[...] = jnp.zeros_like(GA)
        y_dnf[s].wait_recv()

        def body(b, rows):
            v = MID[s, rows, :]
            inv = lax.rsqrt(jnp.mean(v * v, axis=-1, keepdims=True) + EPS)
            scaled = v * inv
            dn = YS[s, rows, :].astype(F32) + YR[s, rows, :].astype(F32)
            flag = jnp.where(b // (HALF // ROWS) == y, 1.0, 0.0)
            GF[...] += flag * jnp.sum((dn * scaled).reshape(ROWS // 8, 8, WIDTH), axis=0)
            u = dn * fgain_ref[...]
            dm = COT[s, rows, :].astype(F32) + inv * (
                u - scaled * jnp.mean(u * scaled, axis=-1, keepdims=True)
            )
            MID[s, rows, :] = dm
            DML[s, rows, :] = dm.astype(BF)

        row_loop(body)
        seq_rows = slice(s * SEQ_LEN, (s + 1) * SEQ_LEN)

        def body(j):
            DAT[seq_rows, tile_cols(0, j)] = mm(DML[s], w_tile(tile_cols(COL_OUT, j))).astype(BF)

        tile_loop(2, body)

    def attend_back(s):
        seq_rows = slice(s * SEQ_LEN, (s + 1) * SEQ_LEN)

        def body(p):
            cols = pair_cols(p)
            do = DAT[seq_rows, cols]
            dprobs = mm_nt(stacked(V[s, :, cols]), do)
            probs_low = PT[s * PAIRS + p]
            parts = []
            for h in range(2):
                part = slice(h * SEQ_LEN, (h + 1) * SEQ_LEN)
                pr = probs_low[part].astype(F32)
                dp = dprobs[part]
                dot = jnp.sum(pr * dp, axis=0, keepdims=True)
                ds = (pr * (dp - dot)).astype(BF)
                wide = ds.astype(F32)
                same = wide * SAME[s]
                same_sum = jnp.sum(same, axis=0, keepdims=True)
                other_sum = jnp.sum(wide - same, axis=0, keepdims=True)
                if s == 0:
                    BS[0, p * 2 + h] = same_sum
                    BS[1, p * 2 + h] = other_sum
                else:
                    BS[0, p * 2 + h] += same_sum
                    BS[1, p * 2 + h] += other_sum
                parts.append(ds)
            dsc = jnp.concatenate(parts, axis=0)
            dv = mm(probs_low, do)
            dv = jnp.where(low_lane, dv[:SEQ_LEN], dv[SEQ_LEN:])
            dk = mm(dsc, Q[s, :, cols])
            dk = jnp.where(low_lane, dk[:SEQ_LEN], dk[SEQ_LEN:]) * 0.125
            dq = mm_tn(dsc, stacked(K[s, :, cols] * jnp.asarray(0.125, BF)))
            dq = dq * COS[s] - swap(dq) * SIN[s]
            dk = dk * COS[s] - swap(dk) * SIN[s]
            DQKV[seq_rows, cols] = dq.astype(BF)
            DQKV[seq_rows, pl.ds(pl.multiple_of(LOCAL + p * 128, 128), 128)] = dk.astype(BF)
            DQKV[seq_rows, pl.ds(pl.multiple_of(2 * LOCAL + p * 128, 128), 128)] = dv.astype(BF)

        tile_loop(PAIRS, body)

    y_dn = [
        remote(YS.at[s, other_rows], YNR.at[s], y_send.at[7 + s], y_recv.at[7 + s], y_dev)
        for s in range(2)
    ]

    def norm_back(s):
        if s == 0:
            for k in range(2):
                y_dnf[k].wait_send()
        seq_rows = slice(s * SEQ_LEN, (s + 1) * SEQ_LEN)

        def body(zi):
            r = mm_nt(DQKV[seq_rows, 0 : 3 * LOCAL], w_rows(zi, COL_QKV, 3 * LOCAL))
            YS[s, :, tile_cols(0, zi)] = r.astype(BF)

        tile_loop(4, body)
        y_dn[s].start()

    def finish_out():
        y_out.wait_recv()
        for s in range(2):

            def body(b, carry):
                rows = pl.ds(pl.multiple_of(b * ROWS, ROWS), ROWS)
                out_ref[s, rows, :] = (OUTM[s, rows, :] + YDR[s, rows, :].astype(F32)).astype(BF)
                return carry

            lax.fori_loop(0, HALF // ROWS, body, 0)
        flush(out_ref, out_hbm)

    def token_rows(s):
        y_dn[s].wait_recv()

        def body(b, carry):
            rows = pl.ds(pl.multiple_of(b * ROWS, ROWS), ROWS)
            mine = pl.ds(pl.multiple_of(y * HALF + b * ROWS, ROWS), ROWS)
            v = X[s, mine, :].astype(F32)
            inv = lax.rsqrt(jnp.mean(v * v, axis=-1, keepdims=True) + EPS)
            scaled = v * inv
            dn = YS[s, mine, :].astype(F32) + YNR[s, rows, :].astype(F32)
            GA[...] += jnp.sum((dn * scaled).reshape(ROWS // 8, 8, WIDTH), axis=0)
            u = dn * again_ref[...]
            dx = MID[s, mine, :] + inv * (
                u - scaled * jnp.mean(u * scaled, axis=-1, keepdims=True)
            )
            tgrad_ref[s, rows, :] = dx.astype(BF)
            return carry

        lax.fori_loop(0, HALF // ROWS, body, 0)
        flush(tgrad_ref.at[s], tgrad_hbm.at[s])

    def sum_start():
        SV[0] = jnp.zeros((24, 128), F32)
        first_sum = jnp.sum(GA[...], axis=0, keepdims=True)
        second_sum = jnp.sum(GF[...], axis=0, keepdims=True)
        for j in range(8):
            SV[0, j : j + 1, :] = first_sum[:, j * 128 : (j + 1) * 128]
            SV[0, 8 + j : 9 + j, :] = second_sum[:, j * 128 : (j + 1) * 128]
        for kind in range(2):
            row = jnp.zeros((1, 128), F32)
            for h in range(8):
                head_sum = jnp.sum(BS[kind, h], axis=1, keepdims=True)
                row = row + jnp.where(lane == y * 8 + h, head_sum, 0.0)
            SV[0, 16 + kind : 17 + kind, :] = row
        sums[0][0].start()

    sums = [
        [remote(SV.at[0], SR.at[0], sv_send.at[0], sv_recv.at[0], c_dev)],
        [remote(SV.at[1], SR.at[1], sv_send.at[1], sv_recv.at[1], y_dev)],
        [
            remote(SV.at[2], SR.at[2 + k], sv_send.at[2 + k], sv_recv.at[2 + k], z_devs[k])
            for k in range(3)
        ],
        [remote(SV.at[3], SR.at[5], sv_send.at[5], sv_recv.at[5], x_dev)],
    ]

    def sum_stage(i):
        total = SV[i]
        for copy in sums[i]:
            copy.wait_recv()
        first = (0, 1, 2, 5)[i]
        for k in range(len(sums[i])):
            total = total + SR[first + k]
        if i < 3:
            SV[i + 1] = total
            for copy in sums[i + 1]:
                copy.start()
        else:
            for j in range(8):
                cols = slice(j * 128, (j + 1) * 128)
                ga_ref[:, cols] = total[j : j + 1]
                gf_ref[:, cols] = total[8 + j : 9 + j]
            gb_ref[...] = total[16:18, 0:16]

    transposes = {
        TURN_FFN: (NF, T2),
        TURN_NORMED: (N1, T2),
        TURN_MIDDLE: (DML, T),
    }
    plain = {
        START: start,
        TABLES: tables,
        NORM: norm,
        TURN_COTANGENT: turn_cotangent,
        LAST_PRODUCT: last_product,
        GATHER_SENT: gather_sent,
        OUT_SEND: y_out.start,
        OUT_ROWS: finish_out,
        SUM_START: sum_start,
    }
    indexed = {
        PROJECT: project,
        ATTEND: attend,
        PROJECT_OUT: project_out,
        MIDDLE: middle_rows,
        GATE_TILES: gate_tiles,
        UP_TILES: up_tiles,
        HIDDEN_BACK: hidden_back,
        FFN_BACK: ffn_back,
        MIDDLE_BACK: middle_back,
        ATTEND_BACK: attend_back,
        NORM_BACK: norm_back,
        TOKEN_ROWS: token_rows,
        SUM_STAGE: sum_stage,
        GATHER_Z: gather_z,
        GATHER_CORE: gather_c,
        WEIGHT_GRAD: weight_grad,
        SCATTER_X: scatter_x,
        SCATTER_Z: scatter_z,
        SCATTER_PASS: scatter_pass,
        SCATTER_END: scatter_end,
        TURNED_X: turned_x,
        TURNED_END: turned_end,
        SCATTER_OWN: scatter_own,
    }
    for step, index in PROGRAM:
        if step in transposes:
            transpose_into(*transposes[step])
        elif step in plain:
            plain[step]()
        else:
            indexed[step](index)

    y_out.wait_send()
    for copy in flushes:
        copy.wait()
    for s in range(2):
        y_dn[s].wait_send()
    y_tok.wait_send()
    y_cot.wait_send()
    for group in sums:
        for copy in group:
            copy.wait_send()
    for p in range(len(SCATTER)):
        rs_c[p].wait_send()
        for copy in rs_x[p]:
            copy.wait_send()
        rs_z[p][0].wait_send()
        rs_z[p][1].wait_send()
        if SCATTER[p][4]:
            rs_z[p][2].wait_send()
            continue

        @pl.when(middle)
        def _():
            rs_z[p][2].wait_send()

        @pl.when(edge)
        def _():
            rs_relay[p].wait_send()


def finish_kernel(*refs):
    sources, dests, boxes = refs[:9], refs[9:21], refs[21:30]
    in_sem, out_sem = refs[30], refs[31]
    moves = []
    for k, places in ((0, (0,)), (1, (1,)), (5, (11,)), (4, (10,)), (3, (9,)), (2, (3, 4, 5, 7))):
        rows = sources[k].shape[-2] // PARTS
        for part in range(PARTS):
            cut = (slice(None),) * (len(sources[k].shape) - 2) + (pl.ds(part * rows, rows),)
            moves.append((sources[k].at[cut], boxes[k].at[cut], places, cut))
    for k, place in ((6, 2), (7, 8), (8, 6)):
        moves.append((sources[k], boxes[k], (place,), ()))
    loads = [
        pltpu.make_async_copy(source, box, in_sem.at[i])
        for i, (source, box, _, _) in enumerate(moves)
    ]
    for load in loads:
        load.start()
    stores = []
    for load, (_, box, places, cut) in zip(loads, moves):
        load.wait()
        for i, place in enumerate(places):
            part = box if len(places) == 1 else box.at[:, pl.ds(i * LOCAL, LOCAL)]
            dest = dests[place].at[cut] if cut else dests[place]
            store = pltpu.make_async_copy(part, dest, out_sem.at[len(stores)])
            store.start()
            stores.append(store)
    for store in stores:
        store.wait()


def fused_local(
    tokens,
    segment_ids,
    variate_ids,
    time_ids,
    attn_gain,
    w_query,
    w_key,
    w_value,
    head_bias,
    w_out,
    ffn_gain,
    w_gate,
    w_up,
    w_down,
    cotangent,
):
    inverse = 10000.0 ** (-(np.arange(32, dtype=np.float32) / np.float32(32)))
    freq = jnp.asarray(np.tile(inverse.astype(np.float32), 4)[None, :])
    vmem = pl.BlockSpec(memory_space=pltpu.VMEM)
    anym = pl.BlockSpec(memory_space=pl.ANY)
    smem = pl.BlockSpec(memory_space=pltpu.SMEM)
    bf = lambda *shape: pltpu.VMEM(shape, BF)
    fl = lambda *shape: pltpu.VMEM(shape, F32)
    seq3 = (2, SEQ_LEN, WIDTH)
    half3 = (2, HALF, WIDTH)
    dma = pltpu.SemaphoreType.DMA
    scratch = [
        bf(*half3),
        bf(*half3),
        fl(4, SHARD, CHUNK),
        bf(4, 2, 2, SHARD, ALL_COLS),
        bf(4, 2, 2, SHARD, CHUNK),
        bf(3, 4, 2, SHARD, CHUNK),
        bf(4, SHARD, NORMAL_COLS),
        bf(3, SHARD, NORMAL_COLS),
        bf(SHARD, NORMAL_COLS),
        bf(SHARD, TURNED_COLS),
        bf(3, 2, SHARD, TURNED_COLS),
        bf(2, SHARD, TURNED_COLS),
        bf(*seq3),
        bf(*seq3),
        bf(*seq3),
        bf(*seq3),
        bf(2, SEQ_LEN, LOCAL),
        bf(2, SEQ_LEN, LOCAL),
        bf(2, SEQ_LEN, LOCAL),
        bf(2, SEQ_LEN, LOCAL),
        bf(2 * PAIRS, 2 * SEQ_LEN, SEQ_LEN),
        fl(*seq3),
        bf(2 * SEQ_LEN, HIDDEN),
        bf(2 * SEQ_LEN, HIDDEN),
        bf(2 * SEQ_LEN, HIDDEN),
        bf(*seq3),
        bf(*seq3),
        bf(*half3),
        bf(*half3),
        bf(*half3),
        bf(WIDTH, 2 * SEQ_LEN),
        bf(WIDTH, 2 * SEQ_LEN),
        fl(*half3),
        bf(*seq3),
        fl(2, SEQ_LEN, SEQ_LEN),
        fl(2, SEQ_LEN, SEQ_LEN),
        fl(2, SEQ_LEN, 128),
        fl(2, SEQ_LEN, 128),
        fl(8, WIDTH),
        fl(8, WIDTH),
        fl(2, 8, 1, SEQ_LEN),
        fl(4, 24, 128),
        fl(6, 24, 128),
        dma((9,)),
        dma((9 * len(GATHER),)),
        dma((9 * len(GATHER),)),
        dma((9 * len(SCATTER),)),
        dma((9 * len(SCATTER),)),
        dma((9,)),
        dma((9,)),
        dma((6,)),
        dma((6,)),
        pltpu.SemaphoreType.REGULAR,
        pltpu.SemaphoreType.REGULAR,
        dma((len(SCATTER) + 3,)),
    ]
    shape = jax.ShapeDtypeStruct
    outs = pl.pallas_call(
        layer_kernel,
        out_shape=(
            shape(half3, BF),
            shape(half3, BF),
            shape((SHARD, HIDDEN), F32),
            shape((SHARD, HIDDEN), F32),
            shape((SHARD, HIDDEN), F32),
            shape((SHARD, HIDDEN), F32),
            shape((1, WIDTH), F32),
            shape((1, WIDTH), F32),
            shape((2, 16), F32),
        ),
        in_specs=[anym, anym, vmem, vmem, vmem, vmem, vmem, vmem, smem] + [anym] * 7,
        out_specs=(anym,) * 6 + (vmem,) * 3,
        scratch_shapes=scratch,
        compiler_params=pltpu.CompilerParams(
            collective_id=0, has_side_effects=True, vmem_limit_bytes=67043328
        ),
        name="layer",
    )(
        tokens,
        cotangent,
        segment_ids,
        variate_ids,
        time_ids,
        attn_gain.reshape(1, WIDTH),
        ffn_gain.reshape(1, WIDTH),
        freq,
        head_bias,
        w_query,
        w_key,
        w_value,
        w_out.T,
        w_gate,
        w_up,
        w_down.T,
    )
    finals = pl.pallas_call(
        finish_kernel,
        out_shape=(
            shape(half3, BF),
            shape(half3, BF),
            shape((1, WIDTH), F32),
            shape((SHARD, LOCAL), F32),
            shape((SHARD, LOCAL), F32),
            shape((SHARD, LOCAL), F32),
            shape((2, 16), F32),
            shape((SHARD, LOCAL), F32),
            shape((1, WIDTH), F32),
            shape((SHARD, HIDDEN), F32),
            shape((SHARD, HIDDEN), F32),
            shape((SHARD, HIDDEN), F32),
        ),
        in_specs=[anym] * 9,
        out_specs=[anym] * 12,
        scratch_shapes=[
            bf(*half3),
            bf(*half3),
            fl(SHARD, HIDDEN),
            fl(SHARD, HIDDEN),
            fl(SHARD, HIDDEN),
            fl(SHARD, HIDDEN),
            fl(1, WIDTH),
            fl(1, WIDTH),
            fl(2, 16),
            dma((6 * PARTS + 3,)),
            dma((9 * PARTS + 3,)),
        ],
        name="finish",
    )(*outs)
    layer_out, tokens_grad, ga, gq, gk, gv, gb, go, gf, gg, gu, gd = finals
    return (
        layer_out,
        tokens_grad,
        ga.reshape(WIDTH),
        gq,
        gk,
        gv,
        gb,
        go.T,
        gf.reshape(WIDTH),
        gg,
        gu,
        gd.T,
    )


def fits(mesh, tokens, w_query, w_gate):
    sizes = dict(mesh.shape)
    return (
        sizes["fsdp"] == 16
        and sizes["tensor"] == 2
        and tokens.shape == (2, 16 * SEQ_LEN, WIDTH)
        and w_query.shape == (WIDTH, 2 * LOCAL)
        and w_gate.shape == (WIDTH, 2 * HIDDEN)
    )


def solution(mesh):
    placed = (
        P(None, ("fsdp", "tensor"), None),
        P(None, "fsdp"),
        P(None, "fsdp"),
        P(None, "fsdp"),
        P(),
        P("fsdp", "tensor"),
        P("fsdp", "tensor"),
        P("fsdp", "tensor"),
        P(),
        P("tensor", "fsdp"),
        P(),
        P("fsdp", "tensor"),
        P("fsdp", "tensor"),
        P("tensor", "fsdp"),
        P(None, ("fsdp", "tensor"), None),
    )
    outs = (
        P(None, ("fsdp", "tensor"), None),
        P(None, ("fsdp", "tensor"), None),
        P(),
        P("fsdp", "tensor"),
        P("fsdp", "tensor"),
        P("fsdp", "tensor"),
        P(),
        P("tensor", "fsdp"),
        P(),
        P("fsdp", "tensor"),
        P("fsdp", "tensor"),
        P("tensor", "fsdp"),
    )

    def whole(*args):
        body = fused_local if fits(mesh, args[0], args[5], args[11]) else local
        return jax.shard_map(
            body, mesh=mesh, in_specs=placed, out_specs=outs, check_vma=False
        )(*args)

    return whole
```

```python
from functools import partial
from functools import reduce

import jax
import jax.numpy as jnp
import numpy as np
from jax import lax
from jax.experimental import pallas as pl
from jax.experimental.pallas import tpu as pltpu
from jax.sharding import PartitionSpec as P

HEAD_DIM = 64
SEQ_MAX = 1024


EPS = 1e-06


def product(left, right):
    return jnp.dot(left, right, preferred_element_type=jnp.float32)


def product_back(left, right):
    return lax.dot_general(
        left, right, (((1,), (1,)), ((), ())), preferred_element_type=jnp.float32
    )


def outer_sum(left, right):
    return lax.dot_general(
        left, right, (((0,), (0,)), ((), ())), preferred_element_type=jnp.float32
    )


def norm_forward(resid, gain):
    inverse = lax.rsqrt(jnp.mean(resid * resid, axis=-1, keepdims=True) + EPS)
    return (resid * inverse * gain, inverse)


def norm_backward(resid, inverse, gain, upstream):
    scaled = resid * inverse
    weighted = upstream * gain
    back = inverse * (weighted - scaled * jnp.mean(weighted * scaled, axis=-1, keepdims=True))
    return (back, jnp.sum(upstream * scaled, axis=0))


def rope_tables(moments, half_width):
    inverse = 10000.0 ** (-(jnp.arange(half_width, dtype=jnp.float32) / half_width))
    angles = moments.astype(jnp.float32)[:, None] * inverse[None, :]
    return (jnp.cos(angles), jnp.sin(angles))


def rotate(values, cosine, sine):
    half_width = values.shape[-1] // 2
    leading = values[..., :half_width]
    trailing = values[..., half_width:]
    cosine = cosine[:, None, :]
    sine = sine[:, None, :]
    return jnp.concatenate(
        [leading * cosine - trailing * sine, trailing * cosine + leading * sine], axis=-1
    )


def rotate_back(grads, cosine, sine):
    half_width = grads.shape[-1] // 2
    leading = grads[..., :half_width]
    trailing = grads[..., half_width:]
    cosine = cosine[:, None, :]
    sine = sine[:, None, :]
    return jnp.concatenate(
        [leading * cosine + trailing * sine, trailing * cosine - leading * sine], axis=-1
    )


def masked_scores(query, keys, segment, variate, bias_pair):
    scores = jnp.einsum(
        "qhd,khd->hqk", query, keys, preferred_element_type=jnp.float32
    ) * HEAD_DIM ** (-0.5)
    same_variate = variate[:, None] == variate[None, :]
    scores = scores + jnp.where(
        same_variate[None], bias_pair[0][:, None, None], bias_pair[1][:, None, None]
    )
    allowed = segment[:, None] == segment[None, :]
    return (jnp.where(allowed[None], scores, -1e30), same_variate)


def attend_forward(bias_pair, item):
    query, keys, values, segment, variate = item
    scores, unused = masked_scores(query, keys, segment, variate, bias_pair)
    highest = jnp.max(scores, axis=-1, keepdims=True)
    expo = jnp.exp(scores - highest)
    total = jnp.sum(expo, axis=-1, keepdims=True)
    probs = (expo / total).astype(jnp.bfloat16)
    attended = jnp.einsum("hqk,khd->qhd", probs, values, preferred_element_type=jnp.float32)
    return (attended.astype(jnp.bfloat16), (highest + jnp.log(total))[..., 0])


def attend_backward(bias_pair, item):
    query, keys, values, dattended, segment, variate, logsum = item
    scores, same_variate = masked_scores(query, keys, segment, variate, bias_pair)
    probs = jnp.exp(scores - logsum[..., None])
    probs_low = probs.astype(jnp.bfloat16)
    dprobs = jnp.einsum("qhd,khd->hqk", dattended, values, preferred_element_type=jnp.float32)
    dvalues = jnp.einsum("hqk,qhd->khd", probs_low, dattended, preferred_element_type=jnp.float32)
    dscores = (probs * (dprobs - jnp.sum(probs * dprobs, axis=-1, keepdims=True))).astype(
        jnp.bfloat16
    )
    widened = dscores.astype(jnp.float32)
    same_sum = jnp.sum(jnp.where(same_variate[None], widened, 0.0), axis=(1, 2))
    other_sum = jnp.sum(jnp.where(same_variate[None], 0.0, widened), axis=(1, 2))
    dquery = jnp.einsum(
        "hqk,khd->qhd", dscores, keys, preferred_element_type=jnp.float32
    ) * HEAD_DIM ** (-0.5)
    dkeys = jnp.einsum(
        "hqk,qhd->khd", dscores, query, preferred_element_type=jnp.float32
    ) * HEAD_DIM ** (-0.5)
    return (dquery, dkeys, dvalues, jnp.stack([same_sum, other_sum]))


def local(
    tokens,
    segment_ids,
    variate_ids,
    time_ids,
    attn_gain,
    w_query,
    w_key,
    w_value,
    head_bias,
    w_out,
    ffn_gain,
    w_gate,
    w_up,
    w_down,
    cotangent,
):
    micro_count, row_count, model_width = tokens.shape
    group_rows = segment_ids.shape[1]
    seq_len = min(SEQ_MAX, group_rows)
    seq_count = group_rows // seq_len
    local_width = w_query.shape[1]
    local_heads = local_width // HEAD_DIM
    head_start = lax.axis_index("tensor") * local_heads
    bias_pair = lax.dynamic_slice_in_dim(head_bias, head_start, local_heads, 1)
    shards = (w_query, w_key, w_value, w_out, w_gate, w_up, w_down)
    heads_shape = (group_rows, local_heads, HEAD_DIM)
    seq_shape = (seq_count, seq_len, local_heads, HEAD_DIM)

    def spread_normed(block):
        return lax.all_gather(block, "tensor", axis=0, tiled=True)

    def spread_grads(block):
        return lax.all_gather(block, "tensor", axis=0, tiled=True)

    def branch_rows(left, right):
        return lax.psum_scatter(product(left, right), "tensor", scatter_dimension=0, tiled=True)

    def back_rows(lefts, rights):
        pieces = [product_back(left, right) for left, right in zip(lefts, rights)]
        return lax.psum_scatter(reduce(jnp.add, pieces), "tensor", scatter_dimension=0, tiled=True)

    outputs = []
    input_grads = []
    grad_shards = None
    gain_first = jnp.zeros((model_width,), jnp.float32)
    gain_second = jnp.zeros((model_width,), jnp.float32)
    bias_grad = jnp.zeros((2, local_heads), jnp.float32)
    for micro_index in range(micro_count):
        full_weights = (
            lax.all_gather(shards[0], "fsdp", axis=0, tiled=True),
            lax.all_gather(shards[1], "fsdp", axis=0, tiled=True),
            lax.all_gather(shards[2], "fsdp", axis=0, tiled=True),
            lax.all_gather(shards[3], "fsdp", axis=1, tiled=True),
            lax.all_gather(shards[4], "fsdp", axis=0, tiled=True),
            lax.all_gather(shards[5], "fsdp", axis=0, tiled=True),
            lax.all_gather(shards[6], "fsdp", axis=1, tiled=True),
        )
        query_full, key_full, value_full, out_full, gate_full, up_full, down_full = full_weights
        resid = tokens[micro_index].astype(jnp.float32)
        segment = segment_ids[micro_index].reshape(seq_count, seq_len)
        variate = variate_ids[micro_index].reshape(seq_count, seq_len)
        cosine, sine = rope_tables(time_ids[micro_index], HEAD_DIM // 2)
        normed, inverse_first = norm_forward(resid, attn_gain)
        normed_all = spread_normed(normed.astype(jnp.bfloat16))
        query = rotate(product(normed_all, query_full).reshape(heads_shape), cosine, sine).astype(
            jnp.bfloat16
        )
        keys = rotate(product(normed_all, key_full).reshape(heads_shape), cosine, sine).astype(
            jnp.bfloat16
        )
        values = product(normed_all, value_full).astype(jnp.bfloat16)
        query_seq = query.reshape(seq_shape)
        keys_seq = keys.reshape(seq_shape)
        values_seq = values.reshape(seq_shape)
        attended, logsum = lax.map(
            partial(attend_forward, bias_pair), (query_seq, keys_seq, values_seq, segment, variate)
        )
        attended = attended.reshape(group_rows, local_width)
        middle = resid + branch_rows(attended, out_full)
        normed_ffn, inverse_second = norm_forward(middle, ffn_gain)
        normed_ffn_all = spread_normed(normed_ffn.astype(jnp.bfloat16))
        gate = product(normed_ffn_all, gate_full)
        upward = product(normed_ffn_all, up_full)
        sigmoid = jax.nn.sigmoid(gate)
        hidden = (gate * sigmoid * upward).astype(jnp.bfloat16)
        outputs.append((middle + branch_rows(hidden, down_full)).astype(jnp.bfloat16))
        full_weights = (
            lax.all_gather(shards[0], "fsdp", axis=0, tiled=True),
            lax.all_gather(shards[1], "fsdp", axis=0, tiled=True),
            lax.all_gather(shards[2], "fsdp", axis=0, tiled=True),
            lax.all_gather(shards[3], "fsdp", axis=1, tiled=True),
            lax.all_gather(shards[4], "fsdp", axis=0, tiled=True),
            lax.all_gather(shards[5], "fsdp", axis=0, tiled=True),
            lax.all_gather(shards[6], "fsdp", axis=1, tiled=True),
        )
        query_full, key_full, value_full, out_full, gate_full, up_full, down_full = full_weights
        grad_out = cotangent[micro_index].astype(jnp.float32)
        grad_ffn_all = spread_grads(cotangent[micro_index])
        dhidden = product_back(grad_ffn_all, down_full)
        dgate = (dhidden * upward * (sigmoid + gate * sigmoid * (1.0 - sigmoid))).astype(
            jnp.bfloat16
        )
        dupward = (dhidden * gate * sigmoid).astype(jnp.bfloat16)
        dnormed_ffn = back_rows((dgate, dupward), (gate_full, up_full))
        grad_gate = outer_sum(normed_ffn_all, dgate)
        grad_up = outer_sum(normed_ffn_all, dupward)
        grad_down = outer_sum(hidden, grad_ffn_all)
        dmiddle, gain_term = norm_backward(middle, inverse_second, ffn_gain, dnormed_ffn)
        gain_second = gain_second + gain_term
        dmiddle = dmiddle + grad_out
        grad_attn_all = spread_grads(dmiddle.astype(jnp.bfloat16))
        dattended = product_back(grad_attn_all, out_full).astype(jnp.bfloat16)
        grad_out_proj = outer_sum(attended, grad_attn_all)
        back_items = (
            query_seq,
            keys_seq,
            values_seq,
            dattended.reshape(seq_shape),
            segment,
            variate,
            logsum,
        )
        dquery, dkeys, dvalues, bias_terms = lax.map(
            partial(attend_backward, bias_pair), back_items
        )
        bias_grad = bias_grad + jnp.sum(bias_terms, axis=0)
        dquery = (
            rotate_back(dquery.reshape(heads_shape), cosine, sine)
            .astype(jnp.bfloat16)
            .reshape(group_rows, local_width)
        )
        dkeys = (
            rotate_back(dkeys.reshape(heads_shape), cosine, sine)
            .astype(jnp.bfloat16)
            .reshape(group_rows, local_width)
        )
        dvalues = dvalues.astype(jnp.bfloat16).reshape(group_rows, local_width)
        dnormed = back_rows((dquery, dkeys, dvalues), (query_full, key_full, value_full))
        grad_query = outer_sum(normed_all, dquery)
        grad_key = outer_sum(normed_all, dkeys)
        grad_value = outer_sum(normed_all, dvalues)
        dresid, gain_term = norm_backward(resid, inverse_first, attn_gain, dnormed)
        gain_first = gain_first + gain_term
        input_grads.append((dresid + dmiddle).astype(jnp.bfloat16))
        summed = (
            lax.psum_scatter(
                grad_query.astype(jnp.bfloat16), "fsdp", scatter_dimension=0, tiled=True
            ).astype(jnp.float32),
            lax.psum_scatter(
                grad_key.astype(jnp.bfloat16), "fsdp", scatter_dimension=0, tiled=True
            ).astype(jnp.float32),
            lax.psum_scatter(
                grad_value.astype(jnp.bfloat16), "fsdp", scatter_dimension=0, tiled=True
            ).astype(jnp.float32),
            lax.psum_scatter(
                grad_out_proj.astype(jnp.bfloat16), "fsdp", scatter_dimension=1, tiled=True
            ).astype(jnp.float32),
            lax.psum_scatter(
                grad_gate.astype(jnp.bfloat16), "fsdp", scatter_dimension=0, tiled=True
            ).astype(jnp.float32),
            lax.psum_scatter(
                grad_up.astype(jnp.bfloat16), "fsdp", scatter_dimension=0, tiled=True
            ).astype(jnp.float32),
            lax.psum_scatter(
                grad_down.astype(jnp.bfloat16), "fsdp", scatter_dimension=1, tiled=True
            ).astype(jnp.float32),
        )
        grad_shards = summed if grad_shards is None else jax.tree.map(jnp.add, grad_shards, summed)
    bias_full = lax.dynamic_update_slice_in_dim(
        jnp.zeros((2, head_bias.shape[1]), jnp.float32), bias_grad, head_start, 1
    )
    gain_first, gain_second, bias_full = lax.psum(
        (gain_first, gain_second, bias_full), ("fsdp", "tensor")
    )
    return (
        jnp.stack(outputs),
        jnp.stack(input_grads),
        gain_first,
        grad_shards[0],
        grad_shards[1],
        grad_shards[2],
        bias_full,
        grad_shards[3],
        gain_second,
        grad_shards[4],
        grad_shards[5],
        grad_shards[6],
    )


BF = jnp.bfloat16
F32 = jnp.float32
MESH = pl.DeviceIdType.MESH
SHARD = 64
SEQ_LEN = 256
HALF = 128
WIDTH = 1024
LOCAL = 512
HIDDEN = 2048
PAIRS = 4
COL_QKV, COL_OUT, COL_GATE, COL_UP, COL_DOWN = 0, 1536, 2048, 4096, 6144
ALL_COLS = 8192
LOAD_COLS = (0, 512, 1024, COL_OUT, COL_GATE, COL_UP, COL_DOWN)
LOAD_ENDS = LOAD_COLS[1:] + (ALL_COLS,)
GATHER = (
    (0, 512, False, False, True),
    (512, 512, False, False, True),
    (1024, 512, False, False, True),
    (1536, 512, False, False, True),
    (2048, 512, False, False, True),
    (2560, 512, False, False, False),
    (3072, 512, False, False, False),
    (3584, 512, False, False, False),
    (4096, 512, False, False, False),
    (4608, 512, False, False, False),
    (5120, 512, False, False, False),
    (5632, 512, False, False, False),
    (6144, 512, True, False, False),
    (6656, 512, True, False, False),
    (7168, 512, True, False, False),
    (7680, 512, True, False, False),
)
CHUNK = 2048
SCATTER = (
    (0, 0, 512, False, False, False),
    (0, 512, 512, False, False, False),
    (0, 1024, 512, False, False, False),
    (0, 1536, 512, False, False, False),
    (1, 0, 512, False, False, False),
    (1, 512, 512, False, False, False),
    (1, 1024, 512, False, False, False),
    (1, 1536, 512, True, False, False),
    (2, 0, 512, False, False, True),
    (2, 512, 512, False, False, True),
    (2, 1024, 512, False, False, True),
    (2, 1536, 512, False, False, True),
    (3, 0, 512, False, False, True),
    (3, 512, 512, False, False, True),
    (3, 1024, 512, False, False, True),
    (3, 1536, 512, False, True, True),
)
NORMAL_COLS = sum(piece[2] for piece in SCATTER if not piece[3])
TURNED_COLS = max(128, sum(piece[2] for piece in SCATTER if piece[3]))
FIRST = 5
DEPTH = 5
(
    START,
    TABLES,
    NORM,
    PROJECT,
    ATTEND,
    PROJECT_OUT,
    MIDDLE,
    GATE_TILES,
    UP_TILES,
    TURN_COTANGENT,
    TURN_FFN,
    TURN_NORMED,
    TURN_MIDDLE,
    HIDDEN_BACK,
    LAST_PRODUCT,
    GATHER_SENT,
    FFN_BACK,
    OUT_SEND,
    MIDDLE_BACK,
    ATTEND_BACK,
    NORM_BACK,
    OUT_ROWS,
    TOKEN_ROWS,
    SUM_START,
    SUM_STAGE,
    GATHER_Z,
    GATHER_CORE,
    WEIGHT_GRAD,
    SCATTER_X,
    SCATTER_Z,
    SCATTER_PASS,
    SCATTER_END,
    TURNED_X,
    TURNED_END,
    SCATTER_OWN,
) = range(35)
PROGRAM = (
    (START, 0),
    (GATHER_Z, 0),
    (GATHER_Z, 1),
    (NORM, 0),
    (TABLES, 0),
    (GATHER_Z, 2),
    (GATHER_Z, 3),
    (GATHER_CORE, 0),
    (GATHER_Z, 4),
    (TURN_COTANGENT, 0),
    (PROJECT, 0),
    (GATHER_CORE, 1),
    (GATHER_Z, 5),
    (GATHER_CORE, 2),
    (PROJECT, 2),
    (GATHER_Z, 6),
    (PROJECT, 1),
    (GATHER_CORE, 3),
    (GATHER_Z, 7),
    (ATTEND, 0),
    (PROJECT_OUT, 0),
    (GATHER_CORE, 4),
    (ATTEND, 1),
    (PROJECT_OUT, 1),
    (GATHER_CORE, 5),
    (GATHER_Z, 8),
    (GATHER_Z, 9),
    (GATHER_CORE, 6),
    (GATHER_Z, 10),
    (GATHER_CORE, 7),
    (GATHER_CORE, 8),
    (GATHER_Z, 11),
    (MIDDLE, 0),
    (MIDDLE, 1),
    (GATE_TILES, 1),
    (GATHER_Z, 12),
    (GATE_TILES, 0),
    (GATHER_CORE, 9),
    (TURN_FFN, 0),
    (UP_TILES, 0),
    (WEIGHT_GRAD, 1),
    (GATHER_CORE, 10),
    (GATHER_Z, 13),
    (WEIGHT_GRAD, 0),
    (SCATTER_X, 1),
    (SCATTER_X, 0),
    (GATHER_Z, 14),
    (GATHER_CORE, 11),
    (HIDDEN_BACK, 0),
    (UP_TILES, 1),
    (GATHER_Z, 15),
    (WEIGHT_GRAD, 2),
    (SCATTER_Z, 1),
    (WEIGHT_GRAD, 3),
    (HIDDEN_BACK, 1),
    (SCATTER_X, 2),
    (FFN_BACK, 0),
    (SCATTER_Z, 0),
    (SCATTER_X, 3),
    (GATHER_SENT, 0),
    (LAST_PRODUCT, 0),
    (WEIGHT_GRAD, 4),
    (SCATTER_Z, 2),
    (WEIGHT_GRAD, 7),
    (SCATTER_X, 4),
    (WEIGHT_GRAD, 5),
    (SCATTER_X, 7),
    (FFN_BACK, 1),
    (SCATTER_X, 5),
    (WEIGHT_GRAD, 11),
    (SCATTER_PASS, 1),
    (WEIGHT_GRAD, 8),
    (MIDDLE_BACK, 0),
    (SCATTER_X, 8),
    (SCATTER_Z, 3),
    (WEIGHT_GRAD, 10),
    (SCATTER_PASS, 0),
    (WEIGHT_GRAD, 9),
    (WEIGHT_GRAD, 6),
    (SCATTER_Z, 4),
    (SCATTER_X, 11),
    (ATTEND_BACK, 0),
    (SCATTER_X, 10),
    (SCATTER_X, 9),
    (SCATTER_Z, 5),
    (MIDDLE_BACK, 1),
    (SCATTER_Z, 8),
    (SCATTER_PASS, 7),
    (TURN_NORMED, 0),
    (NORM_BACK, 0),
    (SCATTER_X, 6),
    (SCATTER_Z, 11),
    (ATTEND_BACK, 1),
    (SCATTER_PASS, 3),
    (WEIGHT_GRAD, 14),
    (SCATTER_PASS, 2),
    (TURN_MIDDLE, 0),
    (SCATTER_X, 14),
    (SCATTER_OWN, 11),
    (SCATTER_OWN, 9),
    (SCATTER_Z, 10),
    (SCATTER_Z, 9),
    (SCATTER_PASS, 4),
    (NORM_BACK, 1),
    (SCATTER_PASS, 5),
    (WEIGHT_GRAD, 15),
    (WEIGHT_GRAD, 12),
    (SCATTER_END, 0),
    (SCATTER_Z, 6),
    (WEIGHT_GRAD, 13),
    (TOKEN_ROWS, 0),
    (SCATTER_X, 15),
    (SCATTER_X, 13),
    (SCATTER_Z, 14),
    (SCATTER_PASS, 8),
    (SCATTER_X, 12),
    (TOKEN_ROWS, 1),
    (SCATTER_PASS, 10),
    (SCATTER_END, 4),
    (SCATTER_END, 5),
    (SCATTER_END, 3),
    (SCATTER_END, 1),
    (SUM_START, 0),
    (SCATTER_PASS, 11),
    (OUT_SEND, 0),
    (SCATTER_OWN, 10),
    (SUM_STAGE, 0),
    (SCATTER_OWN, 8),
    (SCATTER_Z, 15),
    (SCATTER_Z, 13),
    (OUT_ROWS, 0),
    (SCATTER_OWN, 15),
    (SCATTER_PASS, 6),
    (SCATTER_PASS, 14),
    (SCATTER_PASS, 9),
    (SCATTER_Z, 12),
    (TURNED_X, 7),
    (SCATTER_OWN, 14),
    (SUM_STAGE, 1),
    (SCATTER_END, 10),
    (SCATTER_PASS, 13),
    (SCATTER_END, 11),
    (SCATTER_END, 8),
    (SCATTER_PASS, 15),
    (SCATTER_OWN, 13),
    (SCATTER_END, 2),
    (SCATTER_OWN, 12),
    (SCATTER_END, 6),
    (SCATTER_PASS, 12),
    (SCATTER_END, 15),
    (SUM_STAGE, 2),
    (SCATTER_END, 14),
    (SCATTER_END, 13),
    (SCATTER_END, 9),
    (TURNED_END, 7),
    (SUM_STAGE, 3),
    (SCATTER_END, 12),
)
WEIGHT_ORDER = [p for step, p in PROGRAM if step == WEIGHT_GRAD]
CORE_ORDER = [p for step, p in PROGRAM if step == SCATTER_X]
FIRST_QUERY = [p for p in WEIGHT_ORDER if SCATTER[p][0] == 3][0]
LAST_DOWN = [p for p in CORE_ORDER if SCATTER[p][0] == 0][-1]
PARTS = 1
NEGATIVE = -1e30


def mm(left, right):
    return jnp.dot(left, right, preferred_element_type=F32)


def mm_nt(left, right):
    return lax.dot_general(left, right, (((1,), (1,)), ((), ())), preferred_element_type=F32)


def mm_tn(left, right):
    return lax.dot_general(left, right, (((0,), (0,)), ((), ())), preferred_element_type=F32)


def layer_kernel(
    tok_ref,
    cot_in,
    seg_ref,
    var_ref,
    time_ref,
    again_ref,
    fgain_ref,
    freq_ref,
    bias_ref,
    wq_ref,
    wk_ref,
    wv_ref,
    wo_ref,
    wg_ref,
    wu_ref,
    wd_ref,
    out_hbm,
    tgrad_hbm,
    gqkvo_hbm,
    gg_hbm,
    gu_hbm,
    gd_hbm,
    ga_ref,
    gf_ref,
    gb_ref,
    out_ref,
    tgrad_ref,
    RES,
    W,
    GD,
    RC,
    RX,
    RZ,
    RL,
    RXS,
    RZS,
    RLS,
    X,
    COT,
    N1,
    NF,
    Q,
    K,
    V,
    ATT,
    PT,
    MID,
    GT,
    UP,
    HID,
    YS,
    YR,
    YDS,
    YDR,
    YNR,
    T,
    T2,
    OUTM,
    DML,
    SAME,
    NEGM,
    COS,
    SIN,
    GF,
    GA,
    BS,
    SV,
    SR,
    local_sem,
    ag_send,
    ag_recv,
    rs_send,
    rs_recv,
    y_send,
    y_recv,
    sv_send,
    sv_recv,
    credit,
    core_credit,
    flush_sem,
):
    f = lax.axis_index("fsdp")
    y = lax.axis_index("tensor")
    z, x, c = f // 4, (f // 2) % 2, f % 2
    zs = (z + 1 - 2 * (z % 2), (z + 2) % 4, 3 - z)
    z_devs = [(zk * 4 + x * 2 + c, y) for zk in zs]
    x_dev = (z * 4 + (1 - x) * 2 + c, y)
    c_dev = (z * 4 + x * 2 + 1 - c, y)
    y_dev = (f, 1 - y)
    partners = z_devs + [x_dev, c_dev, y_dev]

    def remote(src, dst, send, recv, dev):
        return pltpu.make_async_remote_copy(
            src_ref=src, dst_ref=dst, send_sem=send, recv_sem=recv, device_id=dev, device_id_type=MESH
        )

    barrier = pltpu.get_barrier_semaphore()
    for dev in partners:
        pl.semaphore_signal(barrier, inc=1, device_id=dev, device_id_type=MESH)
    own_rows = pl.ds(pl.multiple_of(y * HALF, HALF), HALF)
    other_rows = pl.ds(pl.multiple_of((1 - y) * HALF, HALF), HALF)
    loads = [
        (tok_ref, X.at[:, own_rows]),
        (cot_in, COT.at[:, own_rows]),
        (wq_ref, W.at[z, x, c, :, pl.ds(0, LOCAL)]),
        (wk_ref, W.at[z, x, c, :, pl.ds(LOCAL, LOCAL)]),
        (wv_ref, W.at[z, x, c, :, pl.ds(2 * LOCAL, LOCAL)]),
        (wo_ref, W.at[z, x, c, :, pl.ds(COL_OUT, LOCAL)]),
        (wg_ref, W.at[z, x, c, :, pl.ds(COL_GATE, HIDDEN)]),
        (wu_ref, W.at[z, x, c, :, pl.ds(COL_UP, HIDDEN)]),
        (wd_ref, W.at[z, x, c, :, pl.ds(COL_DOWN, HIDDEN)]),
    ]
    loads = [
        pltpu.make_async_copy(src, dst, local_sem.at[i]) for i, (src, dst) in enumerate(loads)
    ]
    for load in loads:
        load.start()
    loaded = set()

    def load_wait(*which):
        for i in which:
            if i not in loaded:
                loaded.add(i)
                loads[i].wait()

    pl.semaphore_wait(barrier, len(partners))
    middle = ((z + 1) // 2) % 2 == 1
    edge = ((z + 1) // 2) % 2 == 0

    ag_own, ag_pass, ag_x, ag_c = [], [], [], []
    for i, (c0, n, turned, straight, early) in enumerate(GATHER):
        cols = pl.ds(c0, n)

        def block(zi):
            if turned:
                return W.at[zi, :, c, :, cols]
            return W.at[zi, x, c, :, cols]

        at = i * 9
        ag_own.append(
            [
                remote(block(z), block(z), ag_send.at[at + k], ag_recv.at[at + k], z_devs[k])
                for k in range(3)
            ]
        )
        ag_pass.append(
            [
                remote(
                    block(zs[k]),
                    block(zs[k]),
                    ag_send.at[at + (0, 3, 1)[k]],
                    ag_recv.at[at + 3 - k],
                    z_devs[0],
                )
                for k in (1, 2)
            ]
        )
        part = W.at[z, x, c, :, cols] if turned else W.at[:, x, c, :, cols]
        if early:
            parts = [block(zi) for zi in (z, *zs)]
        else:
            parts = [part]
        ag_x.append(
            [
                remote(part, part, ag_send.at[at + k], ag_recv.at[at + k], x_dev)
                for k, part in zip((4, 6, 7, 8), parts)
            ]
        )
        part = W.at[:, :, c, :, cols]
        ag_c.append(remote(part, part, ag_send.at[at + 5], ag_recv.at[at + 5], c_dev))

    def own_load(i):
        c0, n = GATHER[i][:2]
        for k, base in enumerate(LOAD_COLS):
            if base < c0 + n and c0 < LOAD_ENDS[k]:
                load_wait(2 + k)

    def gather_own(i):
        own_load(i)
        if GATHER[i][2]:
            ag_x[i][0].wait_recv()
        ag_own[i][0].start()
        if GATHER[i][3]:
            ag_own[i][1].start()
            ag_own[i][2].start()
            return

        @pl.when(edge)
        def _():
            ag_own[i][1].start()

        @pl.when(middle)
        def _():
            ag_own[i][2].start()

    def gather_z(i):
        if GATHER[i][3]:
            ag_own[i][1].wait_recv()
        else:

            @pl.when(middle)
            def _():
                for k in (1, 2):
                    ag_own[i][k].wait_recv()
                    ag_pass[i][k - 1].start()

        for k in range(max(FIRST, i + DEPTH if i else FIRST), min(i + DEPTH + 1, len(GATHER))):
            gather_own(k)
        ag_own[i][0].wait_recv()
        if GATHER[i][3]:
            ag_own[i][2].wait_recv()
        else:

            @pl.when(edge)
            def _():
                ag_own[i][1].wait_recv()
                ag_own[i][2].wait_recv()

        if GATHER[i][2]:
            ag_c[i].start()
        else:
            for copy in ag_x[i][1 if GATHER[i][4] else 0 :]:
                copy.start()

    def gather_c(i):
        for copy in ag_x[i]:
            copy.wait_recv()
        ag_c[i].start()

    ended = set()

    def gather_end(c0, n):
        for i, (start_col, size, *_) in enumerate(GATHER):
            if start_col < c0 + n and c0 < start_col + size and i not in ended:
                ended.add(i)
                ag_c[i].wait_recv()

    y_tok = remote(X.at[:, own_rows], X.at[:, own_rows], y_send.at[0], y_recv.at[0], y_dev)
    y_cot = remote(COT.at[:, own_rows], COT.at[:, own_rows], y_send.at[1], y_recv.at[1], y_dev)

    def start():
        for i in range(FIRST):
            gather_own(i)
        for i in range(len(GATHER)):
            if GATHER[i][2] or GATHER[i][4]:
                own_load(i)
                ag_x[i][0].start()
        load_wait(0)
        y_tok.start()
        load_wait(1)
        y_cot.start()

        @pl.when(edge)
        def _():
            for p, (_, _, n, turned, straight, _) in enumerate(SCATTER):
                spot = sum(piece[2] for piece in SCATTER[:p] if piece[3] == turned)
                if turned and not straight:
                    RZS[2, :, :, pl.ds(spot, n)] = jnp.zeros((2, SHARD, n), BF)
                elif not straight:
                    RZ[2, :, pl.ds(spot, n)] = jnp.zeros((SHARD, n), BF)

    lane = lax.broadcasted_iota(jnp.int32, (1, 128), 1)
    low_lane = lane < 64
    lead_lane = (lane % 64) < 32

    def column(row):
        return jnp.transpose(jnp.broadcast_to(row.astype(F32), (128, SEQ_LEN)))

    def tables():
        for s in range(2):
            moments = column(time_ref[s : s + 1, :])
            angles = moments * freq_ref[...]
            COS[s] = jnp.cos(angles)
            sine = jnp.sin(angles)
            SIN[s] = jnp.where(lead_lane, -sine, sine)
            seg_row = seg_ref[s : s + 1, :].astype(F32)
            var_row = var_ref[s : s + 1, :].astype(F32)
            seg_col = column(seg_ref[s : s + 1, :])
            var_col = column(var_ref[s : s + 1, :])
            for h in range(2):
                part = slice(h * 128, (h + 1) * 128)
                SAME[s, :, part] = jnp.where(var_col == var_row[:, part], 1.0, 0.0)
                NEGM[s, :, part] = jnp.where(seg_col == seg_row[:, part], 0.0, NEGATIVE)

    def swap(values):
        return jnp.where(
            lead_lane, pltpu.roll(values, 96, axis=1), pltpu.roll(values, 32, axis=1)
        )

    ROWS = 64
    BLOCKS = SEQ_LEN // ROWS

    def row_loop(body):
        def step(b, carry):
            body(b, pl.ds(pl.multiple_of(b * ROWS, ROWS), ROWS))
            return carry

        lax.fori_loop(0, BLOCKS, step, 0)

    def tile_loop(count, body):
        def step(j, carry):
            body(j)
            return carry

        lax.fori_loop(0, count, step, 0)

    def tile_cols(base, j, size=256):
        return pl.ds(pl.multiple_of(base + j * size, size), size)

    def w_tile(cols):
        return W[:, :, :, :, cols].reshape(WIDTH, 256)

    def w_rows(zi, c0, n):
        return W[zi, :, :, :, pl.ds(c0, n)].reshape(256, n)

    def transpose_into(src, T):
        for s in range(2):

            def body(j):
                cols = tile_cols(0, j)
                T[cols, s * SEQ_LEN : (s + 1) * SEQ_LEN] = jnp.transpose(src[s, :, cols])

            tile_loop(4, body)

    def norm():
        y_tok.wait_recv()
        for s in range(2):

            def body(b, rows):
                v = X[s, rows, :].astype(F32)
                inv = lax.rsqrt(jnp.mean(v * v, axis=-1, keepdims=True) + EPS)
                N1[s, rows, :] = (v * inv * again_ref[...]).astype(BF)

            row_loop(body)

    def project(kind):
        gather_end(kind * LOCAL, LOCAL)
        dest = (Q, K, V)[kind]

        def body(j):
            r = mm(N1[...].reshape(2 * SEQ_LEN, WIDTH), w_tile(tile_cols(kind * LOCAL, j)))
            for h in range(2):
                part = r[:, h * 128 : (h + 1) * 128]
                if kind < 2:
                    cosine = COS[...].reshape(2 * SEQ_LEN, 128)
                    sine = SIN[...].reshape(2 * SEQ_LEN, 128)
                    part = part * cosine + swap(part) * sine
                dest[:, :, pl.ds(pl.multiple_of(j * 256 + h * 128, 128), 128)] = part.astype(
                    BF
                ).reshape(2, SEQ_LEN, 128)

        tile_loop(2, body)

    def stacked(values):
        zero = jnp.zeros_like(values)
        return jnp.concatenate(
            [jnp.where(low_lane, values, zero), jnp.where(low_lane, zero, values)], axis=0
        )

    def pair_cols(p):
        return pl.ds(pl.multiple_of(p * 128, 128), 128)

    y_att = [
        remote(YS.at[s], YR.at[s], y_send.at[2 + s], y_recv.at[2 + s], y_dev) for s in range(2)
    ]
    def attend(s):
        def body(p):
            cols = pair_cols(p)
            keys = stacked(K[s, :, cols] * jnp.asarray(0.125, BF))
            scores = mm_nt(keys, Q[s, :, cols])
            parts = []
            for h in range(2):
                head = y * 8 + p * 2 + h
                same_bias = bias_ref[0, head]
                other_bias = bias_ref[1, head]
                sc = scores[h * SEQ_LEN : (h + 1) * SEQ_LEN]
                sc = sc + (SAME[s] * (same_bias - other_bias) + (NEGM[s] + other_bias))
                top = jnp.max(sc, axis=0, keepdims=True)
                expo = jnp.exp(sc - top)
                total = jnp.sum(expo, axis=0, keepdims=True)
                parts.append((expo * (1.0 / total)).astype(BF))
            probs = jnp.concatenate(parts, axis=0)
            PT[s * PAIRS + p] = probs
            ATT[s, :, cols] = mm_tn(probs, stacked(V[s, :, cols])).astype(BF)

        tile_loop(PAIRS, body)

    def project_out(s):
        if s == 0:
            gather_end(COL_OUT, LOCAL)
        for zi in range(4):
            YS[s, :, zi * 256 : (zi + 1) * 256] = mm_nt(
                ATT[s], w_rows(zi, COL_OUT, LOCAL)
            ).astype(BF)
        y_att[s].start()

    def middle_rows(s):
        y_att[s].wait_recv()

        def body(b, rows):
            v = X[s, rows, :].astype(F32) + (YS[s, rows, :].astype(F32) + YR[s, rows, :].astype(F32))
            MID[s, rows, :] = v
            inv = lax.rsqrt(jnp.mean(v * v, axis=-1, keepdims=True) + EPS)
            NF[s, rows, :] = (v * inv * fgain_ref[...]).astype(BF)

        row_loop(body)
        if s == 1:
            for k in range(2):
                y_att[k].wait_send()
            pl.semaphore_signal(credit, inc=1, device_id=y_dev, device_id_type=MESH)

    def gate_tiles(half):
        gather_end(COL_GATE + half * 1024, 1024)

        def body(j):
            cols = tile_cols(half * 1024, j)
            GT[:, cols] = mm(
                NF[...].reshape(2 * SEQ_LEN, WIDTH), w_tile(tile_cols(COL_GATE + half * 1024, j))
            ).astype(BF)

        tile_loop(4, body)

    def up_tiles(half):
        gather_end(COL_UP + half * 1024, 1024)

        def body(j):
            cols = tile_cols(half * 1024, j)
            up = mm(
                NF[...].reshape(2 * SEQ_LEN, WIDTH), w_tile(tile_cols(COL_UP + half * 1024, j))
            )
            UP[:, cols] = up.astype(BF)
            gate = GT[:, cols].astype(F32)
            HID[:, cols] = (gate * jax.nn.sigmoid(gate) * up).astype(BF)

        tile_loop(4, body)

    def turn_cotangent():
        y_cot.wait_recv()
        transpose_into(COT, T)

    homes = ((GD, 0), (W, COL_DOWN), (W, COL_GATE), (W, COL_UP))
    results = tuple(RES.at[ch] for ch in range(4))
    result_homes = (gd_hbm, gg_hbm, gu_hbm, gqkvo_hbm)
    flushes = []

    def flush(src, dst):
        copy = pltpu.make_async_copy(src, dst, flush_sem.at[len(flushes)])
        copy.start()
        flushes.append(copy)

    def flush_result(p):
        ch, c0, n = SCATTER[p][:3]
        cols = pl.ds(c0, n)
        flush(results[ch].at[:, cols], result_homes[ch].at[:, cols])


    def home(ch, *index, c0=0, n=CHUNK):
        ref, base = homes[ch]
        return ref.at[index + (slice(None), pl.ds(base + c0, n))]

    every = slice(None)
    slots = (0, 1, 2, 0)
    rs_c, rs_x, rs_z, rs_relay = [], [], [], []
    spots = []
    for p, (ch, c0, n, turned, straight, late) in enumerate(SCATTER):
        spot = sum(piece[2] for piece in SCATTER[:p] if piece[3] == turned)
        spots.append(spot)
        at = p * 9

        def sems(k):
            return rs_send.at[at + k], rs_recv.at[at + k]

        rs_c.append(
            remote(
                home(ch, every, every, 1 - c, c0=c0, n=n),
                RC.at[slots[ch], :, :, :, pl.ds(c0, n)],
                *sems(0),
                c_dev,
            )
        )
        cols = pl.ds(spot, n)
        if turned:
            rs_x.append(
                [remote(home(ch, z, 1 - x, c, c0=c0, n=n), RXS.at[:, cols], *sems(1), x_dev)]
            )
            views = [home(ch, zk, every, c, c0=c0, n=n) for zk in zs]
            boxes, relay = [RZS.at[k, :, :, cols] for k in range(3)], RLS.at[:, :, cols]
        else:
            blocks = (*zs, z) if late else (every,)
            rs_x.append(
                [
                    remote(
                        home(ch, zi, 1 - x, c, c0=c0, n=n), RX.at[zi, :, cols], *sems(k), x_dev
                    )
                    for k, zi in zip((1, 6, 7, 8), blocks)
                ]
            )
            views = [home(ch, zk, x, c, c0=c0, n=n) for zk in zs]
            boxes, relay = [RZ.at[k, :, cols] for k in range(3)], RL.at[:, cols]
        rs_z.append(
            [remote(views[k], boxes[k], *sems(2 + k), z_devs[k]) for k in range(3)]
        )
        rs_relay.append(remote(views[2], relay, *sems(5), z_devs[0]))

    def add_core(p, xi):
        ch, c0, n, turned, straight, late = SCATTER[p]

        def body(zi):
            view = home(ch, zi, xi, c, c0=c0, n=n)
            view[...] = view[...] + RC[slots[ch], zi, xi, :, pl.ds(c0, n)]

        tile_loop(4, body)

    def send_z(p):
        rs_z[p][0].start()
        if SCATTER[p][4]:
            rs_z[p][1].start()
            rs_z[p][2].start()
            return

        @pl.when(middle)
        def _():
            rs_z[p][2].start()

        @pl.when(edge)
        def _():
            rs_z[p][1].start()
            rs_relay[p].start()

    def scatter_x(p):
        rs_c[p].wait_recv()
        add_core(p, 1 - x)
        if SCATTER[p][3]:
            add_core(p, x)
            send_z(p)
        else:
            for copy in rs_x[p][:3]:
                copy.start()
            add_core(p, x)
        if p == LAST_DOWN:
            pl.semaphore_signal(core_credit, inc=1, device_id=c_dev, device_id_type=MESH)

    def scatter_z(p):
        ch, c0, n, turned, straight, late = SCATTER[p]
        for copy in rs_x[p][:3]:
            copy.wait_recv()

        def body(zi):
            view = home(ch, zi, x, c, c0=c0, n=n)
            view[...] = view[...] + RX[zi, :, pl.ds(spots[p], n)]

        if late:
            for zi in zs:
                body(zi)
        else:
            tile_loop(4, body)
        send_z(p)

    def scatter_own(p):
        rs_x[p][3].start()

    def scatter_pass(p):
        ch, c0, n, turned, straight, late = SCATTER[p]
        if straight:
            return

        @pl.when(middle)
        def _():
            rs_relay[p].wait_recv()
            if turned:
                view = home(ch, zs[1], every, c, c0=c0, n=n)
                view[...] = view[...] + RLS[:, :, pl.ds(spots[p], n)]
            else:
                view = home(ch, zs[1], x, c, c0=c0, n=n)
                view[...] = view[...] + RL[:, pl.ds(spots[p], n)]
            rs_z[p][1].start()

    def wait_z(p):
        rs_z[p][0].wait_recv()
        rs_z[p][1].wait_recv()
        if SCATTER[p][4]:
            rs_z[p][2].wait_recv()
            return

        @pl.when(middle)
        def _():
            rs_z[p][2].wait_recv()

    def scatter_end(p):
        ch, c0, n, turned, straight, late = SCATTER[p]
        wait_z(p)
        if late:
            rs_x[p][3].wait_recv()

        def body(j):
            total = home(ch, z, x, c)[:, tile_cols(c0, j)].astype(F32)
            if late:
                total = total + RX[z, :, tile_cols(spots[p], j)].astype(F32)
            for k in range(3):
                total = total + RZ[k, :, tile_cols(spots[p], j)].astype(F32)
            results[ch][:, tile_cols(c0, j)] = total

        tile_loop(n // 256, body)
        flush_result(p)

    def turned_x(p):
        ch, c0, n, turned, straight, late = SCATTER[p]
        wait_z(p)
        for xi in range(2):
            view = home(ch, z, xi, c, c0=c0, n=n)
            total = view[...].astype(F32)
            for k in range(3):
                total = total + RZS[k, xi, :, pl.ds(spots[p], n)].astype(F32)
            view[...] = total.astype(BF)
        rs_x[p][0].start()

    def turned_end(p):
        ch, c0, n, turned, straight, late = SCATTER[p]
        rs_x[p][0].wait_recv()
        own = home(ch, z, x, c, c0=c0, n=n)[...].astype(F32)
        results[ch][:, c0 : c0 + n] = own + RXS[:, pl.ds(spots[p], n)].astype(F32)
        flush_result(p)

    def weight_tiles(ch, c0, n):
        ref, base = homes[ch]

        def body(j):
            cols = tile_cols(c0, j)
            if ch == 0:
                left, right = T, HID[:, cols]
            elif ch == 1:
                left, right = T2, GT[:, cols]
            elif ch == 2:
                left, right = T2, UP[:, cols]
            elif c0 < 3 * LOCAL:
                left, right = T2, DQKV[:, cols]
            else:
                left, right = T, ATT[:, :, tile_cols(c0 - 3 * LOCAL, j)].reshape(2 * SEQ_LEN, 256)
            r = mm(left[...], right)
            ref[:, :, :, :, tile_cols(base + c0, j)] = r.astype(BF).reshape(4, 2, 2, SHARD, 256)

        tile_loop(n // 256, body)

    def weight_grad(p):
        ch, c0, n, turned, straight, late = SCATTER[p]
        if p == FIRST_QUERY:
            pl.semaphore_wait(core_credit, 1)
        if ch == 3 and c0 < 3 * LOCAL < c0 + n:
            weight_tiles(ch, c0, 3 * LOCAL - c0)
            weight_tiles(ch, 3 * LOCAL, c0 + n - 3 * LOCAL)
        else:
            weight_tiles(ch, c0, n)
        rs_c[p].start()

    def hidden_back(half):
        gather_end(COL_DOWN + half * 1024, 1024)

        def body(j):
            cols = tile_cols(half * 1024, j)
            dhid = mm(
                COT[...].reshape(2 * SEQ_LEN, WIDTH), w_tile(tile_cols(COL_DOWN + half * 1024, j))
            )
            gate = GT[:, cols].astype(F32)
            up = UP[:, cols].astype(F32)
            sig = jax.nn.sigmoid(gate)
            GT[:, cols] = (dhid * up * (sig + gate * sig * (1.0 - sig))).astype(BF)
            UP[:, cols] = (dhid * gate * sig).astype(BF)

        tile_loop(4, body)

    def gather_sent():
        for i in range(len(GATHER)):
            ag_own[i][0].wait_send()
            for copy in ag_x[i]:
                copy.wait_send()
            ag_c[i].wait_send()
            if GATHER[i][3]:
                ag_own[i][1].wait_send()
                ag_own[i][2].wait_send()
                continue

            @pl.when(edge)
            def _():
                ag_own[i][1].wait_send()

            @pl.when(middle)
            def _():
                ag_own[i][2].wait_send()
                for copy in ag_pass[i]:
                    copy.wait_send()

    def last_product():
        def body(zi):
            cols = tile_cols(0, zi)
            r = mm_nt(HID[...], w_rows(zi, COL_DOWN, HIDDEN)).reshape(2, 2, HALF, 256)
            mine = jnp.where(y == 0, r[:, 0], r[:, 1])
            OUTM[:, :, cols] = MID[:, own_rows, cols] + mine
            YDS[:, :, cols] = jnp.where(y == 0, r[:, 1], r[:, 0]).astype(BF)

        tile_loop(4, body)

    y_dnf = [
        remote(YS.at[s], YR.at[s], y_send.at[4 + s], y_recv.at[4 + s], y_dev) for s in range(2)
    ]
    y_out = remote(YDS, YDR, y_send.at[6], y_recv.at[6], y_dev)

    def ffn_back(s):
        if s == 0:
            pl.semaphore_wait(credit, 1)
        rows = slice(s * SEQ_LEN, (s + 1) * SEQ_LEN)

        def body(zi):
            r = mm_nt(GT[rows, :], w_rows(zi, COL_GATE, HIDDEN))
            r = r + mm_nt(UP[rows, :], w_rows(zi, COL_UP, HIDDEN))
            YS[s, :, tile_cols(0, zi)] = r.astype(BF)

        tile_loop(4, body)
        y_dnf[s].start()

    DAT = HID.at[:, 3 * LOCAL : 4 * LOCAL]
    DQKV = HID

    def middle_back(s):
        if s == 0:
            GF[...] = jnp.zeros_like(GF)
            GA[...] = jnp.zeros_like(GA)
        y_dnf[s].wait_recv()

        def body(b, rows):
            v = MID[s, rows, :]
            inv = lax.rsqrt(jnp.mean(v * v, axis=-1, keepdims=True) + EPS)
            scaled = v * inv
            dn = YS[s, rows, :].astype(F32) + YR[s, rows, :].astype(F32)
            flag = jnp.where(b // (HALF // ROWS) == y, 1.0, 0.0)
            GF[...] += flag * jnp.sum((dn * scaled).reshape(ROWS // 8, 8, WIDTH), axis=0)
            u = dn * fgain_ref[...]
            dm = COT[s, rows, :].astype(F32) + inv * (
                u - scaled * jnp.mean(u * scaled, axis=-1, keepdims=True)
            )
            MID[s, rows, :] = dm
            DML[s, rows, :] = dm.astype(BF)

        row_loop(body)
        seq_rows = slice(s * SEQ_LEN, (s + 1) * SEQ_LEN)

        def body(j):
            DAT[seq_rows, tile_cols(0, j)] = mm(DML[s], w_tile(tile_cols(COL_OUT, j))).astype(BF)

        tile_loop(2, body)

    def attend_back(s):
        seq_rows = slice(s * SEQ_LEN, (s + 1) * SEQ_LEN)

        def body(p):
            cols = pair_cols(p)
            do = DAT[seq_rows, cols]
            dprobs = mm_nt(stacked(V[s, :, cols]), do)
            probs_low = PT[s * PAIRS + p]
            parts = []
            for h in range(2):
                part = slice(h * SEQ_LEN, (h + 1) * SEQ_LEN)
                pr = probs_low[part].astype(F32)
                dp = dprobs[part]
                dot = jnp.sum(pr * dp, axis=0, keepdims=True)
                ds = (pr * (dp - dot)).astype(BF)
                wide = ds.astype(F32)
                same = wide * SAME[s]
                same_sum = jnp.sum(same, axis=0, keepdims=True)
                other_sum = jnp.sum(wide - same, axis=0, keepdims=True)
                if s == 0:
                    BS[0, p * 2 + h] = same_sum
                    BS[1, p * 2 + h] = other_sum
                else:
                    BS[0, p * 2 + h] += same_sum
                    BS[1, p * 2 + h] += other_sum
                parts.append(ds)
            dsc = jnp.concatenate(parts, axis=0)
            dv = mm(probs_low, do)
            dv = jnp.where(low_lane, dv[:SEQ_LEN], dv[SEQ_LEN:])
            dk = mm(dsc, Q[s, :, cols])
            dk = jnp.where(low_lane, dk[:SEQ_LEN], dk[SEQ_LEN:]) * 0.125
            dq = mm_tn(dsc, stacked(K[s, :, cols] * jnp.asarray(0.125, BF)))
            dq = dq * COS[s] - swap(dq) * SIN[s]
            dk = dk * COS[s] - swap(dk) * SIN[s]
            DQKV[seq_rows, cols] = dq.astype(BF)
            DQKV[seq_rows, pl.ds(pl.multiple_of(LOCAL + p * 128, 128), 128)] = dk.astype(BF)
            DQKV[seq_rows, pl.ds(pl.multiple_of(2 * LOCAL + p * 128, 128), 128)] = dv.astype(BF)

        tile_loop(PAIRS, body)

    y_dn = [
        remote(YS.at[s, other_rows], YNR.at[s], y_send.at[7 + s], y_recv.at[7 + s], y_dev)
        for s in range(2)
    ]

    def norm_back(s):
        if s == 0:
            for k in range(2):
                y_dnf[k].wait_send()
        seq_rows = slice(s * SEQ_LEN, (s + 1) * SEQ_LEN)

        def body(zi):
            r = mm_nt(DQKV[seq_rows, 0 : 3 * LOCAL], w_rows(zi, COL_QKV, 3 * LOCAL))
            YS[s, :, tile_cols(0, zi)] = r.astype(BF)

        tile_loop(4, body)
        y_dn[s].start()

    def finish_out():
        y_out.wait_recv()
        for s in range(2):

            def body(b, carry):
                rows = pl.ds(pl.multiple_of(b * ROWS, ROWS), ROWS)
                out_ref[s, rows, :] = (OUTM[s, rows, :] + YDR[s, rows, :].astype(F32)).astype(BF)
                return carry

            lax.fori_loop(0, HALF // ROWS, body, 0)
        flush(out_ref, out_hbm)

    def token_rows(s):
        y_dn[s].wait_recv()

        def body(b, carry):
            rows = pl.ds(pl.multiple_of(b * ROWS, ROWS), ROWS)
            mine = pl.ds(pl.multiple_of(y * HALF + b * ROWS, ROWS), ROWS)
            v = X[s, mine, :].astype(F32)
            inv = lax.rsqrt(jnp.mean(v * v, axis=-1, keepdims=True) + EPS)
            scaled = v * inv
            dn = YS[s, mine, :].astype(F32) + YNR[s, rows, :].astype(F32)
            GA[...] += jnp.sum((dn * scaled).reshape(ROWS // 8, 8, WIDTH), axis=0)
            u = dn * again_ref[...]
            dx = MID[s, mine, :] + inv * (
                u - scaled * jnp.mean(u * scaled, axis=-1, keepdims=True)
            )
            tgrad_ref[s, rows, :] = dx.astype(BF)
            return carry

        lax.fori_loop(0, HALF // ROWS, body, 0)
        flush(tgrad_ref.at[s], tgrad_hbm.at[s])

    def sum_start():
        SV[0] = jnp.zeros((24, 128), F32)
        first_sum = jnp.sum(GA[...], axis=0, keepdims=True)
        second_sum = jnp.sum(GF[...], axis=0, keepdims=True)
        for j in range(8):
            SV[0, j : j + 1, :] = first_sum[:, j * 128 : (j + 1) * 128]
            SV[0, 8 + j : 9 + j, :] = second_sum[:, j * 128 : (j + 1) * 128]
        for kind in range(2):
            row = jnp.zeros((1, 128), F32)
            for h in range(8):
                head_sum = jnp.sum(BS[kind, h], axis=1, keepdims=True)
                row = row + jnp.where(lane == y * 8 + h, head_sum, 0.0)
            SV[0, 16 + kind : 17 + kind, :] = row
        sums[0][0].start()

    sums = [
        [remote(SV.at[0], SR.at[0], sv_send.at[0], sv_recv.at[0], c_dev)],
        [remote(SV.at[1], SR.at[1], sv_send.at[1], sv_recv.at[1], y_dev)],
        [
            remote(SV.at[2], SR.at[2 + k], sv_send.at[2 + k], sv_recv.at[2 + k], z_devs[k])
            for k in range(3)
        ],
        [remote(SV.at[3], SR.at[5], sv_send.at[5], sv_recv.at[5], x_dev)],
    ]

    def sum_stage(i):
        total = SV[i]
        for copy in sums[i]:
            copy.wait_recv()
        first = (0, 1, 2, 5)[i]
        for k in range(len(sums[i])):
            total = total + SR[first + k]
        if i < 3:
            SV[i + 1] = total
            for copy in sums[i + 1]:
                copy.start()
        else:
            for j in range(8):
                cols = slice(j * 128, (j + 1) * 128)
                ga_ref[:, cols] = total[j : j + 1]
                gf_ref[:, cols] = total[8 + j : 9 + j]
            gb_ref[...] = total[16:18, 0:16]

    transposes = {
        TURN_FFN: (NF, T2),
        TURN_NORMED: (N1, T2),
        TURN_MIDDLE: (DML, T),
    }
    plain = {
        START: start,
        TABLES: tables,
        NORM: norm,
        TURN_COTANGENT: turn_cotangent,
        LAST_PRODUCT: last_product,
        GATHER_SENT: gather_sent,
        OUT_SEND: y_out.start,
        OUT_ROWS: finish_out,
        SUM_START: sum_start,
    }
    indexed = {
        PROJECT: project,
        ATTEND: attend,
        PROJECT_OUT: project_out,
        MIDDLE: middle_rows,
        GATE_TILES: gate_tiles,
        UP_TILES: up_tiles,
        HIDDEN_BACK: hidden_back,
        FFN_BACK: ffn_back,
        MIDDLE_BACK: middle_back,
        ATTEND_BACK: attend_back,
        NORM_BACK: norm_back,
        TOKEN_ROWS: token_rows,
        SUM_STAGE: sum_stage,
        GATHER_Z: gather_z,
        GATHER_CORE: gather_c,
        WEIGHT_GRAD: weight_grad,
        SCATTER_X: scatter_x,
        SCATTER_Z: scatter_z,
        SCATTER_PASS: scatter_pass,
        SCATTER_END: scatter_end,
        TURNED_X: turned_x,
        TURNED_END: turned_end,
        SCATTER_OWN: scatter_own,
    }
    for step, index in PROGRAM:
        if step in transposes:
            transpose_into(*transposes[step])
        elif step in plain:
            plain[step]()
        else:
            indexed[step](index)

    y_out.wait_send()
    for copy in flushes:
        copy.wait()
    for s in range(2):
        y_dn[s].wait_send()
    y_tok.wait_send()
    y_cot.wait_send()
    for group in sums:
        for copy in group:
            copy.wait_send()
    for p in range(len(SCATTER)):
        rs_c[p].wait_send()
        for copy in rs_x[p]:
            copy.wait_send()
        rs_z[p][0].wait_send()
        rs_z[p][1].wait_send()
        if SCATTER[p][4]:
            rs_z[p][2].wait_send()
            continue

        @pl.when(middle)
        def _():
            rs_z[p][2].wait_send()

        @pl.when(edge)
        def _():
            rs_relay[p].wait_send()


def finish_kernel(*refs):
    sources, dests, boxes = refs[:9], refs[9:21], refs[21:30]
    in_sem, out_sem = refs[30], refs[31]
    moves = []
    for k, places in ((0, (0,)), (1, (1,)), (5, (11,)), (4, (10,)), (3, (9,)), (2, (3, 4, 5, 7))):
        rows = sources[k].shape[-2] // PARTS
        for part in range(PARTS):
            cut = (slice(None),) * (len(sources[k].shape) - 2) + (pl.ds(part * rows, rows),)
            moves.append((sources[k].at[cut], boxes[k].at[cut], places, cut))
    for k, place in ((6, 2), (7, 8), (8, 6)):
        moves.append((sources[k], boxes[k], (place,), ()))
    loads = [
        pltpu.make_async_copy(source, box, in_sem.at[i])
        for i, (source, box, _, _) in enumerate(moves)
    ]
    for load in loads:
        load.start()
    stores = []
    for load, (_, box, places, cut) in zip(loads, moves):
        load.wait()
        for i, place in enumerate(places):
            part = box if len(places) == 1 else box.at[:, pl.ds(i * LOCAL, LOCAL)]
            dest = dests[place].at[cut] if cut else dests[place]
            store = pltpu.make_async_copy(part, dest, out_sem.at[len(stores)])
            store.start()
            stores.append(store)
    for store in stores:
        store.wait()


def fused_local(
    tokens,
    segment_ids,
    variate_ids,
    time_ids,
    attn_gain,
    w_query,
    w_key,
    w_value,
    head_bias,
    w_out,
    ffn_gain,
    w_gate,
    w_up,
    w_down,
    cotangent,
):
    inverse = 10000.0 ** (-(np.arange(32, dtype=np.float32) / np.float32(32)))
    freq = jnp.asarray(np.tile(inverse.astype(np.float32), 4)[None, :])
    vmem = pl.BlockSpec(memory_space=pltpu.VMEM)
    anym = pl.BlockSpec(memory_space=pl.ANY)
    smem = pl.BlockSpec(memory_space=pltpu.SMEM)
    bf = lambda *shape: pltpu.VMEM(shape, BF)
    fl = lambda *shape: pltpu.VMEM(shape, F32)
    seq3 = (2, SEQ_LEN, WIDTH)
    half3 = (2, HALF, WIDTH)
    dma = pltpu.SemaphoreType.DMA
    scratch = [
        bf(*half3),
        bf(*half3),
        fl(4, SHARD, CHUNK),
        bf(4, 2, 2, SHARD, ALL_COLS),
        bf(4, 2, 2, SHARD, CHUNK),
        bf(3, 4, 2, SHARD, CHUNK),
        bf(4, SHARD, NORMAL_COLS),
        bf(3, SHARD, NORMAL_COLS),
        bf(SHARD, NORMAL_COLS),
        bf(SHARD, TURNED_COLS),
        bf(3, 2, SHARD, TURNED_COLS),
        bf(2, SHARD, TURNED_COLS),
        bf(*seq3),
        bf(*seq3),
        bf(*seq3),
        bf(*seq3),
        bf(2, SEQ_LEN, LOCAL),
        bf(2, SEQ_LEN, LOCAL),
        bf(2, SEQ_LEN, LOCAL),
        bf(2, SEQ_LEN, LOCAL),
        bf(2 * PAIRS, 2 * SEQ_LEN, SEQ_LEN),
        fl(*seq3),
        bf(2 * SEQ_LEN, HIDDEN),
        bf(2 * SEQ_LEN, HIDDEN),
        bf(2 * SEQ_LEN, HIDDEN),
        bf(*seq3),
        bf(*seq3),
        bf(*half3),
        bf(*half3),
        bf(*half3),
        bf(WIDTH, 2 * SEQ_LEN),
        bf(WIDTH, 2 * SEQ_LEN),
        fl(*half3),
        bf(*seq3),
        fl(2, SEQ_LEN, SEQ_LEN),
        fl(2, SEQ_LEN, SEQ_LEN),
        fl(2, SEQ_LEN, 128),
        fl(2, SEQ_LEN, 128),
        fl(8, WIDTH),
        fl(8, WIDTH),
        fl(2, 8, 1, SEQ_LEN),
        fl(4, 24, 128),
        fl(6, 24, 128),
        dma((9,)),
        dma((9 * len(GATHER),)),
        dma((9 * len(GATHER),)),
        dma((9 * len(SCATTER),)),
        dma((9 * len(SCATTER),)),
        dma((9,)),
        dma((9,)),
        dma((6,)),
        dma((6,)),
        pltpu.SemaphoreType.REGULAR,
        pltpu.SemaphoreType.REGULAR,
        dma((len(SCATTER) + 3,)),
    ]
    shape = jax.ShapeDtypeStruct
    outs = pl.pallas_call(
        layer_kernel,
        out_shape=(
            shape(half3, BF),
            shape(half3, BF),
            shape((SHARD, HIDDEN), F32),
            shape((SHARD, HIDDEN), F32),
            shape((SHARD, HIDDEN), F32),
            shape((SHARD, HIDDEN), F32),
            shape((1, WIDTH), F32),
            shape((1, WIDTH), F32),
            shape((2, 16), F32),
        ),
        in_specs=[anym, anym, vmem, vmem, vmem, vmem, vmem, vmem, smem] + [anym] * 7,
        out_specs=(anym,) * 6 + (vmem,) * 3,
        scratch_shapes=scratch,
        compiler_params=pltpu.CompilerParams(
            collective_id=0, has_side_effects=True, vmem_limit_bytes=67043328
        ),
        name="layer",
    )(
        tokens,
        cotangent,
        segment_ids,
        variate_ids,
        time_ids,
        attn_gain.reshape(1, WIDTH),
        ffn_gain.reshape(1, WIDTH),
        freq,
        head_bias,
        w_query,
        w_key,
        w_value,
        w_out.T,
        w_gate,
        w_up,
        w_down.T,
    )
    finals = pl.pallas_call(
        finish_kernel,
        out_shape=(
            shape(half3, BF),
            shape(half3, BF),
            shape((1, WIDTH), F32),
            shape((SHARD, LOCAL), F32),
            shape((SHARD, LOCAL), F32),
            shape((SHARD, LOCAL), F32),
            shape((2, 16), F32),
            shape((SHARD, LOCAL), F32),
            shape((1, WIDTH), F32),
            shape((SHARD, HIDDEN), F32),
            shape((SHARD, HIDDEN), F32),
            shape((SHARD, HIDDEN), F32),
        ),
        in_specs=[anym] * 9,
        out_specs=[anym] * 12,
        scratch_shapes=[
            bf(*half3),
            bf(*half3),
            fl(SHARD, HIDDEN),
            fl(SHARD, HIDDEN),
            fl(SHARD, HIDDEN),
            fl(SHARD, HIDDEN),
            fl(1, WIDTH),
            fl(1, WIDTH),
            fl(2, 16),
            dma((6 * PARTS + 3,)),
            dma((9 * PARTS + 3,)),
        ],
        name="finish",
    )(*outs)
    layer_out, tokens_grad, ga, gq, gk, gv, gb, go, gf, gg, gu, gd = finals
    return (
        layer_out,
        tokens_grad,
        ga.reshape(WIDTH),
        gq,
        gk,
        gv,
        gb,
        go.T,
        gf.reshape(WIDTH),
        gg,
        gu,
        gd.T,
    )


def fits(mesh, tokens, w_query, w_gate):
    sizes = dict(mesh.shape)
    return (
        sizes["fsdp"] == 16
        and sizes["tensor"] == 2
        and tokens.shape == (2, 16 * SEQ_LEN, WIDTH)
        and w_query.shape == (WIDTH, 2 * LOCAL)
        and w_gate.shape == (WIDTH, 2 * HIDDEN)
    )


def solution(mesh):
    placed = (
        P(None, ("fsdp", "tensor"), None),
        P(None, "fsdp"),
        P(None, "fsdp"),
        P(None, "fsdp"),
        P(),
        P("fsdp", "tensor"),
        P("fsdp", "tensor"),
        P("fsdp", "tensor"),
        P(),
        P("tensor", "fsdp"),
        P(),
        P("fsdp", "tensor"),
        P("fsdp", "tensor"),
        P("tensor", "fsdp"),
        P(None, ("fsdp", "tensor"), None),
    )
    outs = (
        P(None, ("fsdp", "tensor"), None),
        P(None, ("fsdp", "tensor"), None),
        P(),
        P("fsdp", "tensor"),
        P("fsdp", "tensor"),
        P("fsdp", "tensor"),
        P(),
        P("tensor", "fsdp"),
        P(),
        P("fsdp", "tensor"),
        P("fsdp", "tensor"),
        P("tensor", "fsdp"),
    )

    def whole(*args):
        body = fused_local if fits(mesh, args[0], args[5], args[11]) else local
        return jax.shard_map(
            body, mesh=mesh, in_specs=placed, out_specs=outs, check_vma=False
        )(*args)

    return whole
```
